32 devices in a mesh: shot: 2 (over y), depth: 2 (over core), lat: 8 (over z, x).
Axes of the slice: x: 2, y: 2, z: 4, core: 2. Of those that a mesh axis runs over, the one named last changes fastest.
Arguments:
- sources: float32 [6, 2, 32, 4096], P('shot', None, 'depth', 'lat'), parts along dimension 0, may hold values from -6 to 6
- blocks: float32 [4, 32, 7, 2, 128, 128], P(('shot', 'depth'), 'lat'), parts along dimension 0, may hold values from -0.125 to 0.125
- block_cols: int32 [2, 32, 7], P('depth', 'lat'), may hold values from 0 to 31, as said below
- refl_level: int32 [4096], P('lat'), may hold values from 0 to 1
- refl_coef: float32 [2, 4096], P(None, 'lat'), may hold values from -0.5 to 0.5
Outputs:
- bottom: float32 [6, 2, 32, 4096], P('shot', None, 'depth', 'lat'), parts along dimension 0
The draws below stay inside these ranges and needn't reach their ends.
There are 2 independent parts, one for each index of `shot`. The reference program is written for one: setup_inputs(seed, part) draws one part's arguments, and reference() takes and returns one part's arrays. A program takes and returns all parts, laid end to end along the dimension named above; an argument that names none is the same for every part. Nothing has to cross between parts.
Inputs may be any that keep to these rules, and one draw needn't show every extreme that they name: block_cols[l, b, 0] = b, and every entry of row b lies within 4 block rows of b; a row may name a column twice.
All inputs are finite; a program needn't handle non-finite values.
Results may differ from the reference program's by a relative error of at most 0.0001.
Values sent between devices are 32-bit elements; how exact they have to be, the bound alone decides.
No kernel may reach another device: no remote copies, remote signals or barrier semaphores. Data moves between devices by JAX's collectives and lax.ppermute only.
A program may use at most 64 MiB of HBM per device.

```python
import jax
import jax.numpy as jnp
from jax import lax

B = 128
NNZ = 7
PANELS = 3
S = 32
BR_DEV = 4
LEVELS = 2
NB = 32
NPTS = 4096


def draw_block_cols(key, part):
    reach_rows = BR_DEV
    candidates = jnp.concatenate([jnp.arange(-reach_rows, 0), jnp.arange(1, reach_rows + 1)]).astype(jnp.int32)
    scores = jax.random.randint(key, (LEVELS, NB, 2 * reach_rows), 0, 1 << 20).astype(jnp.int32)
    scores = scores * (2 * reach_rows) + jnp.arange(2 * reach_rows).astype(jnp.int32)
    chosen = jnp.argsort(scores, axis=-1)[:, :, :NNZ - 1]
    offsets = candidates[chosen]
    row_ids = jnp.arange(NB).astype(jnp.int32)[None, :, None]
    columns = row_ids + offsets
    columns = jnp.where((columns < 0) | (columns >= NB), row_ids - offsets, columns)
    diagonal = jnp.broadcast_to(row_ids, (LEVELS, NB, 1))
    return jnp.concatenate([diagonal, columns], axis=-1).astype(jnp.int32)


def set_ends(result, stream_key, low, largest):
    place = [jax.random.randint(jax.random.fold_in(stream_key, axis), (), 0, length) for axis, length in enumerate(result.shape)]
    longest = result.shape.index(max(result.shape))
    beside = place[:longest] + [(place[longest] + 1) % result.shape[longest]] + place[longest + 1:]
    return result.at[tuple(place)].set(low).at[tuple(beside)].set(largest)


def level_of(stream_key, shape, shards, least, largest):
    gain = 1.0
    for axis_at, shards_of in shards:
        heights = jax.random.uniform(jax.random.fold_in(jax.random.fold_in(stream_key, 6), axis_at), (shards_of,), jnp.float32, least / len(shards), largest / len(shards))
        gain = gain * jnp.repeat(jnp.exp(heights), shape[axis_at] // shards_of).reshape((-1,) + (1,) * (len(shape) - 1 - axis_at))
    return gain


def gaussian(stream_key, dims, width, limit, split=(), dtype=jnp.bfloat16):
    gain = level_of(stream_key, dims, split, -0.22, 0.18) if split else 1.0
    drawn = jax.random.normal(stream_key, dims, jnp.float32) * width * gain
    return jnp.minimum(jnp.maximum(drawn, -limit), limit).astype(dtype)


def setup_inputs(seed: int = 0, part: int = 0) -> dict:
    arg_keys = jax.random.split(jax.random.key(seed), 6)
    own_keys = jax.random.split(jax.random.fold_in(arg_keys[5], part), 6)
    sources = gaussian(own_keys[0], (PANELS, 2, S, NPTS), 1.0, 6.0, ((2, 2), (3, 8)), jnp.float32)
    blocks = gaussian(own_keys[1], (LEVELS, NB, NNZ, 2, B, B), (2 * NNZ * B) ** -0.5, 0.125, ((0, 2), (1, 8)), jnp.float32)
    block_cols = draw_block_cols(jax.random.fold_in(arg_keys[5], 71), part)
    refl_level = set_ends(jax.random.randint(arg_keys[3], (NPTS,), 0, LEVELS), jax.random.fold_in(arg_keys[3], 1), 0, LEVELS - 1).astype(jnp.int32)
    refl_coef = jnp.clip(jax.random.uniform(arg_keys[4], (2, NPTS), jnp.float32, -0.5, 0.5) * level_of(arg_keys[4], (2, NPTS), ((1, 8),), -0.4, 0.0), -0.5, 0.5)
    return {"sources": sources, "blocks": blocks, "block_cols": block_cols, "refl_level": refl_level, "refl_coef": refl_coef}


def reference(sources, blocks, block_cols, refl_level, refl_coef):
    channels = PANELS * S
    wavefield = jnp.transpose(sources, (1, 0, 2, 3)).reshape(2, channels, NPTS)
    for level_index in range(LEVELS):
        at_level = refl_level == level_index
        coef_re = jnp.where(at_level, refl_coef[0], jnp.float32(0.0))
        coef_im = jnp.where(at_level, refl_coef[1], jnp.float32(0.0))
        field_re = wavefield[0]
        field_im = wavefield[1]
        combined = jnp.concatenate([field_re + coef_re * field_re - coef_im * field_im,
                                    field_im + coef_re * field_im + coef_im * field_re], axis=0)
        stacked = combined.reshape(2 * channels, NB, B)

        def one_row(row_args):
            row_cols, row_blocks = row_args
            picked = jnp.take(stacked, row_cols, axis=1)
            real_part = jnp.einsum("cjp,jpq->cq", picked, row_blocks[:, 0], precision=lax.Precision.HIGHEST)
            imag_part = jnp.einsum("cjp,jpq->cq", picked, row_blocks[:, 1], precision=lax.Precision.HIGHEST)
            return jnp.concatenate([real_part[:channels] - imag_part[channels:],
                                    imag_part[:channels] + real_part[channels:]], axis=0)

        rows_out = lax.map(one_row, (block_cols[level_index], blocks[level_index]))
        wavefield = jnp.transpose(rows_out, (1, 0, 2)).reshape(2, channels, NPTS)
    return jnp.transpose(wavefield.reshape(2, PANELS, S, NPTS), (1, 0, 2, 3))
```

```python
import functools

import jax
import jax.numpy as jnp
from jax import lax
from jax.experimental import pallas as pl
from jax.experimental.pallas import tpu as pltpu
from jax.sharding import PartitionSpec as P

VMEM = pl.BlockSpec(memory_space=pltpu.VMEM)
SMEM = pl.BlockSpec(memory_space=pltpu.SMEM)


def reflected(field_re, field_im, at_level, coef_re, coef_im):
    coef_re = jnp.where(at_level, coef_re, 0.0)
    coef_im = jnp.where(at_level, coef_im, 0.0)
    return (
        field_re + coef_re * field_re - coef_im * field_im,
        field_im + coef_re * field_im + coef_im * field_re,
    )


def enter_kernel(sources, refl_level, refl_coef, total):
    panels, _, part, _ = sources.shape
    at_level = refl_level[...] == 0
    for k in range(panels):
        re, im = reflected(
            sources[k, 0], sources[k, 1], at_level, refl_coef[0:1, :], refl_coef[1:2, :]
        )
        total[0, k * part : (k + 1) * part, :] = re
        total[1, k * part : (k + 1) * part, :] = im


def split_kernel(depth, own, received, high, low):
    level = pl.program_id(0)

    def write(blocks):
        for j in range(blocks.shape[2]):
            for c in range(2):
                value = blocks[0, 0, j, c]
                head = value.astype(jnp.bfloat16)
                lanes = slice(c * value.shape[1], (c + 1) * value.shape[1])
                high[0, 0, j, :, lanes] = head
                low[0, 0, j, :, lanes] = (value - head.astype(jnp.float32)).astype(
                    jnp.bfloat16
                )

    @pl.when(level == depth[0])
    def _():
        write(own)

    @pl.when(level != depth[0])
    def _():
        write(received)


def level_kernel(
    level, last, cols, where, own, swapped, diagonal, high, low, refl_level, refl_coef, out, parts
):
    _, block_rows, per_row, block_size, _ = high.shape
    channels = own.shape[1]
    rows = 2 * channels

    def place(field, first):
        for b in range(block_rows):
            lanes = slice(b * block_size, (b + 1) * block_size)
            for c in range(2):
                value = field[c, :, lanes]
                head = value.astype(jnp.bfloat16)
                at = c * channels
                parts[first + b, at : at + channels, :] = head
                parts[first + b, rows + at : rows + at + channels, :] = (
                    value - head.astype(jnp.float32)
                ).astype(jnp.bfloat16)

    place(own, block_rows)
    place(swapped, where[1])
    place(diagonal, where[2])
    for b in range(block_rows):
        picked = jnp.concatenate(
            [parts[cols[b, j] - where[0]] for j in range(per_row)], axis=1
        )
        head = high[0, b].reshape(per_row * block_size, 2 * block_size)
        tail = low[0, b].reshape(per_row * block_size, 2 * block_size)
        both = jnp.dot(picked, head, preferred_element_type=jnp.float32)
        product = (
            both[:rows]
            + both[rows:]
            + jnp.dot(picked[:rows], tail, preferred_element_type=jnp.float32)
        )
        re = product[:channels, :block_size] - product[channels:, block_size:]
        im = product[:channels, block_size:] + product[channels:, :block_size]
        lanes = slice(b * block_size, (b + 1) * block_size)
        if last:
            panels, _, part, _ = out.shape
            for k in range(panels):
                out[k, 0, :, lanes] = re[k * part : (k + 1) * part]
                out[k, 1, :, lanes] = im[k * part : (k + 1) * part]
        else:
            re, im = reflected(
                re,
                im,
                refl_level[:, lanes] == level + 1,
                refl_coef[0:1, lanes],
                refl_coef[1:2, lanes],
            )
            out[0, :, lanes] = re
            out[1, :, lanes] = im


def per_device(sources, blocks, block_cols, refl_level, refl_coef):
    lat_count = lax.axis_size("lat")
    lat_pos = lax.axis_index("lat")
    depth_pos = lax.axis_index("depth").astype(jnp.int32)
    panels, _, part, points = sources.shape
    _, block_rows, per_row, _, block_size, _ = blocks.shape
    channels = panels * part
    over_depth = [(0, 1), (1, 0)]
    pairs = [(i, i + 1) for i in range(0, lat_count - 1, 2)]
    pairs += [(j, i) for i, j in pairs]
    crossing = [(i, i + 1) for i in range(1, lat_count - 1, 2)]
    crossing += [(j, i) for i, j in crossing]
    refl_level = refl_level.reshape(1, points)

    other_blocks = lax.ppermute(blocks, "depth", over_depth)
    other_cols = lax.ppermute(block_cols, "depth", over_depth)
    total = pl.pallas_call(
        enter_kernel,
        out_shape=jax.ShapeDtypeStruct((2, channels, points), jnp.float32),
        in_specs=[VMEM] * 3,
        out_specs=VMEM,
        compiler_params=pltpu.CompilerParams(vmem_limit_bytes=4 << 20),
        name="enter",
    )(sources, refl_level, refl_coef)

    split_shape = (2, block_rows, per_row, block_size, 2 * block_size)
    block_shape = (1, 1, per_row, 2, block_size, block_size)

    def own_map(level, b, depth):
        first = jnp.where(depth[0] == 0, block_rows - 1, 0)
        return (0, jnp.where(level == depth[0], b, first), 0, 0, 0, 0)

    def received_map(level, b, depth):
        first = jnp.where(depth[0] == 1, block_rows - 1, 0)
        return (0, jnp.where(level != depth[0], b, first), 0, 0, 0, 0)

    out_block = pl.BlockSpec(
        (1, 1, per_row, block_size, 2 * block_size), lambda level, b, depth: (level, b, 0, 0, 0)
    )
    high, low = pl.pallas_call(
        split_kernel,
        out_shape=[jax.ShapeDtypeStruct(split_shape, jnp.bfloat16)] * 2,
        grid_spec=pltpu.PrefetchScalarGridSpec(
            num_scalar_prefetch=1,
            grid=(2, block_rows),
            in_specs=[
                pl.BlockSpec(block_shape, own_map),
                pl.BlockSpec(block_shape, received_map),
            ],
            out_specs=[out_block, out_block],
        ),
        cost_estimate=pl.CostEstimate(flops=0, bytes_accessed=4 * blocks.size * 4, transcendentals=0),
        compiler_params=pltpu.CompilerParams(vmem_limit_bytes=12 << 20),
        name="split",
    )(depth_pos.reshape(1), blocks, other_blocks)

    odd = (lat_pos % 2).astype(jnp.int32)
    first_row = ((lat_pos - 1) * block_rows).astype(jnp.int32)
    where = jnp.stack([first_row, 2 * block_rows * (1 - odd), 2 * block_rows * odd])
    first_cols = jnp.where(depth_pos == 0, block_cols, other_cols)[0]
    second_cols = jnp.where(depth_pos == 0, other_cols, block_cols)[0]
    for level, cols in enumerate((first_cols, second_cols)):
        last = level == 1
        diagonal = lax.ppermute(total, "lat", crossing)
        swapped = lax.ppermute(total, "lat", pairs)
        shape = (panels, 2, part, points) if last else (2, channels, points)
        level_block = pl.BlockSpec(
            (1, block_rows, per_row, block_size, 2 * block_size),
            functools.partial(lambda level, i: (level, 0, 0, 0, 0), level),
        )
        whole = pl.BlockSpec((2, channels, points), lambda i: (0, 0, 0))
        total = pl.pallas_call(
            functools.partial(level_kernel, level, last),
            out_shape=jax.ShapeDtypeStruct(shape, jnp.float32),
            grid=(1,),
            in_specs=[SMEM, SMEM, whole, whole, whole, level_block, level_block, VMEM, VMEM],
            out_specs=VMEM,
            scratch_shapes=[
                pltpu.VMEM((3 * block_rows, 4 * channels, block_size), jnp.bfloat16)
            ],
            cost_estimate=pl.CostEstimate(
                flops=12 * channels * points * per_row * block_size,
                bytes_accessed=2 * blocks.size * 4,
                transcendentals=0,
            ),
            compiler_params=pltpu.CompilerParams(vmem_limit_bytes=16 << 20),
            name="level",
        )(cols, where, total, swapped, diagonal, high, low, refl_level, refl_coef)
    return total


def solution(mesh):
    placed = (
        P("shot", None, "depth", "lat"),
        P(("shot", "depth"), "lat", None, None, None, None),
        P("depth", "lat", None),
        P("lat"),
        P(None, "lat"),
    )
    return jax.shard_map(
        per_device,
        mesh=mesh,
        in_specs=placed,
        out_specs=P("shot", None, "depth", "lat"),
        check_vma=False,
    )
```

```python
import functools

import jax
import jax.numpy as jnp
from jax import lax
from jax.experimental import pallas as pl
from jax.experimental.pallas import tpu as pltpu
from jax.sharding import PartitionSpec as P

VMEM = pl.BlockSpec(memory_space=pltpu.VMEM)
SMEM = pl.BlockSpec(memory_space=pltpu.SMEM)
HBM = pl.BlockSpec(memory_space=pltpu.HBM)
MIB = 1 << 20


def reflected(field_re, field_im, at_level, coef_re, coef_im):
    coef_re = jnp.where(at_level, coef_re, 0.0)
    coef_im = jnp.where(at_level, coef_im, 0.0)
    return (
        field_re + coef_re * field_re - coef_im * field_im,
        field_im + coef_re * field_im + coef_im * field_re,
    )


def enter_kernel(sources, refl_level, refl_coef, total, held, level_held, coef_held, sems):
    copies = [
        pltpu.make_async_copy(a, b, sems.at[i])
        for i, (a, b) in enumerate(
            ((sources, held), (refl_level, level_held), (refl_coef, coef_held))
        )
    ]
    for copy in copies:
        copy.start()
    for copy in copies:
        copy.wait()
    panels, _, part, _ = held.shape
    at_level = level_held[...] == 0
    for k in range(panels):
        re, im = reflected(
            held[k, 0], held[k, 1], at_level, coef_held[0:1, :], coef_held[1:2, :]
        )
        total[0, k * part : (k + 1) * part, :] = re
        total[1, k * part : (k + 1) * part, :] = im


def head_and_tail(value):
    head = value.astype(jnp.bfloat16)
    return head, (value - head.astype(jnp.float32)).astype(jnp.bfloat16)


def pieces(field):
    value = field[...].reshape(field.shape[0] * field.shape[1], field.shape[2])
    return jnp.concatenate(head_and_tail(value), axis=0)


def product(left, high, low):
    rows = left.shape[0] // 2
    high = high.reshape(high.shape[0] * high.shape[1], high.shape[2])
    low = low.reshape(high.shape)
    both = jnp.dot(left, high, preferred_element_type=jnp.float32)
    cross = jnp.dot(left[:rows], low, preferred_element_type=jnp.float32)
    return both[:rows] + both[rows:] + cross


def prepare_kernel(
    level, own_cols, other_cols, own, received, field, high, low, sums, held, sems
):
    block_rows, per_row, _, size, _ = held.shape
    here = lax.axis_index("depth") == level
    first_row = lax.axis_index("lat") * block_rows
    for b in range(block_rows):

        @pl.when(here)
        def _():
            pltpu.make_async_copy(own.at[0, b], held.at[b], sems.at[b]).start()

        @pl.when(jnp.logical_not(here))
        def _():
            pltpu.make_async_copy(received.at[0, b], held.at[b], sems.at[b]).start()

    left = pieces(field)
    for b in range(block_rows):
        first = first_row + b - block_rows
        at = [
            jnp.where(here, own_cols[0, b, j], other_cols[0, b, j]) - first
            for j in range(per_row)
        ]
        for o in range(2 * block_rows + 1):
            absent = functools.reduce(jnp.logical_and, [a != o for a in at])

            @pl.when(absent)
            def _():
                zeros = jnp.zeros((size, 2 * size), jnp.bfloat16)
                high[b, o] = zeros
                low[b, o] = zeros

        same = [[at[i] == at[j] for i in range(j)] for j in range(per_row)]
        repeated = functools.reduce(jnp.logical_or, sum(same, []))
        pltpu.make_async_copy(own.at[0, b], held.at[b], sems.at[b]).wait()

        @pl.when(repeated)
        def _():
            for j in reversed(range(1, per_row)):
                unmerged = True
                for i in reversed(range(j)):

                    @pl.when(jnp.logical_and(same[j][i], unmerged))
                    def _():
                        held[b, i] = held[b, i] + held[b, j]

                    unmerged = jnp.logical_and(unmerged, jnp.logical_not(same[j][i]))

        for j in reversed(range(per_row)):
            for c in range(2):
                head, tail = head_and_tail(held[b, j, c])
                high[b, at[j], :, c * size : (c + 1) * size] = head
                low[b, at[j], :, c * size : (c + 1) * size] = tail
        band = slice(block_rows - b, 2 * block_rows - b)
        sums[b] = product(left, high[b, band], low[b, band])


def add_halo(halo, high, low, is_left, add):
    block_rows, span, size, _ = high.shape
    left = pieces(halo)

    @pl.when(is_left)
    def _():
        for b in range(block_rows):
            band = slice(0, block_rows - b)
            add(b, product(left[:, b * size :], high[b, band], low[b, band]))

    @pl.when(jnp.logical_not(is_left))
    def _():
        for b in range(block_rows):
            band = slice(span - 1 - b, span)
            add(b, product(left[:, : (b + 1) * size], high[b, band], low[b, band]))


def first_halo_kernel(halo, high, low, sums, out):
    def add(b, value):
        out[b] = sums[b] + value

    add_halo(halo, high, low, lax.axis_index("lat") % 2 == 1, add)


def leaving(value):
    channels, size = value.shape[0] // 2, value.shape[1] // 2
    return (
        value[:channels, :size] - value[channels:, size:],
        value[:channels, size:] + value[channels:, :size],
    )


def last_halo_kernel(level, halo, high, low, sums, refl_level, refl_coef, out):
    def add(b, value):
        re, im = leaving(sums[b] + value)
        lanes = slice(b * re.shape[1], (b + 1) * re.shape[1])
        re, im = reflected(
            re,
            im,
            refl_level[:, lanes] == level + 1,
            refl_coef[0:1, lanes],
            refl_coef[1:2, lanes],
        )
        out[0, :, lanes] = re
        out[1, :, lanes] = im

    add_halo(halo, high, low, lax.axis_index("lat") % 2 == 0, add)


def bottom_kernel(halo, high, low, sums, out, held, sems):
    panels, _, part, _ = out.shape
    block_rows, _, size, _ = high.shape

    def copy_out(b):
        lanes = pl.ds(b * size, size)
        return pltpu.make_async_copy(
            held.at[b], out.at[:, :, :, lanes], sems.at[b]
        )

    def add(b, value):
        re, im = leaving(sums[b] + value)
        held[b, :, 0] = re.reshape(panels, part, size)
        held[b, :, 1] = im.reshape(panels, part, size)
        copy_out(b).start()

    add_halo(halo, high, low, lax.axis_index("lat") % 2 == 0, add)
    for b in range(block_rows):
        copy_out(b).wait()


def in_hbm(value):
    return pltpu.with_memory_space_constraint(value, pltpu.HBM)


def params(mib):
    return pltpu.CompilerParams(vmem_limit_bytes=mib * MIB)


def cost(flops, transferred):
    return pl.CostEstimate(flops=flops, bytes_accessed=transferred, transcendentals=0)


def per_device(sources, blocks, block_cols, refl_level, refl_coef):
    lat_count = lax.axis_size("lat")
    panels, _, part, points = sources.shape
    _, block_rows, per_row, _, size, _ = blocks.shape
    channels = panels * part
    f32, bf16 = jnp.float32, jnp.bfloat16
    axes = ("depth", "lat")
    over_depth = [(0, 1), (1, 0)]
    even = range(0, lat_count - 1, 2)
    uneven = range(1, lat_count - 1, 2)
    alone_even = range(lat_count - lat_count % 2, lat_count)
    alone_uneven = [0] + list(range(lat_count - 1 + lat_count % 2, lat_count))

    def over_lat(firsts, alone):
        pairs = [(d * lat_count + i, d * lat_count + i + 1) for d in range(2) for i in firsts]
        pairs += [(i, lat_count + i) for i in alone]
        return pairs + [(j, i) for i, j in pairs]

    refl_level = refl_level.reshape(1, points)
    other_blocks = lax.ppermute(blocks, "depth", over_depth)
    other_cols = lax.ppermute(block_cols, "depth", over_depth)
    field_shape = jax.ShapeDtypeStruct((2, channels, points), f32)
    total = pl.pallas_call(
        enter_kernel,
        out_shape=field_shape,
        in_specs=[HBM] * 3,
        out_specs=VMEM,
        scratch_shapes=[
            pltpu.VMEM(sources.shape, f32),
            pltpu.VMEM((1, points), jnp.int32),
            pltpu.VMEM((2, points), f32),
            pltpu.SemaphoreType.DMA((3,)),
        ],
        compiler_params=params(4),
        name="enter",
    )(in_hbm(sources), in_hbm(refl_level), in_hbm(refl_coef))

    band_shape = jax.ShapeDtypeStruct((block_rows, 2 * block_rows + 1, size, 2 * size), bf16)
    sums_shape = jax.ShapeDtypeStruct((block_rows, 2 * channels, 2 * size), f32)
    macs = 6 * channels * points * 2 * size
    for level in range(2):
        diagonal = lax.ppermute(total, axes, over_lat(uneven, alone_uneven))
        swapped = lax.ppermute(total, axes, over_lat(even, alone_even))
        high, low, sums = pl.pallas_call(
            functools.partial(prepare_kernel, level),
            out_shape=[band_shape, band_shape, sums_shape],
            in_specs=[SMEM, SMEM, HBM, HBM, VMEM],
            out_specs=[VMEM] * 3,
            scratch_shapes=[
                pltpu.VMEM(blocks.shape[1:], f32),
                pltpu.SemaphoreType.DMA((block_rows,)),
            ],
            compiler_params=params(16),
            cost_estimate=cost(4 * macs, 8 * blocks.size),
            name="prepare",
        )(in_hbm(block_cols), other_cols, in_hbm(blocks), other_blocks, total)
        sums = pl.pallas_call(
            first_halo_kernel,
            out_shape=sums_shape,
            in_specs=[VMEM] * 4,
            out_specs=VMEM,
            compiler_params=params(12),
            cost_estimate=cost(macs, blocks.size),
            name="first_halo",
        )(swapped, high, low, sums)
        if level == 0:
            total = pl.pallas_call(
                functools.partial(last_halo_kernel, level),
                out_shape=field_shape,
                in_specs=[VMEM] * 6,
                out_specs=VMEM,
                compiler_params=params(12),
                cost_estimate=cost(macs, blocks.size),
                name="last_halo",
            )(diagonal, high, low, sums, refl_level, refl_coef)
    return pl.pallas_call(
        bottom_kernel,
        out_shape=jax.ShapeDtypeStruct(sources.shape, f32),
        in_specs=[VMEM] * 4,
        out_specs=HBM,
        scratch_shapes=[
            pltpu.VMEM((block_rows, panels, 2, part, size), f32),
            pltpu.SemaphoreType.DMA((block_rows,)),
        ],
        compiler_params=params(12),
        cost_estimate=cost(macs, blocks.size),
        name="bottom",
    )(diagonal, high, low, sums)


def solution(mesh):
    placed = (
        P("shot", None, "depth", "lat"),
        P(("shot", "depth"), "lat", None, None, None, None),
        P("depth", "lat", None),
        P("lat"),
        P(None, "lat"),
    )
    return jax.shard_map(
        per_device,
        mesh=mesh,
        in_specs=placed,
        out_specs=P("shot", None, "depth", "lat"),
        check_vma=False,
    )
```

```python
import functools

import jax
import jax.numpy as jnp
from jax import lax
from jax.experimental import pallas as pl
from jax.experimental.pallas import tpu as pltpu
from jax.sharding import PartitionSpec as P

VMEM = pl.BlockSpec(memory_space=pltpu.VMEM)
SMEM = pl.BlockSpec(memory_space=pltpu.SMEM)
HBM = pl.BlockSpec(memory_space=pltpu.HBM)
MIB = 1 << 20


def reflected(field_re, field_im, coef_re, coef_im):
    return (
        field_re + coef_re * field_re - coef_im * field_im,
        field_im + coef_re * field_im + coef_im * field_re,
    )


def entered(sources, coef):
    panels = [
        reflected(sources[k, 0], sources[k, 1], coef[0:1, :], coef[1:2, :])
        for k in range(sources.shape[0])
    ]
    return jnp.concatenate([re for re, _ in panels] + [im for _, im in panels], axis=0)


def enter_kernel(
    sources, refl_level, refl_coef, total, first_coef, next_coef, held, level_held, coef_held, sems
):
    copies = [
        pltpu.make_async_copy(a, b, sems.at[i])
        for i, (a, b) in enumerate(
            ((sources, held), (refl_level, level_held), (refl_coef, coef_held))
        )
    ]
    for copy in copies:
        copy.start()
    for copy in copies:
        copy.wait()
    first_coef[...] = jnp.where(level_held[...] == 0, coef_held[...], 0.0)
    next_coef[...] = jnp.where(level_held[...] == 1, coef_held[...], 0.0)
    total[...] = entered(held, first_coef)


def head_and_tail(value):
    head = value.astype(jnp.bfloat16)
    return head, (value - head.astype(jnp.float32)).astype(jnp.bfloat16)


def pieces(value):
    return jnp.concatenate(head_and_tail(value), axis=0)


def product(left, high, low):
    rows = left.shape[0] // 2
    high = high.reshape(high.shape[0] * high.shape[1], high.shape[2])
    low = low.reshape(high.shape)
    both = jnp.dot(left, high, preferred_element_type=jnp.float32)
    cross = jnp.dot(left[:rows], low, preferred_element_type=jnp.float32)
    return both[:rows] + both[rows:] + cross


def prepare_kernel(
    level, own_cols, other_cols, own, received, field, high, low, sums, held, sems
):
    block_rows, per_row, _, size, _ = held.shape
    here = lax.axis_index("depth") == level
    first_row = lax.axis_index("lat") * block_rows
    for b in range(block_rows):

        @pl.when(here)
        def _():
            pltpu.make_async_copy(own.at[0, b], held.at[b], sems.at[b]).start()

        @pl.when(jnp.logical_not(here))
        def _():
            pltpu.make_async_copy(received.at[0, b], held.at[b], sems.at[b]).start()

    left = pieces(field[...])
    span = 2 * block_rows + 1
    zeros = jnp.zeros((size, 2 * size), jnp.bfloat16)

    def clear(b, o):
        high[b, o] = zeros
        low[b, o] = zeros

    for b in range(block_rows):
        first = first_row + b - block_rows

        def offset(j):
            return jnp.where(here, own_cols[0, b, j], other_cols[0, b, j]) - first

        at = [offset(j) for j in range(per_row)]
        bits = [jnp.left_shift(1, a) for a in at]
        present = functools.reduce(jnp.bitwise_or, bits)
        repeated = sum(bits) != present
        pltpu.make_async_copy(own.at[0, b], held.at[b], sems.at[b]).wait()

        @pl.when(repeated)
        def _():
            def merge(n, merged):
                j = per_row - 1 - n // per_row
                i = per_row - 1 - n % per_row
                hit = (i < j) & (offset(i) == offset(j)) & (merged != j)

                @pl.when(hit)
                def _():
                    held[b, i] = held[b, i] + held[b, j]

                return jnp.where(hit, j, merged)

            lax.fori_loop(0, per_row * per_row, merge, jnp.int32(per_row))

            def clear_one(o, carry):
                clear(b, o)
                return carry

            lax.fori_loop(0, span, clear_one, 0)

        if span - per_row == 2:
            absent = (1 << span) - 1 - present
            lowest = sum(
                jnp.where(absent % (2 << o) == 0, 1, 0) for o in range(span - 1)
            )
            highest = sum(jnp.where(absent >= (2 << o), 1, 0) for o in range(span - 1))
            clear(b, lowest)
            clear(b, highest)
        else:
            for o in range(span):
                clear(b, o)
        for j in reversed(range(per_row)):
            for c in range(2):
                head, tail = head_and_tail(held[b, j, c])
                high[b, at[j], :, c * size : (c + 1) * size] = head
                low[b, at[j], :, c * size : (c + 1) * size] = tail
        band = slice(block_rows - b, 2 * block_rows - b)
        sums[b] = product(left, high[b, band], low[b, band])


def add_halos(swapped, diagonal, high, low, sums, finish):
    block_rows, span, size, _ = high.shape

    def both(before, after):
        for b in range(block_rows):
            ahead = slice(0, block_rows - b)
            behind = slice(span - 1 - b, span)
            finish(
                b,
                sums[b]
                + product(before[:, b * size :], high[b, ahead], low[b, ahead])
                + product(after[:, : (b + 1) * size], high[b, behind], low[b, behind]),
            )

    swapped, diagonal = pieces(swapped), pieces(diagonal)
    even = lax.axis_index("lat") % 2 == 0

    @pl.when(even)
    def _():
        both(diagonal, swapped)

    @pl.when(jnp.logical_not(even))
    def _():
        both(swapped, diagonal)


def leaving(value):
    channels, size = value.shape[0] // 2, value.shape[1] // 2
    return (
        value[:channels, :size] - value[channels:, size:],
        value[:channels, size:] + value[channels:, :size],
    )


def first_level_kernel(
    swapped, diagonal, swapped_coef, diagonal_coef, high, low, sums, next_coef, out
):
    def finish(b, value):
        re, im = leaving(value)
        channels, size = re.shape
        lanes = slice(b * size, (b + 1) * size)
        re, im = reflected(re, im, next_coef[0:1, lanes], next_coef[1:2, lanes])
        out[:channels, lanes] = re
        out[channels:, lanes] = im

    add_halos(
        entered(swapped, swapped_coef),
        entered(diagonal, diagonal_coef),
        high,
        low,
        sums,
        finish,
    )


def bottom_kernel(swapped, diagonal, high, low, sums, out, held, sems):
    panels, _, part, _ = out.shape
    block_rows, _, size, _ = high.shape

    def copy_out(b):
        lanes = pl.ds(b * size, size)
        return pltpu.make_async_copy(
            held.at[b], out.at[:, :, :, lanes], sems.at[b]
        )

    def finish(b, value):
        re, im = leaving(value)
        held[b, :, 0] = re.reshape(panels, part, size)
        held[b, :, 1] = im.reshape(panels, part, size)
        copy_out(b).start()

    add_halos(swapped[...], diagonal[...], high, low, sums, finish)
    for b in range(block_rows):
        copy_out(b).wait()


def in_hbm(value):
    return pltpu.with_memory_space_constraint(value, pltpu.HBM)


def params(mib):
    return pltpu.CompilerParams(vmem_limit_bytes=mib * MIB)


def cost(flops, transferred):
    return pl.CostEstimate(flops=flops, bytes_accessed=transferred, transcendentals=0)


def per_device(sources, blocks, block_cols, refl_level, refl_coef):
    lat_count = lax.axis_size("lat")
    panels, _, part, points = sources.shape
    _, block_rows, per_row, _, size, _ = blocks.shape
    channels = panels * part
    f32, bf16 = jnp.float32, jnp.bfloat16
    axes = ("depth", "lat")
    over_depth = [(0, 1), (1, 0)]
    even = range(0, lat_count - 1, 2)
    uneven = range(1, lat_count - 1, 2)
    alone_even = range(lat_count - lat_count % 2, lat_count)
    alone_uneven = [0] + list(range(lat_count - 1 + lat_count % 2, lat_count))

    def over_lat(firsts, alone):
        pairs = [(d * lat_count + i, d * lat_count + i + 1) for d in range(2) for i in firsts]
        pairs += [(i, lat_count + i) for i in alone]
        return pairs + [(j, i) for i, j in pairs]

    across = over_lat(uneven, alone_uneven)
    beside = over_lat(even, alone_even)
    other_blocks = lax.ppermute(blocks, "depth", over_depth)
    diagonal = lax.ppermute(sources, axes, across)
    swapped = lax.ppermute(sources, axes, beside)
    other_cols = lax.ppermute(block_cols, "depth", over_depth)
    field_shape = jax.ShapeDtypeStruct((2 * channels, points), f32)
    coef_shape = jax.ShapeDtypeStruct((2, points), f32)
    total, first_coef, next_coef = pl.pallas_call(
        enter_kernel,
        out_shape=[field_shape, coef_shape, coef_shape],
        in_specs=[HBM] * 3,
        out_specs=[VMEM] * 3,
        scratch_shapes=[
            pltpu.VMEM(sources.shape, f32),
            pltpu.VMEM((1, points), jnp.int32),
            pltpu.VMEM((2, points), f32),
            pltpu.SemaphoreType.DMA((3,)),
        ],
        compiler_params=params(4),
        name="enter",
    )(in_hbm(sources), in_hbm(refl_level.reshape(1, points)), in_hbm(refl_coef))
    diagonal_coef = lax.ppermute(first_coef, axes, across)
    swapped_coef = lax.ppermute(first_coef, axes, beside)

    band_shape = jax.ShapeDtypeStruct((block_rows, 2 * block_rows + 1, size, 2 * size), bf16)
    sums_shape = jax.ShapeDtypeStruct((block_rows, 2 * channels, 2 * size), f32)
    macs = 6 * channels * points * 2 * size

    def prepare(level, total):
        return pl.pallas_call(
            functools.partial(prepare_kernel, level),
            out_shape=[band_shape, band_shape, sums_shape],
            in_specs=[SMEM, SMEM, HBM, HBM, VMEM],
            out_specs=[VMEM] * 3,
            scratch_shapes=[
                pltpu.VMEM(blocks.shape[1:], f32),
                pltpu.SemaphoreType.DMA((block_rows,)),
            ],
            compiler_params=params(16),
            cost_estimate=cost(4 * macs, 8 * blocks.size),
            name="prepare",
        )(in_hbm(block_cols), other_cols, in_hbm(blocks), other_blocks, total)

    high, low, sums = prepare(0, total)
    total = pl.pallas_call(
        first_level_kernel,
        out_shape=field_shape,
        in_specs=[VMEM] * 8,
        out_specs=VMEM,
        compiler_params=params(12),
        cost_estimate=cost(2 * macs, blocks.size),
        name="first_level",
    )(swapped, diagonal, swapped_coef, diagonal_coef, high, low, sums, next_coef)
    diagonal = lax.ppermute(total, axes, across)
    swapped = lax.ppermute(total, axes, beside)
    high, low, sums = prepare(1, total)
    return pl.pallas_call(
        bottom_kernel,
        out_shape=jax.ShapeDtypeStruct(sources.shape, f32),
        in_specs=[VMEM] * 5,
        out_specs=HBM,
        scratch_shapes=[
            pltpu.VMEM((block_rows, panels, 2, part, size), f32),
            pltpu.SemaphoreType.DMA((block_rows,)),
        ],
        compiler_params=params(12),
        cost_estimate=cost(2 * macs, blocks.size),
        name="bottom",
    )(swapped, diagonal, high, low, sums)


def solution(mesh):
    placed = (
        P("shot", None, "depth", "lat"),
        P(("shot", "depth"), "lat", None, None, None, None),
        P("depth", "lat", None),
        P("lat"),
        P(None, "lat"),
    )
    return jax.shard_map(
        per_device,
        mesh=mesh,
        in_specs=placed,
        out_specs=P("shot", None, "depth", "lat"),
        check_vma=False,
    )
```

```python
import functools

import jax
import jax.numpy as jnp
from jax import lax
from jax.experimental import pallas as pl
from jax.experimental.pallas import tpu as pltpu
from jax.sharding import PartitionSpec as P

VMEM = pl.BlockSpec(memory_space=pltpu.VMEM)
SMEM = pl.BlockSpec(memory_space=pltpu.SMEM)
HBM = pl.BlockSpec(memory_space=pltpu.HBM)
MIB = 1 << 20


def reflected(field_re, field_im, coef_re, coef_im):
    return (
        field_re + coef_re * field_re - coef_im * field_im,
        field_im + coef_re * field_im + coef_im * field_re,
    )


def entered(sources, coef):
    panels = [
        reflected(sources[k, 0], sources[k, 1], coef[0:1, :], coef[1:2, :])
        for k in range(sources.shape[0])
    ]
    return jnp.concatenate([re for re, _ in panels] + [im for _, im in panels], axis=0)


def enter_kernel(
    sources, refl_level, refl_coef, total, first_coef, next_coef, held, level_held, coef_held, sems
):
    copies = [
        pltpu.make_async_copy(a, b, sems.at[i])
        for i, (a, b) in enumerate(
            ((sources, held), (refl_level, level_held), (refl_coef, coef_held))
        )
    ]
    for copy in copies:
        copy.start()
    for copy in copies:
        copy.wait()
    first_coef[...] = jnp.where(level_held[...] == 0, coef_held[...], 0.0)
    next_coef[...] = jnp.where(level_held[...] == 1, coef_held[...], 0.0)
    total[...] = entered(held, first_coef)


def head_and_tail(value):
    head = value.astype(jnp.bfloat16)
    return head, (value - head.astype(jnp.float32)).astype(jnp.bfloat16)


def pieces(value):
    return jnp.concatenate(head_and_tail(value), axis=0)


def product(left, high, low):
    rows = left.shape[0] // 2
    high = high.reshape(high.shape[0] * high.shape[1], high.shape[2])
    low = low.reshape(high.shape)
    both = jnp.dot(left, high, preferred_element_type=jnp.float32)
    cross = jnp.dot(left[:rows], low, preferred_element_type=jnp.float32)
    return both[:rows] + both[rows:] + cross


def prepare_kernel(
    level, own_cols, other_cols, own, received, field, high, low, sums, held, left, sems
):
    block_rows, per_row, _, size, _ = held.shape
    here = lax.axis_index("depth") == level
    first_row = lax.axis_index("lat") * block_rows
    for b in range(block_rows):

        @pl.when(here)
        def _():
            pltpu.make_async_copy(own.at[0, b], held.at[b], sems.at[b]).start()

        @pl.when(jnp.logical_not(here))
        def _():
            pltpu.make_async_copy(received.at[0, b], held.at[b], sems.at[b]).start()

    span = 2 * block_rows + 1
    zeros = jnp.zeros((size, 2 * size), jnp.bfloat16)

    def clear(b, o):
        high[b, o] = zeros
        low[b, o] = zeros

    rows_at, rows_repeated = [], []
    for b in range(block_rows):
        first = first_row + b - block_rows
        at = [
            jnp.where(here, own_cols[0, b, j], other_cols[0, b, j]) - first
            for j in range(per_row)
        ]
        bits = [jnp.left_shift(1, a) for a in at]
        present = functools.reduce(jnp.bitwise_or, bits)
        repeated = sum(bits) != present
        rows_at.append(at)
        rows_repeated.append(repeated)
        absent = (1 << span) - 1 - present
        if span - per_row == 2:
            clear(b, sum(jnp.where(absent % (2 << o) == 0, 1, 0) for o in range(span - 1)))
            clear(b, sum(jnp.where(absent >= (2 << o), 1, 0) for o in range(span - 1)))
        else:
            repeated = True

        @pl.when(repeated)
        def _():
            def clear_one(o, carry):
                @pl.when(jnp.bitwise_and(jnp.right_shift(absent, o), 1) == 1)
                def _():
                    clear(b, o)

                return carry

            lax.fori_loop(0, span, clear_one, 0)

    left[...] = pieces(field[...])
    for b in range(block_rows):
        at = rows_at[b]
        pltpu.make_async_copy(own.at[0, b], held.at[b], sems.at[b]).wait()

        @pl.when(rows_repeated[b])
        def _():
            for j in reversed(range(1, per_row)):
                target = jnp.int32(per_row)
                for i in range(j):
                    target = jnp.where(at[i] == at[j], i, target)

                @pl.when(target < per_row)
                def _():
                    held[b, target] = held[b, target] + held[b, j]

        def split(n, carry):
            rows = pl.ds(pl.multiple_of(n * 16, 16), 16)
            for j in reversed(range(per_row)):
                head, tail = head_and_tail(
                    jnp.concatenate([held[b, j, 0, rows], held[b, j, 1, rows]], axis=1)
                )
                high[b, at[j], rows] = head
                low[b, at[j], rows] = tail
            return carry

        lax.fori_loop(0, size // 16, split, 0)
    for b in range(block_rows):
        band = slice(block_rows - b, 2 * block_rows - b)
        sums[b] = product(left[...], high[b, band], low[b, band])


def add_halos(swapped, diagonal, high, low, sums, finish):
    block_rows, span, size, _ = high.shape

    def both(before, after):
        for b in range(block_rows):
            ahead = slice(0, block_rows - b)
            behind = slice(span - 1 - b, span)
            finish(
                b,
                sums[b]
                + product(before[:, b * size :], high[b, ahead], low[b, ahead])
                + product(after[:, : (b + 1) * size], high[b, behind], low[b, behind]),
            )

    swapped, diagonal = pieces(swapped), pieces(diagonal)
    even = lax.axis_index("lat") % 2 == 0

    @pl.when(even)
    def _():
        both(diagonal, swapped)

    @pl.when(jnp.logical_not(even))
    def _():
        both(swapped, diagonal)


def leaving(value):
    channels, size = value.shape[0] // 2, value.shape[1] // 2
    return (
        value[:channels, :size] - value[channels:, size:],
        value[:channels, size:] + value[channels:, :size],
    )


def first_level_kernel(
    swapped, diagonal, swapped_coef, diagonal_coef, high, low, sums, next_coef, out
):
    def finish(b, value):
        re, im = leaving(value)
        channels, size = re.shape
        lanes = slice(b * size, (b + 1) * size)
        re, im = reflected(re, im, next_coef[0:1, lanes], next_coef[1:2, lanes])
        out[:channels, lanes] = re
        out[channels:, lanes] = im

    add_halos(
        entered(swapped, swapped_coef),
        entered(diagonal, diagonal_coef),
        high,
        low,
        sums,
        finish,
    )


def bottom_kernel(swapped, diagonal, high, low, sums, out, held, sems):
    panels, _, part, _ = out.shape
    block_rows, _, size, _ = high.shape

    def copy_out(b):
        lanes = pl.ds(b * size, size)
        return pltpu.make_async_copy(
            held.at[b], out.at[:, :, :, lanes], sems.at[b]
        )

    def finish(b, value):
        re, im = leaving(value)
        held[b, :, 0] = re.reshape(panels, part, size)
        held[b, :, 1] = im.reshape(panels, part, size)
        copy_out(b).start()

    add_halos(swapped[...], diagonal[...], high, low, sums, finish)
    for b in range(block_rows):
        copy_out(b).wait()


def in_hbm(value):
    return pltpu.with_memory_space_constraint(value, pltpu.HBM)


def params(mib):
    return pltpu.CompilerParams(vmem_limit_bytes=mib * MIB)


def cost(flops, transferred):
    return pl.CostEstimate(flops=flops, bytes_accessed=transferred, transcendentals=0)


def per_device(sources, blocks, block_cols, refl_level, refl_coef):
    lat_count = lax.axis_size("lat")
    panels, _, part, points = sources.shape
    _, block_rows, per_row, _, size, _ = blocks.shape
    channels = panels * part
    f32, bf16 = jnp.float32, jnp.bfloat16
    axes = ("depth", "lat")
    over_depth = [(0, 1), (1, 0)]
    even = range(0, lat_count - 1, 2)
    uneven = range(1, lat_count - 1, 2)
    alone_even = range(lat_count - lat_count % 2, lat_count)
    alone_uneven = [0] + list(range(lat_count - 1 + lat_count % 2, lat_count))

    def over_lat(firsts, alone):
        pairs = [(d * lat_count + i, d * lat_count + i + 1) for d in range(2) for i in firsts]
        pairs += [(i, lat_count + i) for i in alone]
        return pairs + [(j, i) for i, j in pairs]

    across = over_lat(uneven, alone_uneven)
    beside = over_lat(even, alone_even)
    other_blocks = lax.ppermute(blocks, "depth", over_depth)
    diagonal = lax.ppermute(sources, axes, across)
    swapped = lax.ppermute(sources, axes, beside)
    other_cols = lax.ppermute(block_cols, "depth", over_depth)
    field_shape = jax.ShapeDtypeStruct((2 * channels, points), f32)
    coef_shape = jax.ShapeDtypeStruct((2, points), f32)
    total, first_coef, next_coef = pl.pallas_call(
        enter_kernel,
        out_shape=[field_shape, coef_shape, coef_shape],
        in_specs=[HBM] * 3,
        out_specs=[VMEM] * 3,
        scratch_shapes=[
            pltpu.VMEM(sources.shape, f32),
            pltpu.VMEM((1, points), jnp.int32),
            pltpu.VMEM((2, points), f32),
            pltpu.SemaphoreType.DMA((3,)),
        ],
        compiler_params=params(4),
        name="enter",
    )(in_hbm(sources), in_hbm(refl_level.reshape(1, points)), in_hbm(refl_coef))
    diagonal_coef = lax.ppermute(first_coef, axes, across)
    swapped_coef = lax.ppermute(first_coef, axes, beside)

    band_shape = jax.ShapeDtypeStruct((block_rows, 2 * block_rows + 1, size, 2 * size), bf16)
    sums_shape = jax.ShapeDtypeStruct((block_rows, 2 * channels, 2 * size), f32)
    macs = 6 * channels * points * 2 * size

    def prepare(level, total):
        return pl.pallas_call(
            functools.partial(prepare_kernel, level),
            out_shape=[band_shape, band_shape, sums_shape],
            in_specs=[SMEM, SMEM, HBM, HBM, VMEM],
            out_specs=[VMEM] * 3,
            scratch_shapes=[
                pltpu.VMEM(blocks.shape[1:], f32),
                pltpu.VMEM((4 * channels, points), bf16),
                pltpu.SemaphoreType.DMA((block_rows,)),
            ],
            compiler_params=params(16),
            cost_estimate=cost(4 * macs, 8 * blocks.size),
            name="prepare",
        )(in_hbm(block_cols), other_cols, in_hbm(blocks), other_blocks, total)

    high, low, sums = prepare(0, total)
    total = pl.pallas_call(
        first_level_kernel,
        out_shape=field_shape,
        in_specs=[VMEM] * 8,
        out_specs=VMEM,
        compiler_params=params(12),
        cost_estimate=cost(2 * macs, blocks.size),
        name="first_level",
    )(swapped, diagonal, swapped_coef, diagonal_coef, high, low, sums, next_coef)
    diagonal = lax.ppermute(total, axes, across)
    swapped = lax.ppermute(total, axes, beside)
    high, low, sums = prepare(1, total)
    return pl.pallas_call(
        bottom_kernel,
        out_shape=jax.ShapeDtypeStruct(sources.shape, f32),
        in_specs=[VMEM] * 5,
        out_specs=HBM,
        scratch_shapes=[
            pltpu.VMEM((block_rows, panels, 2, part, size), f32),
            pltpu.SemaphoreType.DMA((block_rows,)),
        ],
        compiler_params=params(12),
        cost_estimate=cost(2 * macs, blocks.size),
        name="bottom",
    )(swapped, diagonal, high, low, sums)


def solution(mesh):
    placed = (
        P("shot", None, "depth", "lat"),
        P(("shot", "depth"), "lat", None, None, None, None),
        P("depth", "lat", None),
        P("lat"),
        P(None, "lat"),
    )
    return jax.shard_map(
        per_device,
        mesh=mesh,
        in_specs=placed,
        out_specs=P("shot", None, "depth", "lat"),
        check_vma=False,
    )
```

```python
import functools

import jax
import jax.numpy as jnp
from jax import lax
from jax.experimental import pallas as pl
from jax.experimental.pallas import tpu as pltpu
from jax.sharding import PartitionSpec as P

VMEM = pl.BlockSpec(memory_space=pltpu.VMEM)
SMEM = pl.BlockSpec(memory_space=pltpu.SMEM)
HBM = pl.BlockSpec(memory_space=pltpu.HBM)
MIB = 1 << 20


def reflected(field_re, field_im, coef_re, coef_im):
    return (
        field_re + coef_re * field_re - coef_im * field_im,
        field_im + coef_re * field_im + coef_im * field_re,
    )


def entered(sources, coef):
    panels = [
        reflected(sources[k, 0], sources[k, 1], coef[0:1, :], coef[1:2, :])
        for k in range(sources.shape[0])
    ]
    return jnp.concatenate([re for re, _ in panels] + [im for _, im in panels], axis=0)


def enter_kernel(
    sources, refl_level, refl_coef, total, first_coef, next_coef, held, level_held, coef_held, sems
):
    copies = [
        pltpu.make_async_copy(a, b, sems.at[i])
        for i, (a, b) in enumerate(
            ((sources, held), (refl_level, level_held), (refl_coef, coef_held))
        )
    ]
    for copy in copies:
        copy.start()
    for copy in copies:
        copy.wait()
    first_coef[...] = jnp.where(level_held[...] == 0, coef_held[...], 0.0)
    next_coef[...] = jnp.where(level_held[...] == 1, coef_held[...], 0.0)
    total[...] = entered(held, first_coef)


def head_and_tail(value):
    head = value.astype(jnp.bfloat16)
    return head, (value - head.astype(jnp.float32)).astype(jnp.bfloat16)


def pieces(value):
    return jnp.concatenate(head_and_tail(value), axis=0)


def product(left, high, low):
    rows = left.shape[0] // 2
    high = high.reshape(high.shape[0] * high.shape[1], high.shape[2])
    low = low.reshape(high.shape)
    both = jnp.dot(left, high, preferred_element_type=jnp.float32)
    cross = jnp.dot(left[:rows], low, preferred_element_type=jnp.float32)
    return both[:rows] + both[rows:] + cross


def prepare_kernel(
    level, own_cols, other_cols, own, received, field, high, low, sums, held, left, sems
):
    block_rows, per_row, _, size, _ = held.shape
    here = lax.axis_index("depth") == level
    first_row = lax.axis_index("lat") * block_rows
    for b in range(block_rows):

        @pl.when(here)
        def _():
            pltpu.make_async_copy(own.at[0, b], held.at[b], sems.at[b]).start()

        @pl.when(jnp.logical_not(here))
        def _():
            pltpu.make_async_copy(received.at[0, b], held.at[b], sems.at[b]).start()

    span = 2 * block_rows + 1
    zeros = jnp.zeros((size, 2 * size), jnp.bfloat16)

    def clear(b, o):
        high[b, o] = zeros
        low[b, o] = zeros

    rows_at, rows_repeated = [], []
    for b in range(block_rows):
        first = first_row + b - block_rows
        at = [
            jnp.where(here, own_cols[0, b, j], other_cols[0, b, j]) - first
            for j in range(per_row)
        ]
        bits = [jnp.left_shift(1, a) for a in at]
        present = functools.reduce(jnp.bitwise_or, bits)
        repeated = sum(bits) != present
        rows_at.append(at)
        rows_repeated.append(repeated)
        absent = (1 << span) - 1 - present
        if span - per_row == 2:
            clear(b, sum(jnp.where(absent % (2 << o) == 0, 1, 0) for o in range(span - 1)))
            clear(b, sum(jnp.where(absent >= (2 << o), 1, 0) for o in range(span - 1)))
        else:
            repeated = True

        @pl.when(repeated)
        def _():
            def clear_one(o, carry):
                @pl.when(jnp.bitwise_and(jnp.right_shift(absent, o), 1) == 1)
                def _():
                    clear(b, o)

                return carry

            lax.fori_loop(0, span, clear_one, 0)

    left[...] = pieces(field[...])
    for b in range(block_rows):
        at = rows_at[b]
        pltpu.make_async_copy(own.at[0, b], held.at[b], sems.at[b]).wait()

        @pl.when(rows_repeated[b])
        def _():
            for j in reversed(range(1, per_row)):
                target = jnp.int32(per_row)
                for i in range(j):
                    target = jnp.where(at[i] == at[j], i, target)

                @pl.when(target < per_row)
                def _():
                    held[b, target] = held[b, target] + held[b, j]

        def split(n, carry):
            rows = pl.ds(pl.multiple_of(n * 16, 16), 16)
            for j in reversed(range(per_row)):
                head, tail = head_and_tail(
                    jnp.concatenate([held[b, j, 0, rows], held[b, j, 1, rows]], axis=1)
                )
                high[b, at[j], rows] = head
                low[b, at[j], rows] = tail
            return carry

        lax.fori_loop(0, size // 16, split, 0)
    for b in range(block_rows):
        band = slice(block_rows - b, 2 * block_rows - b)
        sums[b] = product(left[...], high[b, band], low[b, band])


def add_halo(value, is_left, left, high, low, sums, finish):
    block_rows, span, size, _ = high.shape
    left[...] = pieces(value)

    @pl.when(is_left)
    def _():
        for b in range(block_rows):
            band = slice(0, block_rows - b)
            part = product(left[:, b * size :], high[b, band], low[b, band])
            finish(b, sums[b] + part)

    @pl.when(jnp.logical_not(is_left))
    def _():
        for b in range(block_rows):
            band = slice(span - 1 - b, span)
            part = product(left[:, : (b + 1) * size], high[b, band], low[b, band])
            finish(b, sums[b] + part)


def odd_position():
    return lax.axis_index("lat") % 2 == 1


def swapped_kernel(reflects, halo, *refs):
    coef, (high, low, sums, out, left) = refs[:reflects], refs[reflects:]

    def finish(b, value):
        out[b] = value

    value = entered(halo, coef[0]) if reflects else halo[...]
    add_halo(value, odd_position(), left, high, low, sums, finish)


def leaving(value):
    channels, size = value.shape[0] // 2, value.shape[1] // 2
    return (
        value[:channels, :size] - value[channels:, size:],
        value[:channels, size:] + value[channels:, :size],
    )


def first_level_kernel(halo, coef, high, low, sums, next_coef, out, left):
    def finish(b, value):
        re, im = leaving(value)
        channels, size = re.shape
        lanes = slice(b * size, (b + 1) * size)
        re, im = reflected(re, im, next_coef[0:1, lanes], next_coef[1:2, lanes])
        out[:channels, lanes] = re
        out[channels:, lanes] = im

    is_left = jnp.logical_not(odd_position())
    add_halo(entered(halo, coef), is_left, left, high, low, sums, finish)


def bottom_kernel(halo, high, low, sums, out, held, left, sems):
    panels, _, part, _ = out.shape
    block_rows, _, size, _ = high.shape

    def copy_out(b):
        lanes = pl.ds(b * size, size)
        return pltpu.make_async_copy(
            held.at[b], out.at[:, :, :, lanes], sems.at[b]
        )

    def finish(b, value):
        re, im = leaving(value)
        held[b, :, 0] = re.reshape(panels, part, size)
        held[b, :, 1] = im.reshape(panels, part, size)
        copy_out(b).start()

    is_left = jnp.logical_not(odd_position())
    add_halo(halo[...], is_left, left, high, low, sums, finish)
    for b in range(block_rows):
        copy_out(b).wait()


def in_hbm(value):
    return pltpu.with_memory_space_constraint(value, pltpu.HBM)


def params(mib):
    return pltpu.CompilerParams(vmem_limit_bytes=mib * MIB)


def cost(flops, transferred):
    return pl.CostEstimate(flops=flops, bytes_accessed=transferred, transcendentals=0)


def per_device(sources, blocks, block_cols, refl_level, refl_coef):
    lat_count = lax.axis_size("lat")
    panels, _, part, points = sources.shape
    _, block_rows, per_row, _, size, _ = blocks.shape
    channels = panels * part
    f32, bf16 = jnp.float32, jnp.bfloat16
    axes = ("depth", "lat")
    over_depth = [(0, 1), (1, 0)]
    even = range(0, lat_count - 1, 2)
    uneven = range(1, lat_count - 1, 2)
    alone_even = range(lat_count - lat_count % 2, lat_count)
    alone_uneven = [0] + list(range(lat_count - 1 + lat_count % 2, lat_count))

    def over_lat(firsts, alone):
        pairs = [(d * lat_count + i, d * lat_count + i + 1) for d in range(2) for i in firsts]
        pairs += [(i, lat_count + i) for i in alone]
        return pairs + [(j, i) for i, j in pairs]

    across = over_lat(uneven, alone_uneven)
    beside = over_lat(even, alone_even)
    other_blocks = lax.ppermute(blocks, "depth", over_depth)
    swapped = lax.ppermute(sources, axes, beside)
    other_cols = lax.ppermute(block_cols, "depth", over_depth)
    field_shape = jax.ShapeDtypeStruct((2 * channels, points), f32)
    coef_shape = jax.ShapeDtypeStruct((2, points), f32)
    total, first_coef, next_coef = pl.pallas_call(
        enter_kernel,
        out_shape=[field_shape, coef_shape, coef_shape],
        in_specs=[HBM] * 3,
        out_specs=[VMEM] * 3,
        scratch_shapes=[
            pltpu.VMEM(sources.shape, f32),
            pltpu.VMEM((1, points), jnp.int32),
            pltpu.VMEM((2, points), f32),
            pltpu.SemaphoreType.DMA((3,)),
        ],
        compiler_params=params(4),
        name="enter",
    )(in_hbm(sources), in_hbm(refl_level.reshape(1, points)), in_hbm(refl_coef))
    late_sources, first_coef = lax.optimization_barrier((sources, first_coef))
    diagonal = lax.ppermute(late_sources, axes, across)
    diagonal_coef = lax.ppermute(first_coef, axes, across)
    swapped_coef = lax.ppermute(first_coef, axes, beside)

    band_shape = jax.ShapeDtypeStruct((block_rows, 2 * block_rows + 1, size, 2 * size), bf16)
    sums_shape = jax.ShapeDtypeStruct((block_rows, 2 * channels, 2 * size), f32)
    macs = 6 * channels * points * 2 * size

    def prepare(level, total):
        return pl.pallas_call(
            functools.partial(prepare_kernel, level),
            out_shape=[band_shape, band_shape, sums_shape],
            in_specs=[SMEM, SMEM, HBM, HBM, VMEM],
            out_specs=[VMEM] * 3,
            scratch_shapes=[
                pltpu.VMEM(blocks.shape[1:], f32),
                pltpu.VMEM((4 * channels, points), bf16),
                pltpu.SemaphoreType.DMA((block_rows,)),
            ],
            compiler_params=params(16),
            cost_estimate=cost(4 * macs, 8 * blocks.size),
            name="prepare",
        )(in_hbm(block_cols), other_cols, in_hbm(blocks), other_blocks, total)

    left_scratch = pltpu.VMEM((4 * channels, points), bf16)

    def add_swapped(*operands):
        return pl.pallas_call(
            functools.partial(swapped_kernel, len(operands) - 4),
            out_shape=sums_shape,
            in_specs=[VMEM] * len(operands),
            out_specs=VMEM,
            scratch_shapes=[left_scratch],
            compiler_params=params(12),
            cost_estimate=cost(macs, blocks.size),
            name="swapped",
        )(*operands)

    high, low, sums = prepare(0, total)
    sums = add_swapped(swapped, swapped_coef, high, low, sums)
    total = pl.pallas_call(
        first_level_kernel,
        out_shape=field_shape,
        in_specs=[VMEM] * 6,
        out_specs=VMEM,
        scratch_shapes=[left_scratch],
        compiler_params=params(12),
        cost_estimate=cost(macs, blocks.size),
        name="first_level",
    )(diagonal, diagonal_coef, high, low, sums, next_coef)
    swapped = lax.ppermute(total, axes, beside)
    high, low, sums = prepare(1, total)
    late_total, sums = lax.optimization_barrier((total, sums))
    diagonal = lax.ppermute(late_total, axes, across)
    sums = add_swapped(swapped, high, low, sums)
    return pl.pallas_call(
        bottom_kernel,
        out_shape=jax.ShapeDtypeStruct(sources.shape, f32),
        in_specs=[VMEM] * 4,
        out_specs=HBM,
        scratch_shapes=[
            pltpu.VMEM((block_rows, panels, 2, part, size), f32),
            left_scratch,
            pltpu.SemaphoreType.DMA((block_rows,)),
        ],
        compiler_params=params(12),
        cost_estimate=cost(macs, blocks.size),
        name="bottom",
    )(diagonal, high, low, sums)


def solution(mesh):
    placed = (
        P("shot", None, "depth", "lat"),
        P(("shot", "depth"), "lat", None, None, None, None),
        P("depth", "lat", None),
        P("lat"),
        P(None, "lat"),
    )
    return jax.shard_map(
        per_device,
        mesh=mesh,
        in_specs=placed,
        out_specs=P("shot", None, "depth", "lat"),
        check_vma=False,
    )
```

```python
import functools

import jax
import jax.numpy as jnp
from jax import lax
from jax.experimental import pallas as pl
from jax.experimental.pallas import tpu as pltpu
from jax.sharding import PartitionSpec as P


VMEM = pl.BlockSpec(memory_space=pltpu.VMEM)
SMEM = pl.BlockSpec(memory_space=pltpu.SMEM)
HBM = pl.BlockSpec(memory_space=pltpu.HBM)
MIB = 1 << 20


def reflected(field_re, field_im, coef_re, coef_im):
    return (
        field_re + coef_re * field_re - coef_im * field_im,
        field_im + coef_re * field_im + coef_im * field_re,
    )


def entered(sources, coef):
    panels = [
        reflected(sources[k, 0], sources[k, 1], coef[0:1, :], coef[1:2, :])
        for k in range(sources.shape[0])
    ]
    return jnp.concatenate([re for re, _ in panels] + [im for _, im in panels], axis=0)


def enter_kernel(
    sources, refl_level, refl_coef, total, first_coef, next_coef, held, level_held, coef_held, sems
):
    copies = [
        pltpu.make_async_copy(a, b, sems.at[i])
        for i, (a, b) in enumerate(
            ((sources, held), (refl_level, level_held), (refl_coef, coef_held))
        )
    ]
    for copy in copies:
        copy.start()
    for copy in copies:
        copy.wait()
    first_coef[...] = jnp.where(level_held[...] == 0, coef_held[...], 0.0)
    next_coef[...] = jnp.where(level_held[...] == 1, coef_held[...], 0.0)
    total[...] = entered(held, first_coef)


def head_and_tail(value):
    head = value.astype(jnp.bfloat16)
    return head, (value - head.astype(jnp.float32)).astype(jnp.bfloat16)


def pieces(value):
    return jnp.concatenate(head_and_tail(value), axis=0)


def product(left, high, low):
    rows = left.shape[0] // 2
    high = high.reshape(high.shape[0] * high.shape[1], high.shape[2])
    low = low.reshape(high.shape)
    both = jnp.dot(left, high, preferred_element_type=jnp.float32)
    cross = jnp.dot(left[:rows], low, preferred_element_type=jnp.float32)
    return both[:rows] + both[rows:] + cross


def prepare_kernel(level, own_cols, other_cols, own, received, *refs):
    fields, (high, low, sums, held, left, sems) = refs[:-6], refs[-6:]
    block_rows, per_row, _, size, _ = held.shape
    here = lax.axis_index("depth") == level
    first_row = lax.axis_index("lat") * block_rows
    for b in range(block_rows):

        @pl.when(here)
        def _():
            pltpu.make_async_copy(own.at[0, b], held.at[b], sems.at[b]).start()

        @pl.when(jnp.logical_not(here))
        def _():
            pltpu.make_async_copy(received.at[0, b], held.at[b], sems.at[b]).start()

    span = 2 * block_rows + 1
    zeros = jnp.zeros((size, 2 * size), jnp.bfloat16)

    def clear(b, o):
        high[b, o] = zeros
        low[b, o] = zeros

    rows_at, rows_repeated = [], []
    for b in range(block_rows):
        first = first_row + b - block_rows
        at = [
            jnp.where(here, own_cols[0, b, j], other_cols[0, b, j]) - first
            for j in range(per_row)
        ]
        bits = [jnp.left_shift(1, a) for a in at]
        present = functools.reduce(jnp.bitwise_or, bits)
        repeated = sum(bits) != present
        rows_at.append(at)
        rows_repeated.append(repeated)
        absent = (1 << span) - 1 - present
        if span - per_row == 2:
            clear(b, sum(jnp.where(absent % (2 << o) == 0, 1, 0) for o in range(span - 1)))
            clear(b, sum(jnp.where(absent >= (2 << o), 1, 0) for o in range(span - 1)))
        else:
            repeated = True

        @pl.when(repeated)
        def _():
            def clear_one(o, carry):
                @pl.when(jnp.bitwise_and(jnp.right_shift(absent, o), 1) == 1)
                def _():
                    clear(b, o)

                return carry

            lax.fori_loop(0, span, clear_one, 0)

    at_lane = 0
    for field in fields:
        left[:, at_lane : at_lane + field.shape[1]] = pieces(field[...])
        at_lane += field.shape[1]
    for b in range(block_rows):
        at = rows_at[b]
        pltpu.make_async_copy(own.at[0, b], held.at[b], sems.at[b]).wait()

        @pl.when(rows_repeated[b])
        def _():
            for j in reversed(range(1, per_row)):
                target = jnp.int32(per_row)
                for i in range(j):
                    target = jnp.where(at[i] == at[j], i, target)

                @pl.when(target < per_row)
                def _():
                    held[b, target] = held[b, target] + held[b, j]

        def split(n, carry):
            rows = pl.ds(pl.multiple_of(n * 16, 16), 16)
            for j in reversed(range(per_row)):
                head, tail = head_and_tail(
                    jnp.concatenate([held[b, j, 0, rows], held[b, j, 1, rows]], axis=1)
                )
                high[b, at[j], rows] = head
                low[b, at[j], rows] = tail
            return carry

        lax.fori_loop(0, size // 16, split, 0)
    for b in range(block_rows):
        band = slice(block_rows - b, 2 * block_rows - b)
        sums[b] = product(left[...], high[b, band], low[b, band])


def order(swapped, diagonal, before, after):
    even = lax.axis_index("lat") % 2 == 0

    @pl.when(even)
    def _():
        before[...] = pieces(diagonal())
        after[...] = pieces(swapped())

    @pl.when(jnp.logical_not(even))
    def _():
        before[...] = pieces(swapped())
        after[...] = pieces(diagonal())


def halo_product(b, first, before, after, high, low):
    block_rows, _, size, _ = high.shape
    last = first + before.shape[1] // size
    total = 0.0
    low_col, high_col = max(b, first), last
    if low_col < high_col:
        lanes = slice((low_col - first) * size, (high_col - first) * size)
        band = slice(low_col - b, high_col - b)
        total = total + product(before[:, lanes], high[b, band], low[b, band])
    low_col, high_col = first, min(b + 1, last)
    if low_col < high_col:
        lanes = slice(0, (high_col - first) * size)
        band = slice(2 * block_rows - b + low_col, 2 * block_rows - b + high_col)
        total = total + product(after[:, lanes], high[b, band], low[b, band])
    return total


def leaving(value):
    channels, size = value.shape[0] // 2, value.shape[1] // 2
    return (
        value[:channels, :size] - value[channels:, size:],
        value[:channels, size:] + value[channels:, :size],
    )


def level_rows(rows, before, after, high, low, sums, next_coef, out):
    for i, b in enumerate(rows):
        re, im = leaving(sums[b] + halo_product(b, 0, before, after, high, low))
        channels, size = re.shape
        lanes = slice(b * size, (b + 1) * size)
        re, im = reflected(re, im, next_coef[0:1, lanes], next_coef[1:2, lanes])
        lanes = slice(i * size, (i + 1) * size)
        out[:channels, lanes] = re
        out[channels:, lanes] = im


def first_rows_kernel(
    rows,
    swapped,
    diagonal,
    swapped_coef,
    diagonal_coef,
    high,
    low,
    sums,
    next_coef,
    out,
    before,
    after,
):
    order(
        lambda: entered(swapped, swapped_coef),
        lambda: entered(diagonal, diagonal_coef),
        before,
        after,
    )
    level_rows(rows, before, after, high, low, sums, next_coef, out)


def first_bottom_kernel(swapped, diagonal, high, low, sums, out, before, after):
    order(lambda: swapped[...], lambda: diagonal[...], before, after)
    for b in range(high.shape[0]):
        out[b] = sums[b] + halo_product(b, 0, before, after, high, low)


def bottom_kernel(first, swapped, diagonal, high, low, sums, out, held, before, after, sems):
    panels, _, part, _ = out.shape
    block_rows, _, size, _ = high.shape
    order(lambda: swapped[...], lambda: diagonal[...], before, after)
    copies = []
    for b in range(block_rows):
        re, im = leaving(sums[b] + halo_product(b, first, before, after, high, low))
        held[b, :, 0] = re.reshape(panels, part, size)
        held[b, :, 1] = im.reshape(panels, part, size)
        lanes = pl.ds(b * size, size)
        copies.append(
            pltpu.make_async_copy(held.at[b], out.at[:, :, :, lanes], sems.at[b])
        )
        copies[-1].start()
    for copy in copies:
        copy.wait()


def in_hbm(value):
    return pltpu.with_memory_space_constraint(value, pltpu.HBM)


def params(mib):
    return pltpu.CompilerParams(vmem_limit_bytes=mib * MIB)


def cost(flops, transferred):
    return pl.CostEstimate(flops=flops, bytes_accessed=transferred, transcendentals=0)


def per_device(sources, blocks, block_cols, refl_level, refl_coef):
    lat_count = lax.axis_size("lat")
    panels, _, part, points = sources.shape
    _, block_rows, _, _, size, _ = blocks.shape
    channels = panels * part
    f32, bf16 = jnp.float32, jnp.bfloat16
    axes = ("depth", "lat")
    over_depth = [(0, 1), (1, 0)]
    even = range(0, lat_count - 1, 2)
    uneven = range(1, lat_count - 1, 2)
    alone_even = range(lat_count - lat_count % 2, lat_count)
    alone_uneven = [0] + list(range(lat_count - 1 + lat_count % 2, lat_count))

    def over_lat(firsts, alone):
        pairs = [(d * lat_count + i, d * lat_count + i + 1) for d in range(2) for i in firsts]
        pairs += [(i, lat_count + i) for i in alone]
        return pairs + [(j, i) for i, j in pairs]

    across = over_lat(uneven, alone_uneven)
    beside = over_lat(even, alone_even)
    other_blocks = lax.ppermute(blocks, "depth", over_depth)
    diagonal = lax.ppermute(sources, axes, across)
    swapped = lax.ppermute(sources, axes, beside)
    other_cols = lax.ppermute(block_cols, "depth", over_depth)
    field_shape = jax.ShapeDtypeStruct((2 * channels, points), f32)
    coef_shape = jax.ShapeDtypeStruct((2, points), f32)
    total, first_coef, next_coef = pl.pallas_call(
        enter_kernel,
        out_shape=[field_shape, coef_shape, coef_shape],
        in_specs=[HBM] * 3,
        out_specs=[VMEM] * 3,
        scratch_shapes=[
            pltpu.VMEM(sources.shape, f32),
            pltpu.VMEM((1, points), jnp.int32),
            pltpu.VMEM((2, points), f32),
            pltpu.SemaphoreType.DMA((3,)),
        ],
        compiler_params=params(4),
        name="enter",
    )(in_hbm(sources), in_hbm(refl_level.reshape(1, points)), in_hbm(refl_coef))
    diagonal_coef = lax.ppermute(first_coef, axes, across)
    swapped_coef = lax.ppermute(first_coef, axes, beside)

    band_shape = jax.ShapeDtypeStruct((block_rows, 2 * block_rows + 1, size, 2 * size), bf16)
    sums_shape = jax.ShapeDtypeStruct((block_rows, 2 * channels, 2 * size), f32)
    macs = 6 * channels * points * 2 * size

    def prepare(level, *fields):
        return pl.pallas_call(
            functools.partial(prepare_kernel, level),
            out_shape=[band_shape, band_shape, sums_shape],
            in_specs=[SMEM, SMEM, HBM, HBM] + [VMEM] * len(fields),
            out_specs=[VMEM] * 3,
            scratch_shapes=[
                pltpu.VMEM(blocks.shape[1:], f32),
                pltpu.VMEM((4 * channels, points), bf16),
                pltpu.SemaphoreType.DMA((block_rows,)),
            ],
            compiler_params=params(16),
            cost_estimate=cost(4 * macs, 8 * blocks.size),
            name="prepare",
        )(in_hbm(block_cols), other_cols, in_hbm(blocks), other_blocks, *fields)

    half = block_rows // 2
    first_rows, second_rows = range(half), range(half, block_rows)

    def part_shape(rows):
        return jax.ShapeDtypeStruct((2 * channels, len(rows) * size), f32)

    def piece_shape(rows):
        return (4 * channels, len(rows) * size), bf16

    every_row = range(block_rows)
    high, low, sums = prepare(0, total)
    first_part, before, after = pl.pallas_call(
        functools.partial(first_rows_kernel, first_rows),
        out_shape=[
            part_shape(first_rows),
            jax.ShapeDtypeStruct(*piece_shape(every_row)),
            jax.ShapeDtypeStruct(*piece_shape(every_row)),
        ],
        in_specs=[VMEM] * 8,
        out_specs=[VMEM] * 3,
        compiler_params=params(12),
        cost_estimate=cost(macs, blocks.size),
        name="first_rows",
    )(swapped, diagonal, swapped_coef, diagonal_coef, high, low, sums, next_coef)
    first_diagonal = lax.ppermute(first_part, axes, across)
    first_swapped = lax.ppermute(first_part, axes, beside)
    second_part = pl.pallas_call(
        functools.partial(level_rows, second_rows),
        out_shape=part_shape(second_rows),
        in_specs=[VMEM] * 6,
        out_specs=VMEM,
        compiler_params=params(12),
        cost_estimate=cost(macs, blocks.size),
        name="second_rows",
    )(before, after, high, low, sums, next_coef)
    second_diagonal = lax.ppermute(second_part, axes, across)
    second_swapped = lax.ppermute(second_part, axes, beside)
    high, low, sums = prepare(1, first_part, second_part)
    sums = pl.pallas_call(
        first_bottom_kernel,
        out_shape=sums_shape,
        in_specs=[VMEM] * 5,
        out_specs=VMEM,
        scratch_shapes=[pltpu.VMEM(*piece_shape(first_rows))] * 2,
        compiler_params=params(12),
        cost_estimate=cost(macs, blocks.size),
        name="first_bottom",
    )(first_swapped, first_diagonal, high, low, sums)
    return pl.pallas_call(
        functools.partial(bottom_kernel, half),
        out_shape=jax.ShapeDtypeStruct(sources.shape, f32),
        in_specs=[VMEM] * 5,
        out_specs=HBM,
        scratch_shapes=[
            pltpu.VMEM((block_rows, panels, 2, part, size), f32),
            pltpu.VMEM(*piece_shape(second_rows)),
            pltpu.VMEM(*piece_shape(second_rows)),
            pltpu.SemaphoreType.DMA((block_rows,)),
        ],
        compiler_params=params(12),
        cost_estimate=cost(macs, blocks.size),
        name="bottom",
    )(second_swapped, second_diagonal, high, low, sums)


def solution(mesh):
    placed = (
        P("shot", None, "depth", "lat"),
        P(("shot", "depth"), "lat", None, None, None, None),
        P("depth", "lat", None),
        P("lat"),
        P(None, "lat"),
    )
    return jax.shard_map(
        per_device,
        mesh=mesh,
        in_specs=placed,
        out_specs=P("shot", None, "depth", "lat"),
        check_vma=False,
    )
```

```python
import functools

import jax
import jax.numpy as jnp
from jax import lax
from jax.experimental import pallas as pl
from jax.experimental.pallas import tpu as pltpu
from jax.sharding import PartitionSpec as P


VMEM = pl.BlockSpec(memory_space=pltpu.VMEM)
SMEM = pl.BlockSpec(memory_space=pltpu.SMEM)
HBM = pl.BlockSpec(memory_space=pltpu.HBM)
MIB = 1 << 20


def reflected(field_re, field_im, coef_re, coef_im):
    return (
        field_re + coef_re * field_re - coef_im * field_im,
        field_im + coef_re * field_im + coef_im * field_re,
    )


def entered(sources, coef):
    panels = [
        reflected(sources[k, 0], sources[k, 1], coef[0:1, :], coef[1:2, :])
        for k in range(sources.shape[0])
    ]
    return jnp.concatenate([re for re, _ in panels] + [im for _, im in panels], axis=0)


def enter_kernel(
    first, sources, refl_level, refl_coef, total, next_coef, held, level_held, coef_held, coef, sems
):
    lanes = pl.ds(first, total.shape[1])
    copies = [
        pltpu.make_async_copy(a, b, sems.at[i])
        for i, (a, b) in enumerate(
            (
                (sources.at[:, :, :, lanes], held),
                (refl_level.at[:, lanes], level_held),
                (refl_coef.at[:, lanes], coef_held),
            )
        )
    ]
    for copy in copies:
        copy.start()
    for copy in copies:
        copy.wait()
    coef[...] = jnp.where(level_held[...] == 0, coef_held[...], 0.0)
    next_coef[...] = jnp.where(level_held[...] == 1, coef_held[...], 0.0)
    total[...] = entered(held, coef)


def head_and_tail(value):
    head = value.astype(jnp.bfloat16)
    return head, (value - head.astype(jnp.float32)).astype(jnp.bfloat16)


def pieces(value):
    return jnp.concatenate(head_and_tail(value), axis=0)


def product(left, high, low):
    rows = left.shape[0] // 2
    high = high.reshape(high.shape[0] * high.shape[1], high.shape[2])
    low = low.reshape(high.shape)
    both = jnp.dot(left, high, preferred_element_type=jnp.float32)
    cross = jnp.dot(left[:rows], low, preferred_element_type=jnp.float32)
    return both[:rows] + both[rows:] + cross


def prepare_kernel(level, own_cols, other_cols, own, received, *refs):
    fields, (high, low, sums, held, left, sems) = refs[:-6], refs[-6:]
    block_rows, per_row, _, size, _ = held.shape
    here = lax.axis_index("depth") == level
    first_row = lax.axis_index("lat") * block_rows
    for b in range(block_rows):

        @pl.when(here)
        def _():
            pltpu.make_async_copy(own.at[0, b], held.at[b], sems.at[b]).start()

        @pl.when(jnp.logical_not(here))
        def _():
            pltpu.make_async_copy(received.at[0, b], held.at[b], sems.at[b]).start()

    span = 2 * block_rows + 1
    zeros = jnp.zeros((size, 2 * size), jnp.bfloat16)

    def clear(b, o):
        high[b, o] = zeros
        low[b, o] = zeros

    rows_at, rows_repeated = [], []
    for b in range(block_rows):
        first = first_row + b - block_rows
        at = [
            jnp.where(here, own_cols[0, b, j], other_cols[0, b, j]) - first
            for j in range(per_row)
        ]
        bits = [jnp.left_shift(1, a) for a in at]
        present = functools.reduce(jnp.bitwise_or, bits)
        repeated = sum(bits) != present
        rows_at.append(at)
        rows_repeated.append(repeated)
        absent = (1 << span) - 1 - present
        if span - per_row == 2:
            clear(b, sum(jnp.where(absent % (2 << o) == 0, 1, 0) for o in range(span - 1)))
            clear(b, sum(jnp.where(absent >= (2 << o), 1, 0) for o in range(span - 1)))
        else:
            repeated = True

        @pl.when(repeated)
        def _():
            def clear_one(o, carry):
                @pl.when(jnp.bitwise_and(jnp.right_shift(absent, o), 1) == 1)
                def _():
                    clear(b, o)

                return carry

            lax.fori_loop(0, span, clear_one, 0)

    at_lane = 0
    for field in fields:
        left[:, at_lane : at_lane + field.shape[1]] = pieces(field[...])
        at_lane += field.shape[1]
    for b in range(block_rows):
        at = rows_at[b]
        pltpu.make_async_copy(own.at[0, b], held.at[b], sems.at[b]).wait()

        @pl.when(rows_repeated[b])
        def _():
            for j in reversed(range(1, per_row)):
                target = jnp.int32(per_row)
                for i in range(j):
                    target = jnp.where(at[i] == at[j], i, target)

                @pl.when(target < per_row)
                def _():
                    held[b, target] = held[b, target] + held[b, j]

        def split(n, carry):
            rows = pl.ds(pl.multiple_of(n * 16, 16), 16)
            for j in reversed(range(per_row)):
                head, tail = head_and_tail(
                    jnp.concatenate([held[b, j, 0, rows], held[b, j, 1, rows]], axis=1)
                )
                high[b, at[j], rows] = head
                low[b, at[j], rows] = tail
            return carry

        lax.fori_loop(0, size // 16, split, 0)
    for b in range(block_rows):
        band = slice(block_rows - b, 2 * block_rows - b)
        sums[b] = product(left[...], high[b, band], low[b, band])


def side_product(b, first, piece, is_before, high, low):
    block_rows, _, size, _ = high.shape
    last = first + piece.shape[1] // size
    if is_before:
        low_col, high_col, shift = max(b, first), last, -b
    else:
        low_col, high_col, shift = first, min(b + 1, last), 2 * block_rows - b
    if low_col >= high_col:
        return 0.0
    lanes = slice((low_col - first) * size, (high_col - first) * size)
    band = slice(low_col + shift, high_col + shift)
    return product(piece[:, lanes], high[b, band], low[b, band])


def by_side(run):
    even = lax.axis_index("lat") % 2 == 0
    pl.when(even)(functools.partial(run, False))
    pl.when(jnp.logical_not(even))(functools.partial(run, True))


def early_kernel(halo, high, low, sums, out, left):
    left[...] = pieces(halo[...])

    def run(swapped_before):
        for b in range(high.shape[0]):
            out[b] = sums[b] + side_product(b, 0, left, swapped_before, high, low)

    by_side(run)


def late_products(rows, swapped, diagonal, high, low, sums, finish):
    first = (diagonal.shape[1] - swapped.shape[1]) // high.shape[2]

    def run(swapped_before):
        for i, b in enumerate(rows):
            finish(
                i,
                b,
                sums[b]
                + side_product(b, 0, diagonal, not swapped_before, high, low)
                + side_product(b, first, swapped, swapped_before, high, low),
            )

    by_side(run)


def take_late(swapped, relayed, diagonal, swapped_left, diagonal_left):
    points = relayed.shape[1]
    swapped_left[...] = pieces(swapped[...])
    diagonal_left[:, :points] = pieces(relayed[...])
    diagonal_left[:, points:] = pieces(diagonal[...])


def leaving(value):
    channels, size = value.shape[0] // 2, value.shape[1] // 2
    return (
        value[:channels, :size] - value[channels:, size:],
        value[:channels, size:] + value[channels:, :size],
    )


def level_rows(rows, swapped, diagonal, high, low, sums, next_coef, out):
    def finish(i, b, value):
        re, im = leaving(value)
        channels, size = re.shape
        lanes = slice(i * size, (i + 1) * size)
        re, im = reflected(re, im, next_coef[0:1, lanes], next_coef[1:2, lanes])
        out[:channels, lanes] = re
        out[channels:, lanes] = im

    late_products(rows, swapped, diagonal, high, low, sums, finish)


def first_rows_kernel(
    rows, swapped, relayed, diagonal, high, low, sums, next_coef, out, swapped_left, diagonal_left
):
    take_late(swapped, relayed, diagonal, swapped_left, diagonal_left)
    level_rows(rows, swapped_left, diagonal_left, high, low, sums, next_coef, out)


def bottom_kernel(
    swapped,
    relayed,
    diagonal,
    high,
    low,
    sums,
    out,
    held,
    swapped_left,
    diagonal_left,
    sems,
):
    panels, _, part, _ = out.shape
    block_rows, _, size, _ = high.shape
    take_late(swapped, relayed, diagonal, swapped_left, diagonal_left)

    def copy_out(b):
        lanes = pl.ds(b * size, size)
        return pltpu.make_async_copy(
            held.at[b], out.at[:, :, :, lanes], sems.at[b]
        )

    def finish(i, b, value):
        re, im = leaving(value)
        held[b, :, 0] = re.reshape(panels, part, size)
        held[b, :, 1] = im.reshape(panels, part, size)
        copy_out(b).start()

    late_products(range(block_rows), swapped_left, diagonal_left, high, low, sums, finish)
    for b in range(block_rows):
        copy_out(b).wait()


def in_hbm(value):
    return pltpu.with_memory_space_constraint(value, pltpu.HBM)


def params(mib):
    return pltpu.CompilerParams(vmem_limit_bytes=mib * MIB)


def cost(flops, transferred):
    return pl.CostEstimate(flops=flops, bytes_accessed=transferred, transcendentals=0)


def per_device(sources, blocks, block_cols, refl_level, refl_coef):
    lat_count = lax.axis_size("lat")
    panels, _, part, points = sources.shape
    _, block_rows, _, _, size, _ = blocks.shape
    channels = panels * part
    f32, bf16 = jnp.float32, jnp.bfloat16
    axes = ("depth", "lat")
    over_depth = [(0, 1), (1, 0)]
    even = range(0, lat_count - 1, 2)
    uneven = range(1, lat_count - 1, 2)
    alone_even = range(lat_count - lat_count % 2, lat_count)
    alone_uneven = [0] + list(range(lat_count - 1 + lat_count % 2, lat_count))

    def over_lat(firsts, alone):
        pairs = [(d * lat_count + i, d * lat_count + i + 1) for d in range(2) for i in firsts]
        pairs += [(i, lat_count + i) for i in alone]
        return pairs + [(j, i) for i, j in pairs]

    across = over_lat(uneven, alone_uneven)
    beside = over_lat(even, alone_even)
    onward = [(i, i + 2) for i in range(0, lat_count - 2, 2)]
    onward += [(i + 2, i) for i in range(1, lat_count - 2, 2)]
    top = lat_count - 1
    onward += [(top, top - 1) if top % 2 == 0 else (top - 1, top), (1, 0)]
    onward = [(d * lat_count + i, d * lat_count + j) for d in range(2) for i, j in onward]
    half = block_rows // 2
    first_rows, second_rows = range(half), range(half, block_rows)

    def part_shape(rows):
        return jax.ShapeDtypeStruct((2 * channels, len(rows) * size), f32)

    def piece_shape(rows):
        return (4 * channels, len(rows) * size), bf16

    def exchange(first, second):
        first_swapped = lax.ppermute(first, axes, beside)
        second = second()
        second_swapped = lax.ppermute(second, axes, beside)
        second_diagonal = lax.ppermute(second, axes, across)
        relayed = lax.ppermute(first_swapped, axes, onward)
        return second, first_swapped, (second_swapped, relayed, second_diagonal)

    other_blocks = lax.ppermute(blocks, "depth", over_depth)
    other_cols = lax.ppermute(block_cols, "depth", over_depth)
    refl_level = refl_level.reshape(1, points)

    def enter(rows):
        width = len(rows) * size
        return pl.pallas_call(
            functools.partial(enter_kernel, rows[0] * size),
            out_shape=[part_shape(rows), jax.ShapeDtypeStruct((2, width), f32)],
            in_specs=[HBM] * 3,
            out_specs=[VMEM] * 2,
            scratch_shapes=[
                pltpu.VMEM((panels, 2, part, width), f32),
                pltpu.VMEM((1, width), jnp.int32),
                pltpu.VMEM((2, width), f32),
                pltpu.VMEM((2, width), f32),
                pltpu.SemaphoreType.DMA((3,)),
            ],
            compiler_params=params(4),
            name="enter",
        )(in_hbm(sources), in_hbm(refl_level), in_hbm(refl_coef))

    coefs = []

    def enter_second():
        part_total, coef = enter(second_rows)
        coefs.append(coef)
        return part_total

    first_total, coef = enter(first_rows)
    coefs.append(coef)
    second_total, early, late = exchange(first_total, enter_second)

    band_shape = jax.ShapeDtypeStruct((block_rows, 2 * block_rows + 1, size, 2 * size), bf16)
    sums_shape = jax.ShapeDtypeStruct((block_rows, 2 * channels, 2 * size), f32)
    macs = 6 * channels * points * 2 * size

    def prepare(level, *fields):
        return pl.pallas_call(
            functools.partial(prepare_kernel, level),
            out_shape=[band_shape, band_shape, sums_shape],
            in_specs=[SMEM, SMEM, HBM, HBM] + [VMEM] * len(fields),
            out_specs=[VMEM] * 3,
            scratch_shapes=[
                pltpu.VMEM(blocks.shape[1:], f32),
                pltpu.VMEM((4 * channels, points), bf16),
                pltpu.SemaphoreType.DMA((block_rows,)),
            ],
            compiler_params=params(16),
            cost_estimate=cost(4 * macs, 8 * blocks.size),
            name="prepare",
        )(in_hbm(block_cols), other_cols, in_hbm(blocks), other_blocks, *fields)

    def early_products(level, halo, *fields):
        high, low, sums = prepare(level, *fields)
        sums = pl.pallas_call(
            early_kernel,
            out_shape=sums_shape,
            in_specs=[VMEM] * 4,
            out_specs=VMEM,
            scratch_shapes=[pltpu.VMEM(*piece_shape(first_rows))],
            compiler_params=params(12),
            cost_estimate=cost(macs, blocks.size),
            name="early",
        )(halo, high, low, sums)
        return high, low, sums

    every_row = range(block_rows)
    high, low, sums = early_products(0, early, first_total, second_total)
    first_part, swapped_left, diagonal_left = pl.pallas_call(
        functools.partial(first_rows_kernel, first_rows),
        out_shape=[
            part_shape(first_rows),
            jax.ShapeDtypeStruct(*piece_shape(second_rows)),
            jax.ShapeDtypeStruct(*piece_shape(every_row)),
        ],
        in_specs=[VMEM] * 7,
        out_specs=[VMEM] * 3,
        compiler_params=params(12),
        cost_estimate=cost(macs, blocks.size),
        name="first_rows",
    )(*late, high, low, sums, coefs[0])

    def level_second():
        return pl.pallas_call(
            functools.partial(level_rows, second_rows),
            out_shape=part_shape(second_rows),
            in_specs=[VMEM] * 6,
            out_specs=VMEM,
            compiler_params=params(12),
            cost_estimate=cost(macs, blocks.size),
            name="second_rows",
        )(swapped_left, diagonal_left, high, low, sums, coefs[1])

    second_part, early, late = exchange(first_part, level_second)
    last_high, last_low, last_sums = early_products(1, early, first_part, second_part)
    return pl.pallas_call(
        bottom_kernel,
        out_shape=jax.ShapeDtypeStruct(sources.shape, f32),
        in_specs=[VMEM] * 6,
        out_specs=HBM,
        scratch_shapes=[
            pltpu.VMEM((block_rows, panels, 2, part, size), f32),
            pltpu.VMEM(*piece_shape(second_rows)),
            pltpu.VMEM(*piece_shape(every_row)),
            pltpu.SemaphoreType.DMA((block_rows,)),
        ],
        compiler_params=params(12),
        cost_estimate=cost(macs, blocks.size),
        name="bottom",
    )(*late, last_high, last_low, last_sums)


def solution(mesh):
    placed = (
        P("shot", None, "depth", "lat"),
        P(("shot", "depth"), "lat", None, None, None, None),
        P("depth", "lat", None),
        P("lat"),
        P(None, "lat"),
    )
    return jax.shard_map(
        per_device,
        mesh=mesh,
        in_specs=placed,
        out_specs=P("shot", None, "depth", "lat"),
        check_vma=False,
    )
```

```python
import functools

import jax
import jax.numpy as jnp
from jax import lax
from jax.experimental import pallas as pl
from jax.experimental.pallas import tpu as pltpu
from jax.sharding import PartitionSpec as P


VMEM = pl.BlockSpec(memory_space=pltpu.VMEM)
SMEM = pl.BlockSpec(memory_space=pltpu.SMEM)
HBM = pl.BlockSpec(memory_space=pltpu.HBM)
MIB = 1 << 20


def reflected(field_re, field_im, coef_re, coef_im):
    return (
        field_re + coef_re * field_re - coef_im * field_im,
        field_im + coef_re * field_im + coef_im * field_re,
    )


def entered(sources, coef):
    panels = [
        reflected(sources[k, 0], sources[k, 1], coef[0:1, :], coef[1:2, :])
        for k in range(sources.shape[0])
    ]
    return jnp.concatenate([re for re, _ in panels] + [im for _, im in panels], axis=0)


def enter_kernel(
    first, sources, refl_level, refl_coef, total, next_coef, held, level_held, coef_held, coef, sems
):
    lanes = pl.ds(first, total.shape[1])
    copies = [
        pltpu.make_async_copy(a, b, sems.at[i])
        for i, (a, b) in enumerate(
            (
                (sources.at[:, :, :, lanes], held),
                (refl_level.at[:, lanes], level_held),
                (refl_coef.at[:, lanes], coef_held),
            )
        )
    ]
    for copy in copies:
        copy.start()
    for copy in copies:
        copy.wait()
    coef[...] = jnp.where(level_held[...] == 0, coef_held[...], 0.0)
    next_coef[...] = jnp.where(level_held[...] == 1, coef_held[...], 0.0)
    total[...] = entered(held, coef)


def head_and_tail(value):
    head = value.astype(jnp.bfloat16)
    return head, (value - head.astype(jnp.float32)).astype(jnp.bfloat16)


def pieces(value):
    return jnp.concatenate(head_and_tail(value), axis=0)


def product(left, high, low):
    rows = left.shape[0] // 2
    high = high.reshape(high.shape[0] * high.shape[1], high.shape[2])
    low = low.reshape(high.shape)
    both = jnp.dot(left, high, preferred_element_type=jnp.float32)
    cross = jnp.dot(left[:rows], low, preferred_element_type=jnp.float32)
    return both[:rows] + both[rows:] + cross


def prepare_kernel(level, rows, own_cols, other_cols, own, received, *refs):
    fields, (high, low, sums, held, left, sems) = refs[:-6], refs[-6:]
    per_row, size = held.shape[1], held.shape[3]
    block_rows = own.shape[1]
    here = lax.axis_index("depth") == level
    first_row = lax.axis_index("lat") * block_rows
    for i, b in enumerate(rows):

        @pl.when(here)
        def _():
            pltpu.make_async_copy(own.at[0, b], held.at[i], sems.at[i]).start()

        @pl.when(jnp.logical_not(here))
        def _():
            pltpu.make_async_copy(received.at[0, b], held.at[i], sems.at[i]).start()

    span = 2 * block_rows + 1
    zeros = jnp.zeros((size, 2 * size), jnp.bfloat16)

    def clear(i, o):
        high[i, o] = zeros
        low[i, o] = zeros

    rows_at, rows_repeated = [], []
    for i, b in enumerate(rows):
        first = first_row + b - block_rows
        at = [
            jnp.where(here, own_cols[0, b, j], other_cols[0, b, j]) - first
            for j in range(per_row)
        ]
        bits = [jnp.left_shift(1, a) for a in at]
        present = functools.reduce(jnp.bitwise_or, bits)
        repeated = sum(bits) != present
        rows_at.append(at)
        rows_repeated.append(repeated)
        absent = (1 << span) - 1 - present
        if span - per_row == 2:
            clear(i, sum(jnp.where(absent % (2 << o) == 0, 1, 0) for o in range(span - 1)))
            clear(i, sum(jnp.where(absent >= (2 << o), 1, 0) for o in range(span - 1)))
        else:
            repeated = True

        @pl.when(repeated)
        def _():
            def clear_one(o, carry):
                @pl.when(jnp.bitwise_and(jnp.right_shift(absent, o), 1) == 1)
                def _():
                    clear(i, o)

                return carry

            lax.fori_loop(0, span, clear_one, 0)

    at_lane = 0
    for field in fields:
        left[:, at_lane : at_lane + field.shape[1]] = pieces(field[...])
        at_lane += field.shape[1]
    for i, b in enumerate(rows):
        at = rows_at[i]
        pltpu.make_async_copy(own.at[0, b], held.at[i], sems.at[i]).wait()

        @pl.when(rows_repeated[i])
        def _():
            for j in reversed(range(1, per_row)):
                target = jnp.int32(per_row)
                for k in range(j):
                    target = jnp.where(at[k] == at[j], k, target)

                @pl.when(target < per_row)
                def _():
                    held[i, target] = held[i, target] + held[i, j]

        def split(n, carry):
            part = pl.ds(pl.multiple_of(n * 16, 16), 16)
            for j in reversed(range(per_row)):
                head, tail = head_and_tail(
                    jnp.concatenate([held[i, j, 0, part], held[i, j, 1, part]], axis=1)
                )
                high[i, at[j], part] = head
                low[i, at[j], part] = tail
            return carry

        lax.fori_loop(0, size // 16, split, 0)
    for i, b in enumerate(rows):
        band = slice(block_rows - b, 2 * block_rows - b)
        sums[i] = product(left[...], high[i, band], low[i, band])


class Bands:
    def __init__(self, refs):
        count = len(refs) // 2
        self.high, self.low = refs[:count], refs[count:]
        self.rows = [(n, i) for n, ref in enumerate(self.high) for i in range(ref.shape[0])]
        self.size = self.high[0].shape[2]

    def product(self, b, left, band):
        n, i = self.rows[b]
        return product(left, self.high[n][i, band], self.low[n][i, band])


def side_product(b, first, piece, is_before, bands):
    block_rows, size = len(bands.rows), bands.size
    last = first + piece.shape[1] // size
    if is_before:
        low_col, high_col, shift = max(b, first), last, -b
    else:
        low_col, high_col, shift = first, min(b + 1, last), 2 * block_rows - b
    if low_col >= high_col:
        return 0.0
    lanes = slice((low_col - first) * size, (high_col - first) * size)
    band = slice(low_col + shift, high_col + shift)
    return bands.product(b, piece[:, lanes], band)


def by_side(run):
    even = lax.axis_index("lat") % 2 == 0
    pl.when(even)(functools.partial(run, False))
    pl.when(jnp.logical_not(even))(functools.partial(run, True))


def early_kernel(halo, *refs):
    bands, parts, (out, left) = Bands(refs[:4]), refs[4:-2], refs[-2:]
    left[...] = pieces(halo[...])

    def run(swapped_before):
        for b, (n, i) in enumerate(bands.rows):
            out[b] = parts[n][i] + side_product(b, 0, left, swapped_before, bands)

    by_side(run)


def late_products(rows, swapped, diagonal, bands, sums, finish):
    first = (diagonal.shape[1] - swapped.shape[1]) // bands.size

    def run(swapped_before):
        for i, b in enumerate(rows):
            finish(
                i,
                b,
                sums[b]
                + side_product(b, 0, diagonal, not swapped_before, bands)
                + side_product(b, first, swapped, swapped_before, bands),
            )

    by_side(run)


def take_late(swapped, relayed, diagonal, swapped_left, diagonal_left):
    points = relayed.shape[1]
    swapped_left[...] = pieces(swapped[...])
    diagonal_left[:, :points] = pieces(relayed[...])
    diagonal_left[:, points:] = pieces(diagonal[...])


def leaving(value):
    channels, size = value.shape[0] // 2, value.shape[1] // 2
    return (
        value[:channels, :size] - value[channels:, size:],
        value[:channels, size:] + value[channels:, :size],
    )


def level_rows(rows, swapped, diagonal, *refs):
    bands, (sums, next_coef, out) = Bands(refs[:4]), refs[4:]

    def finish(i, b, value):
        re, im = leaving(value)
        channels, size = re.shape
        lanes = slice(i * size, (i + 1) * size)
        re, im = reflected(re, im, next_coef[0:1, lanes], next_coef[1:2, lanes])
        out[:channels, lanes] = re
        out[channels:, lanes] = im

    late_products(rows, swapped, diagonal, bands, sums, finish)


def first_rows_kernel(rows, swapped, relayed, diagonal, *refs):
    operands, (swapped_left, diagonal_left) = refs[:-2], refs[-2:]
    take_late(swapped, relayed, diagonal, swapped_left, diagonal_left)
    level_rows(rows, swapped_left, diagonal_left, *operands)


def bottom_kernel(swapped, relayed, diagonal, *refs):
    bands, (sums, out, held, swapped_left, diagonal_left, sems) = Bands(refs[:4]), refs[4:]
    panels, _, part, _ = out.shape
    block_rows, size = len(bands.rows), bands.size
    take_late(swapped, relayed, diagonal, swapped_left, diagonal_left)

    def copy_out(b):
        lanes = pl.ds(b * size, size)
        return pltpu.make_async_copy(
            held.at[b], out.at[:, :, :, lanes], sems.at[b]
        )

    def finish(i, b, value):
        re, im = leaving(value)
        held[b, :, 0] = re.reshape(panels, part, size)
        held[b, :, 1] = im.reshape(panels, part, size)
        copy_out(b).start()

    late_products(range(block_rows), swapped_left, diagonal_left, bands, sums, finish)
    for b in range(block_rows):
        copy_out(b).wait()


def in_hbm(value):
    return pltpu.with_memory_space_constraint(value, pltpu.HBM)


def params(mib):
    return pltpu.CompilerParams(vmem_limit_bytes=mib * MIB)


def cost(flops, transferred):
    return pl.CostEstimate(flops=flops, bytes_accessed=transferred, transcendentals=0)


def per_device(sources, blocks, block_cols, refl_level, refl_coef):
    lat_count = lax.axis_size("lat")
    panels, _, part, points = sources.shape
    _, block_rows, _, _, size, _ = blocks.shape
    channels = panels * part
    f32, bf16 = jnp.float32, jnp.bfloat16
    axes = ("depth", "lat")
    over_depth = [(0, 1), (1, 0)]
    even = range(0, lat_count - 1, 2)
    uneven = range(1, lat_count - 1, 2)
    alone_even = range(lat_count - lat_count % 2, lat_count)
    alone_uneven = [0] + list(range(lat_count - 1 + lat_count % 2, lat_count))

    def over_lat(firsts, alone):
        pairs = [(d * lat_count + i, d * lat_count + i + 1) for d in range(2) for i in firsts]
        pairs += [(i, lat_count + i) for i in alone]
        return pairs + [(j, i) for i, j in pairs]

    across = over_lat(uneven, alone_uneven)
    beside = over_lat(even, alone_even)
    onward = [(i, i + 2) for i in range(0, lat_count - 2, 2)]
    onward += [(i + 2, i) for i in range(1, lat_count - 2, 2)]
    top = lat_count - 1
    onward += [(top, top - 1) if top % 2 == 0 else (top - 1, top), (1, 0)]
    onward = [(d * lat_count + i, d * lat_count + j) for d in range(2) for i, j in onward]
    half = block_rows // 2
    first_rows, second_rows = range(half), range(half, block_rows)

    def part_shape(rows):
        return jax.ShapeDtypeStruct((2 * channels, len(rows) * size), f32)

    def piece_shape(rows):
        return (4 * channels, len(rows) * size), bf16

    def exchange(first, second):
        first_swapped = lax.ppermute(first, axes, beside)
        second = second()
        second_swapped = lax.ppermute(second, axes, beside)
        second_diagonal = lax.ppermute(second, axes, across)
        relayed = lax.ppermute(first_swapped, axes, onward)
        return second, first_swapped, (second_swapped, relayed, second_diagonal)

    other_blocks = lax.ppermute(blocks, "depth", over_depth)
    other_cols = lax.ppermute(block_cols, "depth", over_depth)
    refl_level = refl_level.reshape(1, points)

    def enter(rows):
        width = len(rows) * size
        return pl.pallas_call(
            functools.partial(enter_kernel, rows[0] * size),
            out_shape=[part_shape(rows), jax.ShapeDtypeStruct((2, width), f32)],
            in_specs=[HBM] * 3,
            out_specs=[VMEM] * 2,
            scratch_shapes=[
                pltpu.VMEM((panels, 2, part, width), f32),
                pltpu.VMEM((1, width), jnp.int32),
                pltpu.VMEM((2, width), f32),
                pltpu.VMEM((2, width), f32),
                pltpu.SemaphoreType.DMA((3,)),
            ],
            compiler_params=params(4),
            name="enter",
        )(in_hbm(sources), in_hbm(refl_level), in_hbm(refl_coef))

    coefs = []

    def enter_second():
        part_total, coef = enter(second_rows)
        coefs.append(coef)
        return part_total

    first_total, coef = enter(first_rows)
    coefs.append(coef)
    second_total, early, late = exchange(first_total, enter_second)

    sums_shape = jax.ShapeDtypeStruct((block_rows, 2 * channels, 2 * size), f32)
    macs = 6 * channels * points * 2 * size

    def prepare(level, rows, *fields):
        band = jax.ShapeDtypeStruct((len(rows), 2 * block_rows + 1, size, 2 * size), bf16)
        sums = jax.ShapeDtypeStruct((len(rows), 2 * channels, 2 * size), f32)
        return pl.pallas_call(
            functools.partial(prepare_kernel, level, rows),
            out_shape=[band, band, sums],
            in_specs=[SMEM, SMEM, HBM, HBM] + [VMEM] * len(fields),
            out_specs=[VMEM] * 3,
            scratch_shapes=[
                pltpu.VMEM((len(rows),) + blocks.shape[2:], f32),
                pltpu.VMEM((4 * channels, points), bf16),
                pltpu.SemaphoreType.DMA((len(rows),)),
            ],
            compiler_params=params(16),
            cost_estimate=cost(2 * macs, 4 * blocks.size),
            name="prepare",
        )(in_hbm(block_cols), other_cols, in_hbm(blocks), other_blocks, *fields)

    def early_products(level, halo, *fields):
        first = prepare(level, first_rows, *fields)
        second = prepare(level, second_rows, *fields)
        bands = (first[0], second[0], first[1], second[1])
        sums = pl.pallas_call(
            early_kernel,
            out_shape=sums_shape,
            in_specs=[VMEM] * 7,
            out_specs=VMEM,
            scratch_shapes=[pltpu.VMEM(*piece_shape(first_rows))],
            compiler_params=params(12),
            cost_estimate=cost(macs, blocks.size),
            name="early",
        )(halo, *bands, first[2], second[2])
        return *bands, sums

    every_row = range(block_rows)
    bands = early_products(0, early, first_total, second_total)
    first_part, swapped_left, diagonal_left = pl.pallas_call(
        functools.partial(first_rows_kernel, first_rows),
        out_shape=[
            part_shape(first_rows),
            jax.ShapeDtypeStruct(*piece_shape(second_rows)),
            jax.ShapeDtypeStruct(*piece_shape(every_row)),
        ],
        in_specs=[VMEM] * 9,
        out_specs=[VMEM] * 3,
        compiler_params=params(12),
        cost_estimate=cost(macs, blocks.size),
        name="first_rows",
    )(*late, *bands, coefs[0])

    def level_second():
        return pl.pallas_call(
            functools.partial(level_rows, second_rows),
            out_shape=part_shape(second_rows),
            in_specs=[VMEM] * 8,
            out_specs=VMEM,
            compiler_params=params(12),
            cost_estimate=cost(macs, blocks.size),
            name="second_rows",
        )(swapped_left, diagonal_left, *bands, coefs[1])

    second_part, early, late = exchange(first_part, level_second)
    last_bands = early_products(1, early, first_part, second_part)
    return pl.pallas_call(
        bottom_kernel,
        out_shape=jax.ShapeDtypeStruct(sources.shape, f32),
        in_specs=[VMEM] * 8,
        out_specs=HBM,
        scratch_shapes=[
            pltpu.VMEM((block_rows, panels, 2, part, size), f32),
            pltpu.VMEM(*piece_shape(second_rows)),
            pltpu.VMEM(*piece_shape(every_row)),
            pltpu.SemaphoreType.DMA((block_rows,)),
        ],
        compiler_params=params(12),
        cost_estimate=cost(macs, blocks.size),
        name="bottom",
    )(*late, *last_bands)


def solution(mesh):
    placed = (
        P("shot", None, "depth", "lat"),
        P(("shot", "depth"), "lat", None, None, None, None),
        P("depth", "lat", None),
        P("lat"),
        P(None, "lat"),
    )
    return jax.shard_map(
        per_device,
        mesh=mesh,
        in_specs=placed,
        out_specs=P("shot", None, "depth", "lat"),
        check_vma=False,
    )
```

```python
import functools

import jax
import jax.numpy as jnp
from jax import lax
from jax.experimental import pallas as pl
from jax.experimental.pallas import tpu as pltpu
from jax.sharding import PartitionSpec as P


VMEM = pl.BlockSpec(memory_space=pltpu.VMEM)
SMEM = pl.BlockSpec(memory_space=pltpu.SMEM)
HBM = pl.BlockSpec(memory_space=pltpu.HBM)
MIB = 1 << 20


def reflected(field_re, field_im, coef_re, coef_im):
    return (
        field_re + coef_re * field_re - coef_im * field_im,
        field_im + coef_re * field_im + coef_im * field_re,
    )


def entered(sources, coef):
    panels = [
        reflected(sources[k, 0], sources[k, 1], coef[0:1, :], coef[1:2, :])
        for k in range(sources.shape[0])
    ]
    return jnp.concatenate([re for re, _ in panels] + [im for _, im in panels], axis=0)


def enter_kernel(
    first, sources, refl_level, refl_coef, total, next_coef, held, level_held, coef_held, coef, sems
):
    lanes = pl.ds(first, total.shape[1])
    copies = [
        pltpu.make_async_copy(a, b, sems.at[i])
        for i, (a, b) in enumerate(
            (
                (sources.at[:, :, :, lanes], held),
                (refl_level.at[:, lanes], level_held),
                (refl_coef.at[:, lanes], coef_held),
            )
        )
    ]
    for copy in copies:
        copy.start()
    for copy in copies:
        copy.wait()
    coef[...] = jnp.where(level_held[...] == 0, coef_held[...], 0.0)
    next_coef[...] = jnp.where(level_held[...] == 1, coef_held[...], 0.0)
    total[...] = entered(held, coef)


def head_and_tail(value):
    head = value.astype(jnp.bfloat16)
    return head, (value - head.astype(jnp.float32)).astype(jnp.bfloat16)


def pieces(value):
    return jnp.concatenate(head_and_tail(value), axis=0)


def product(left, high, low):
    rows = left.shape[0] // 2
    high = high.reshape(high.shape[0] * high.shape[1], high.shape[2])
    low = low.reshape(high.shape)
    both = jnp.dot(left, high, preferred_element_type=jnp.float32)
    cross = jnp.dot(left[:rows], low, preferred_element_type=jnp.float32)
    return both[:rows] + both[rows:] + cross


def prepare_kernel(level, rows, own_cols, other_cols, own, received, *refs):
    fields, (high, low, sums, held, left, sems) = refs[:-6], refs[-6:]
    per_row, size = held.shape[1], held.shape[3]
    block_rows = own.shape[1]
    here = lax.axis_index("depth") == level
    first_row = lax.axis_index("lat") * block_rows
    for i, b in enumerate(rows):

        @pl.when(here)
        def _():
            pltpu.make_async_copy(own.at[0, b], held.at[i], sems.at[i]).start()

        @pl.when(jnp.logical_not(here))
        def _():
            pltpu.make_async_copy(received.at[0, b], held.at[i], sems.at[i]).start()

    span = 2 * block_rows + 1
    zeros = jnp.zeros((size, 2 * size), jnp.bfloat16)

    def clear(i, o):
        high[i, o] = zeros
        low[i, o] = zeros

    rows_at, rows_repeated = [], []
    for i, b in enumerate(rows):
        first = first_row + b - block_rows
        at = [
            jnp.where(here, own_cols[0, b, j], other_cols[0, b, j]) - first
            for j in range(per_row)
        ]
        bits = [jnp.left_shift(1, a) for a in at]
        present = functools.reduce(jnp.bitwise_or, bits)
        repeated = sum(bits) != present
        rows_at.append(at)
        rows_repeated.append(repeated)
        absent = (1 << span) - 1 - present
        if span - per_row == 2:
            clear(i, sum(jnp.where(absent % (2 << o) == 0, 1, 0) for o in range(span - 1)))
            clear(i, sum(jnp.where(absent >= (2 << o), 1, 0) for o in range(span - 1)))
        else:
            repeated = True

        @pl.when(repeated)
        def _():
            def clear_one(o, carry):
                @pl.when(jnp.bitwise_and(jnp.right_shift(absent, o), 1) == 1)
                def _():
                    clear(i, o)

                return carry

            lax.fori_loop(0, span, clear_one, 0)

    at_lane = 0
    for field in fields:
        left[:, at_lane : at_lane + field.shape[1]] = pieces(field[...])
        at_lane += field.shape[1]
    for i, b in enumerate(rows):
        at = rows_at[i]
        pltpu.make_async_copy(own.at[0, b], held.at[i], sems.at[i]).wait()

        @pl.when(rows_repeated[i])
        def _():
            for j in reversed(range(1, per_row)):
                target = jnp.int32(per_row)
                for k in range(j):
                    target = jnp.where(at[k] == at[j], k, target)

                @pl.when(target < per_row)
                def _():
                    held[i, target] = held[i, target] + held[i, j]

        def split(n, carry):
            part = pl.ds(pl.multiple_of(n * 16, 16), 16)
            for j in reversed(range(per_row)):
                head, tail = head_and_tail(
                    jnp.concatenate([held[i, j, 0, part], held[i, j, 1, part]], axis=1)
                )
                high[i, at[j], part] = head
                low[i, at[j], part] = tail
            return carry

        lax.fori_loop(0, size // 16, split, 0)
    for i, b in enumerate(rows):
        band = slice(block_rows - b, 2 * block_rows - b)
        sums[i] = product(left[...], high[i, band], low[i, band])


class Bands:
    def __init__(self, groups, refs):
        self.high, self.low = refs[:groups], refs[groups : 2 * groups]
        self.rows = [(n, i) for n, ref in enumerate(self.high) for i in range(ref.shape[0])]
        self.size = self.high[0].shape[2]

    def product(self, b, left, band):
        n, i = self.rows[b]
        return product(left, self.high[n][i, band], self.low[n][i, band])


def side_product(b, first, piece, is_before, bands):
    block_rows, size = len(bands.rows), bands.size
    last = first + piece.shape[1] // size
    if is_before:
        low_col, high_col, shift = max(b, first), last, -b
    else:
        low_col, high_col, shift = first, min(b + 1, last), 2 * block_rows - b
    if low_col >= high_col:
        return 0.0
    lanes = slice((low_col - first) * size, (high_col - first) * size)
    band = slice(low_col + shift, high_col + shift)
    return bands.product(b, piece[:, lanes], band)


def by_side(run):
    even = lax.axis_index("lat") % 2 == 0
    pl.when(even)(functools.partial(run, False))
    pl.when(jnp.logical_not(even))(functools.partial(run, True))


def early_kernel(groups, halo, *refs):
    bands, parts, (out, left) = Bands(groups, refs), refs[2 * groups : -2], refs[-2:]
    left[...] = pieces(halo[...])

    def run(swapped_before):
        for b, (n, i) in enumerate(bands.rows):
            out[b] = parts[n][i] + side_product(b, 0, left, swapped_before, bands)

    by_side(run)


def late_products(rows, swapped, diagonal, bands, sums, finish):
    first = (diagonal.shape[1] - swapped.shape[1]) // bands.size

    def run(swapped_before):
        for i, b in enumerate(rows):
            finish(
                i,
                b,
                sums[b]
                + side_product(b, 0, diagonal, not swapped_before, bands)
                + side_product(b, first, swapped, swapped_before, bands),
            )

    by_side(run)


def take_late(swapped, relayed, diagonal, swapped_left, diagonal_left):
    points = relayed.shape[1]
    swapped_left[...] = pieces(swapped[...])
    diagonal_left[:, :points] = pieces(relayed[...])
    diagonal_left[:, points:] = pieces(diagonal[...])


def leaving(value):
    channels, size = value.shape[0] // 2, value.shape[1] // 2
    return (
        value[:channels, :size] - value[channels:, size:],
        value[:channels, size:] + value[channels:, :size],
    )


def level_rows(groups, rows, swapped, diagonal, *refs):
    bands, (sums, next_coef, out) = Bands(groups, refs), refs[2 * groups :]

    def finish(i, b, value):
        re, im = leaving(value)
        channels, size = re.shape
        lanes = slice(i * size, (i + 1) * size)
        re, im = reflected(re, im, next_coef[0:1, lanes], next_coef[1:2, lanes])
        out[:channels, lanes] = re
        out[channels:, lanes] = im

    late_products(rows, swapped, diagonal, bands, sums, finish)


def first_rows_kernel(groups, rows, swapped, relayed, diagonal, *refs):
    operands, (swapped_left, diagonal_left) = refs[:-2], refs[-2:]
    take_late(swapped, relayed, diagonal, swapped_left, diagonal_left)
    level_rows(groups, rows, swapped_left, diagonal_left, *operands)


def bottom_kernel(groups, swapped, relayed, diagonal, *refs):
    bands = Bands(groups, refs)
    sums, out, held, swapped_left, diagonal_left, sems = refs[2 * groups :]
    panels, _, part, _ = out.shape
    block_rows, size = len(bands.rows), bands.size
    take_late(swapped, relayed, diagonal, swapped_left, diagonal_left)

    def copy_out(b):
        lanes = pl.ds(b * size, size)
        return pltpu.make_async_copy(
            held.at[b], out.at[:, :, :, lanes], sems.at[b]
        )

    def finish(i, b, value):
        re, im = leaving(value)
        held[b, :, 0] = re.reshape(panels, part, size)
        held[b, :, 1] = im.reshape(panels, part, size)
        copy_out(b).start()

    late_products(range(block_rows), swapped_left, diagonal_left, bands, sums, finish)
    for b in range(block_rows):
        copy_out(b).wait()


def in_hbm(value):
    return pltpu.with_memory_space_constraint(value, pltpu.HBM)


def params(mib):
    return pltpu.CompilerParams(vmem_limit_bytes=mib * MIB)


def cost(flops, transferred):
    return pl.CostEstimate(flops=flops, bytes_accessed=transferred, transcendentals=0)


def per_device(sources, blocks, block_cols, refl_level, refl_coef):
    lat_count = lax.axis_size("lat")
    panels, _, part, points = sources.shape
    _, block_rows, _, _, size, _ = blocks.shape
    channels = panels * part
    f32, bf16 = jnp.float32, jnp.bfloat16
    axes = ("depth", "lat")
    over_depth = [(0, 1), (1, 0)]
    even = range(0, lat_count - 1, 2)
    uneven = range(1, lat_count - 1, 2)
    alone_even = range(lat_count - lat_count % 2, lat_count)
    alone_uneven = [0] + list(range(lat_count - 1 + lat_count % 2, lat_count))

    def over_lat(firsts, alone):
        pairs = [(d * lat_count + i, d * lat_count + i + 1) for d in range(2) for i in firsts]
        pairs += [(i, lat_count + i) for i in alone]
        return pairs + [(j, i) for i, j in pairs]

    across = over_lat(uneven, alone_uneven)
    beside = over_lat(even, alone_even)
    onward = [(i, i + 2) for i in range(0, lat_count - 2, 2)]
    onward += [(i + 2, i) for i in range(1, lat_count - 2, 2)]
    top = lat_count - 1
    onward += [(top, top - 1) if top % 2 == 0 else (top - 1, top), (1, 0)]
    onward = [(d * lat_count + i, d * lat_count + j) for d in range(2) for i, j in onward]
    half = block_rows // 2
    first_rows, second_rows = range(half), range(half, block_rows)

    def part_shape(rows):
        return jax.ShapeDtypeStruct((2 * channels, len(rows) * size), f32)

    def piece_shape(rows):
        return (4 * channels, len(rows) * size), bf16

    def exchange(first, second):
        first_swapped = lax.ppermute(first, axes, beside)
        second = second()
        second_swapped = lax.ppermute(second, axes, beside)
        second_diagonal = lax.ppermute(second, axes, across)
        relayed = lax.ppermute(first_swapped, axes, onward)
        return second, first_swapped, (second_swapped, relayed, second_diagonal)

    other_blocks = lax.ppermute(blocks, "depth", over_depth)
    other_cols = lax.ppermute(block_cols, "depth", over_depth)
    refl_level = refl_level.reshape(1, points)

    def enter(rows):
        width = len(rows) * size
        return pl.pallas_call(
            functools.partial(enter_kernel, rows[0] * size),
            out_shape=[part_shape(rows), jax.ShapeDtypeStruct((2, width), f32)],
            in_specs=[HBM] * 3,
            out_specs=[VMEM] * 2,
            scratch_shapes=[
                pltpu.VMEM((panels, 2, part, width), f32),
                pltpu.VMEM((1, width), jnp.int32),
                pltpu.VMEM((2, width), f32),
                pltpu.VMEM((2, width), f32),
                pltpu.SemaphoreType.DMA((3,)),
            ],
            compiler_params=params(4),
            name="enter",
        )(in_hbm(sources), in_hbm(refl_level), in_hbm(refl_coef))

    coefs = []

    def enter_second():
        part_total, coef = enter(second_rows)
        coefs.append(coef)
        return part_total

    first_total, coef = enter(first_rows)
    coefs.append(coef)
    second_total, early, late = exchange(first_total, enter_second)

    sums_shape = jax.ShapeDtypeStruct((block_rows, 2 * channels, 2 * size), f32)
    macs = 6 * channels * points * 2 * size

    def prepare(level, rows, *fields):
        band = jax.ShapeDtypeStruct((len(rows), 2 * block_rows + 1, size, 2 * size), bf16)
        sums = jax.ShapeDtypeStruct((len(rows), 2 * channels, 2 * size), f32)
        return pl.pallas_call(
            functools.partial(prepare_kernel, level, rows),
            out_shape=[band, band, sums],
            in_specs=[SMEM, SMEM, HBM, HBM] + [VMEM] * len(fields),
            out_specs=[VMEM] * 3,
            scratch_shapes=[
                pltpu.VMEM((len(rows),) + blocks.shape[2:], f32),
                pltpu.VMEM((4 * channels, points), bf16),
                pltpu.SemaphoreType.DMA((len(rows),)),
            ],
            compiler_params=params(16),
            cost_estimate=cost(2 * macs, 4 * blocks.size),
            name="prepare",
        )(in_hbm(block_cols), other_cols, in_hbm(blocks), other_blocks, *fields)

    every_row = range(block_rows)
    row_groups = ((every_row,), (every_row[:1], every_row[1:]))

    def early_products(level, halo, *fields):
        ready = []
        for rows in row_groups[level]:
            ready.append(prepare(level, rows, *fields))
        high, low, parts = zip(*ready)
        sums = pl.pallas_call(
            functools.partial(early_kernel, len(ready)),
            out_shape=sums_shape,
            in_specs=[VMEM] * (1 + 3 * len(ready)),
            out_specs=VMEM,
            scratch_shapes=[pltpu.VMEM(*piece_shape(first_rows))],
            compiler_params=params(12),
            cost_estimate=cost(macs, blocks.size),
            name="early",
        )(halo, *high, *low, *parts)
        return *high, *low, sums

    bands = early_products(0, early, first_total, second_total)
    first_part, swapped_left, diagonal_left = pl.pallas_call(
        functools.partial(first_rows_kernel, len(row_groups[0]), first_rows),
        out_shape=[
            part_shape(first_rows),
            jax.ShapeDtypeStruct(*piece_shape(second_rows)),
            jax.ShapeDtypeStruct(*piece_shape(every_row)),
        ],
        in_specs=[VMEM] * (4 + len(bands)),
        out_specs=[VMEM] * 3,
        compiler_params=params(12),
        cost_estimate=cost(macs, blocks.size),
        name="first_rows",
    )(*late, *bands, coefs[0])

    def level_second():
        return pl.pallas_call(
            functools.partial(level_rows, len(row_groups[0]), second_rows),
            out_shape=part_shape(second_rows),
            in_specs=[VMEM] * (3 + len(bands)),
            out_specs=VMEM,
            compiler_params=params(12),
            cost_estimate=cost(macs, blocks.size),
            name="second_rows",
        )(swapped_left, diagonal_left, *bands, coefs[1])

    second_part, early, late = exchange(first_part, level_second)
    last_bands = early_products(1, early, first_part, second_part)
    return pl.pallas_call(
        functools.partial(bottom_kernel, len(row_groups[1])),
        out_shape=jax.ShapeDtypeStruct(sources.shape, f32),
        in_specs=[VMEM] * (3 + len(last_bands)),
        out_specs=HBM,
        scratch_shapes=[
            pltpu.VMEM((block_rows, panels, 2, part, size), f32),
            pltpu.VMEM(*piece_shape(second_rows)),
            pltpu.VMEM(*piece_shape(every_row)),
            pltpu.SemaphoreType.DMA((block_rows,)),
        ],
        compiler_params=params(12),
        cost_estimate=cost(macs, blocks.size),
        name="bottom",
    )(*late, *last_bands)


def solution(mesh):
    placed = (
        P("shot", None, "depth", "lat"),
        P(("shot", "depth"), "lat", None, None, None, None),
        P("depth", "lat", None),
        P("lat"),
        P(None, "lat"),
    )
    return jax.shard_map(
        per_device,
        mesh=mesh,
        in_specs=placed,
        out_specs=P("shot", None, "depth", "lat"),
        check_vma=False,
    )
```

```python
import functools

import jax
import jax.numpy as jnp
from jax import lax
from jax.experimental import pallas as pl
from jax.experimental.pallas import tpu as pltpu
from jax.sharding import PartitionSpec as P


VMEM = pl.BlockSpec(memory_space=pltpu.VMEM)
SMEM = pl.BlockSpec(memory_space=pltpu.SMEM)
HBM = pl.BlockSpec(memory_space=pltpu.HBM)
MIB = 1 << 20


def reflected(field_re, field_im, coef_re, coef_im):
    return (
        field_re + coef_re * field_re - coef_im * field_im,
        field_im + coef_re * field_im + coef_im * field_re,
    )


def entered(sources, coef):
    panels = [
        reflected(sources[k, 0], sources[k, 1], coef[0:1, :], coef[1:2, :])
        for k in range(sources.shape[0])
    ]
    return jnp.concatenate([re for re, _ in panels] + [im for _, im in panels], axis=0)


def enter_kernel(first, tables, sources, refl_level, refl_coef, *refs):
    tables_in, (total, next_coef), refs = refs[:tables], refs[tables : tables + 2], refs[tables + 2 :]
    tables_out, (held, level_held, coef_held, coef, sems) = refs[:tables], refs[tables:]
    lanes = pl.ds(first, total.shape[1])
    copies = [
        pltpu.make_async_copy(a, b, sems.at[i])
        for i, (a, b) in enumerate(
            (
                (sources.at[:, :, :, lanes], held),
                (refl_level.at[:, lanes], level_held),
                (refl_coef.at[:, lanes], coef_held),
                *zip(tables_in, tables_out),
            )
        )
    ]
    for copy in copies:
        copy.start()
    for copy in copies:
        copy.wait()
    coef[...] = jnp.where(level_held[...] == 0, coef_held[...], 0.0)
    next_coef[...] = jnp.where(level_held[...] == 1, coef_held[...], 0.0)
    total[...] = entered(held, coef)


def head_and_tail(value):
    head = value.astype(jnp.bfloat16)
    return head, (value - head.astype(jnp.float32)).astype(jnp.bfloat16)


def pieces(value):
    return jnp.concatenate(head_and_tail(value), axis=0)


def product(left, high, low):
    rows = left.shape[0] // 2
    high = high.reshape(high.shape[0] * high.shape[1], high.shape[2])
    low = low.reshape(high.shape)
    both = jnp.dot(left, high, preferred_element_type=jnp.float32)
    cross = jnp.dot(left[:rows], low, preferred_element_type=jnp.float32)
    return both[:rows] + both[rows:] + cross


def prepare_kernel(level, rows, own_cols, other_cols, own, received, *refs):
    fields, (high, low, sums, held, left, sems) = refs[:-6], refs[-6:]
    per_row, size = held.shape[1], held.shape[3]
    block_rows = own.shape[1]
    here = lax.axis_index("depth") == level
    first_row = lax.axis_index("lat") * block_rows
    for i, b in enumerate(rows):

        @pl.when(here)
        def _():
            pltpu.make_async_copy(own.at[0, b], held.at[i], sems.at[i]).start()

        @pl.when(jnp.logical_not(here))
        def _():
            pltpu.make_async_copy(received.at[0, b], held.at[i], sems.at[i]).start()

    span = 2 * block_rows + 1
    zeros = jnp.zeros((size, 2 * size), jnp.bfloat16)

    def clear(i, o):
        high[i, o] = zeros
        low[i, o] = zeros

    rows_at, rows_repeated = [], []
    for i, b in enumerate(rows):
        first = first_row + b - block_rows
        at = [
            jnp.where(here, own_cols[0, b, j], other_cols[0, b, j]) - first
            for j in range(per_row)
        ]
        bits = [jnp.left_shift(1, a) for a in at]
        present = functools.reduce(jnp.bitwise_or, bits)
        repeated = sum(bits) != present
        rows_at.append(at)
        rows_repeated.append(repeated)
        absent = (1 << span) - 1 - present
        if span - per_row == 2:
            clear(i, sum(jnp.where(absent % (2 << o) == 0, 1, 0) for o in range(span - 1)))
            clear(i, sum(jnp.where(absent >= (2 << o), 1, 0) for o in range(span - 1)))
        else:
            repeated = True

        @pl.when(repeated)
        def _():
            def clear_one(o, carry):
                @pl.when(jnp.bitwise_and(jnp.right_shift(absent, o), 1) == 1)
                def _():
                    clear(i, o)

                return carry

            lax.fori_loop(0, span, clear_one, 0)

    at_lane = 0
    for field in fields:
        left[:, at_lane : at_lane + field.shape[1]] = pieces(field[...])
        at_lane += field.shape[1]
    for i, b in enumerate(rows):
        at = rows_at[i]
        pltpu.make_async_copy(own.at[0, b], held.at[i], sems.at[i]).wait()

        @pl.when(rows_repeated[i])
        def _():
            for j in reversed(range(1, per_row)):
                target = jnp.int32(per_row)
                for k in range(j):
                    target = jnp.where(at[k] == at[j], k, target)

                @pl.when(target < per_row)
                def _():
                    held[i, target] = held[i, target] + held[i, j]

        def split(n, carry):
            part = pl.ds(pl.multiple_of(n * 16, 16), 16)
            for j in reversed(range(per_row)):
                head, tail = head_and_tail(
                    jnp.concatenate([held[i, j, 0, part], held[i, j, 1, part]], axis=1)
                )
                high[i, at[j], part] = head
                low[i, at[j], part] = tail
            return carry

        lax.fori_loop(0, size // 16, split, 0)
    for i, b in enumerate(rows):
        band = slice(block_rows - b, 2 * block_rows - b)
        sums[i] = product(left[...], high[i, band], low[i, band])


class Bands:
    def __init__(self, groups, refs):
        self.high, self.low = refs[:groups], refs[groups : 2 * groups]
        self.rows = [(n, i) for n, ref in enumerate(self.high) for i in range(ref.shape[0])]
        self.size = self.high[0].shape[2]

    def product(self, b, left, band):
        n, i = self.rows[b]
        return product(left, self.high[n][i, band], self.low[n][i, band])


def side_product(b, first, piece, is_before, bands):
    block_rows, size = len(bands.rows), bands.size
    last = first + piece.shape[1] // size
    if is_before:
        low_col, high_col, shift = max(b, first), last, -b
    else:
        low_col, high_col, shift = first, min(b + 1, last), 2 * block_rows - b
    if low_col >= high_col:
        return 0.0
    lanes = slice((low_col - first) * size, (high_col - first) * size)
    band = slice(low_col + shift, high_col + shift)
    return bands.product(b, piece[:, lanes], band)


def by_side(run):
    even = lax.axis_index("lat") % 2 == 0
    pl.when(even)(functools.partial(run, False))
    pl.when(jnp.logical_not(even))(functools.partial(run, True))


def early_kernel(groups, halo, *refs):
    bands, parts, (out, left) = Bands(groups, refs), refs[2 * groups : -2], refs[-2:]
    left[...] = pieces(halo[...])

    def run(swapped_before):
        for b, (n, i) in enumerate(bands.rows):
            out[b] = parts[n][i] + side_product(b, 0, left, swapped_before, bands)

    by_side(run)


def late_products(rows, swapped, diagonal, bands, sums, finish):
    first = (diagonal.shape[1] - swapped.shape[1]) // bands.size

    def run(swapped_before):
        for i, b in enumerate(rows):
            finish(
                i,
                b,
                sums[b]
                + side_product(b, 0, diagonal, not swapped_before, bands)
                + side_product(b, first, swapped, swapped_before, bands),
            )

    by_side(run)


def take_late(swapped, relayed, diagonal, swapped_left, diagonal_left):
    points = relayed.shape[1]
    swapped_left[...] = pieces(swapped[...])
    diagonal_left[:, :points] = pieces(relayed[...])
    diagonal_left[:, points:] = pieces(diagonal[...])


def leaving(value):
    channels, size = value.shape[0] // 2, value.shape[1] // 2
    return (
        value[:channels, :size] - value[channels:, size:],
        value[:channels, size:] + value[channels:, :size],
    )


def level_rows(groups, rows, swapped, diagonal, *refs):
    bands, (sums, next_coef, out) = Bands(groups, refs), refs[2 * groups :]

    def finish(i, b, value):
        re, im = leaving(value)
        channels, size = re.shape
        lanes = slice(i * size, (i + 1) * size)
        re, im = reflected(re, im, next_coef[0:1, lanes], next_coef[1:2, lanes])
        out[:channels, lanes] = re
        out[channels:, lanes] = im

    late_products(rows, swapped, diagonal, bands, sums, finish)


def first_rows_kernel(groups, rows, swapped, relayed, diagonal, *refs):
    operands, (swapped_left, diagonal_left) = refs[:-2], refs[-2:]
    take_late(swapped, relayed, diagonal, swapped_left, diagonal_left)
    level_rows(groups, rows, swapped_left, diagonal_left, *operands)


def bottom_kernel(groups, swapped, relayed, diagonal, *refs):
    bands = Bands(groups, refs)
    sums, out, held, swapped_left, diagonal_left, sems = refs[2 * groups :]
    panels, _, part, _ = out.shape
    block_rows, size = len(bands.rows), bands.size
    take_late(swapped, relayed, diagonal, swapped_left, diagonal_left)

    def copy_out(b):
        lanes = pl.ds(b * size, size)
        return pltpu.make_async_copy(
            held.at[b], out.at[:, :, :, lanes], sems.at[b]
        )

    def finish(i, b, value):
        re, im = leaving(value)
        held[b, :, 0] = re.reshape(panels, part, size)
        held[b, :, 1] = im.reshape(panels, part, size)
        copy_out(b).start()

    late_products(range(block_rows), swapped_left, diagonal_left, bands, sums, finish)
    for b in range(block_rows):
        copy_out(b).wait()


def in_hbm(value):
    return pltpu.with_memory_space_constraint(value, pltpu.HBM)


def params(mib):
    return pltpu.CompilerParams(vmem_limit_bytes=mib * MIB)


def cost(flops, transferred):
    return pl.CostEstimate(flops=flops, bytes_accessed=transferred, transcendentals=0)


def per_device(sources, blocks, block_cols, refl_level, refl_coef):
    lat_count = lax.axis_size("lat")
    panels, _, part, points = sources.shape
    _, block_rows, _, _, size, _ = blocks.shape
    channels = panels * part
    f32, bf16 = jnp.float32, jnp.bfloat16
    axes = ("depth", "lat")
    over_depth = [(0, 1), (1, 0)]
    even = range(0, lat_count - 1, 2)
    uneven = range(1, lat_count - 1, 2)
    alone_even = range(lat_count - lat_count % 2, lat_count)
    alone_uneven = [0] + list(range(lat_count - 1 + lat_count % 2, lat_count))

    def over_lat(firsts, alone):
        pairs = [(d * lat_count + i, d * lat_count + i + 1) for d in range(2) for i in firsts]
        pairs += [(i, lat_count + i) for i in alone]
        return pairs + [(j, i) for i, j in pairs]

    across = over_lat(uneven, alone_uneven)
    beside = over_lat(even, alone_even)
    onward = [(i, i + 2) for i in range(0, lat_count - 2, 2)]
    onward += [(i + 2, i) for i in range(1, lat_count - 2, 2)]
    top = lat_count - 1
    onward += [(top, top - 1) if top % 2 == 0 else (top - 1, top), (1, 0)]
    onward = [(d * lat_count + i, d * lat_count + j) for d in range(2) for i, j in onward]
    half = block_rows // 2
    first_rows, second_rows = range(half), range(half, block_rows)

    def part_shape(rows):
        return jax.ShapeDtypeStruct((2 * channels, len(rows) * size), f32)

    def piece_shape(rows):
        return (4 * channels, len(rows) * size), bf16

    def exchange(first, second):
        first_swapped = lax.ppermute(first, axes, beside)
        second = second()
        second_swapped = lax.ppermute(second, axes, beside)
        second_diagonal = lax.ppermute(second, axes, across)
        relayed = lax.ppermute(first_swapped, axes, onward)
        return second, first_swapped, (second_swapped, relayed, second_diagonal)

    other_blocks = lax.ppermute(blocks, "depth", over_depth)
    other_cols = lax.ppermute(block_cols, "depth", over_depth)
    refl_level = refl_level.reshape(1, points)

    def enter(rows, *tables):
        width = len(rows) * size
        return pl.pallas_call(
            functools.partial(enter_kernel, rows[0] * size, len(tables)),
            out_shape=[
                part_shape(rows),
                jax.ShapeDtypeStruct((2, width), f32),
                *(jax.ShapeDtypeStruct(table.shape, table.dtype) for table in tables),
            ],
            in_specs=[HBM] * (3 + len(tables)),
            out_specs=[VMEM] * (2 + len(tables)),
            scratch_shapes=[
                pltpu.VMEM((panels, 2, part, width), f32),
                pltpu.VMEM((1, width), jnp.int32),
                pltpu.VMEM((2, width), f32),
                pltpu.VMEM((2, width), f32),
                pltpu.SemaphoreType.DMA((3 + len(tables),)),
            ],
            compiler_params=params(4),
            name="enter",
        )(*map(in_hbm, (sources, refl_level, refl_coef, *tables)))

    coefs = []

    def enter_second():
        part_total, coef = enter(second_rows)
        coefs.append(coef)
        return part_total

    first_total, coef, own_cols = enter(first_rows, block_cols)
    coefs.append(coef)
    second_total, early, late = exchange(first_total, enter_second)

    sums_shape = jax.ShapeDtypeStruct((block_rows, 2 * channels, 2 * size), f32)
    macs = 6 * channels * points * 2 * size

    def prepare(level, rows, *fields):
        band = jax.ShapeDtypeStruct((len(rows), 2 * block_rows + 1, size, 2 * size), bf16)
        sums = jax.ShapeDtypeStruct((len(rows), 2 * channels, 2 * size), f32)
        return pl.pallas_call(
            functools.partial(prepare_kernel, level, rows),
            out_shape=[band, band, sums],
            in_specs=[SMEM, SMEM, HBM, HBM] + [VMEM] * len(fields),
            out_specs=[VMEM] * 3,
            scratch_shapes=[
                pltpu.VMEM((len(rows),) + blocks.shape[2:], f32),
                pltpu.VMEM((4 * channels, points), bf16),
                pltpu.SemaphoreType.DMA((len(rows),)),
            ],
            compiler_params=params(16),
            cost_estimate=cost(2 * macs, 4 * blocks.size),
            name="prepare",
        )(own_cols, other_cols, in_hbm(blocks), other_blocks, *fields)

    every_row = range(block_rows)
    row_groups = ((every_row,), (every_row[:1], every_row[1:]))

    def early_products(level, halo, *fields):
        ready = []
        for rows in row_groups[level]:
            ready.append(prepare(level, rows, *fields))
        high, low, parts = zip(*ready)
        sums = pl.pallas_call(
            functools.partial(early_kernel, len(ready)),
            out_shape=sums_shape,
            in_specs=[VMEM] * (1 + 3 * len(ready)),
            out_specs=VMEM,
            scratch_shapes=[pltpu.VMEM(*piece_shape(first_rows))],
            compiler_params=params(12),
            cost_estimate=cost(macs, blocks.size),
            name="early",
        )(halo, *high, *low, *parts)
        return *high, *low, sums

    bands = early_products(0, early, first_total, second_total)
    first_part, swapped_left, diagonal_left = pl.pallas_call(
        functools.partial(first_rows_kernel, len(row_groups[0]), first_rows),
        out_shape=[
            part_shape(first_rows),
            jax.ShapeDtypeStruct(*piece_shape(second_rows)),
            jax.ShapeDtypeStruct(*piece_shape(every_row)),
        ],
        in_specs=[VMEM] * (4 + len(bands)),
        out_specs=[VMEM] * 3,
        compiler_params=params(12),
        cost_estimate=cost(macs, blocks.size),
        name="first_rows",
    )(*late, *bands, coefs[0])

    def level_second():
        return pl.pallas_call(
            functools.partial(level_rows, len(row_groups[0]), second_rows),
            out_shape=part_shape(second_rows),
            in_specs=[VMEM] * (3 + len(bands)),
            out_specs=VMEM,
            compiler_params=params(12),
            cost_estimate=cost(macs, blocks.size),
            name="second_rows",
        )(swapped_left, diagonal_left, *bands, coefs[1])

    second_part, early, late = exchange(first_part, level_second)
    last_bands = early_products(1, early, first_part, second_part)
    return pl.pallas_call(
        functools.partial(bottom_kernel, len(row_groups[1])),
        out_shape=jax.ShapeDtypeStruct(sources.shape, f32),
        in_specs=[VMEM] * (3 + len(last_bands)),
        out_specs=HBM,
        scratch_shapes=[
            pltpu.VMEM((block_rows, panels, 2, part, size), f32),
            pltpu.VMEM(*piece_shape(second_rows)),
            pltpu.VMEM(*piece_shape(every_row)),
            pltpu.SemaphoreType.DMA((block_rows,)),
        ],
        compiler_params=params(12),
        cost_estimate=cost(macs, blocks.size),
        name="bottom",
    )(*late, *last_bands)


def solution(mesh):
    placed = (
        P("shot", None, "depth", "lat"),
        P(("shot", "depth"), "lat", None, None, None, None),
        P("depth", "lat", None),
        P("lat"),
        P(None, "lat"),
    )
    return jax.shard_map(
        per_device,
        mesh=mesh,
        in_specs=placed,
        out_specs=P("shot", None, "depth", "lat"),
        check_vma=False,
    )
```

```python
import functools

import jax
import jax.numpy as jnp
from jax import lax
from jax.experimental import pallas as pl
from jax.experimental.pallas import tpu as pltpu
from jax.sharding import PartitionSpec as P


VMEM = pl.BlockSpec(memory_space=pltpu.VMEM)
SMEM = pl.BlockSpec(memory_space=pltpu.SMEM)
HBM = pl.BlockSpec(memory_space=pltpu.HBM)
MIB = 1 << 20


def reflected(field_re, field_im, coef_re, coef_im):
    return (
        field_re + coef_re * field_re - coef_im * field_im,
        field_im + coef_re * field_im + coef_im * field_re,
    )


def entered(sources, coef):
    panels = [
        reflected(sources[k, 0], sources[k, 1], coef[0:1, :], coef[1:2, :])
        for k in range(sources.shape[0])
    ]
    return jnp.concatenate([re for re, _ in panels] + [im for _, im in panels], axis=0)


def enter_kernel(first, tables, sources, refl_level, refl_coef, *refs):
    tables_in, (total, next_coef), refs = refs[:tables], refs[tables : tables + 2], refs[tables + 2 :]
    tables_out, (held, level_held, coef_held, coef, sems) = refs[:tables], refs[tables:]
    lanes = pl.ds(first, total.shape[1])
    copies = [
        pltpu.make_async_copy(a, b, sems.at[i])
        for i, (a, b) in enumerate(
            (
                (sources.at[:, :, :, lanes], held),
                (refl_level.at[:, lanes], level_held),
                (refl_coef.at[:, lanes], coef_held),
                *zip(tables_in, tables_out),
            )
        )
    ]
    for copy in copies:
        copy.start()
    for copy in copies:
        copy.wait()
    coef[...] = jnp.where(level_held[...] == 0, coef_held[...], 0.0)
    next_coef[...] = jnp.where(level_held[...] == 1, coef_held[...], 0.0)
    total[...] = entered(held, coef)


def head_and_tail(value):
    head = value.astype(jnp.bfloat16)
    return head, (value - head.astype(jnp.float32)).astype(jnp.bfloat16)


def pieces(value):
    return jnp.concatenate(head_and_tail(value), axis=0)


def product(left, high, low):
    rows = left.shape[0] // 2
    high = high.reshape(high.shape[0] * high.shape[1], high.shape[2])
    low = low.reshape(high.shape)
    both = jnp.dot(left, high, preferred_element_type=jnp.float32)
    cross = jnp.dot(left[:rows], low, preferred_element_type=jnp.float32)
    return both[:rows] + both[rows:] + cross


def prepare_kernel(level, rows, halos, done, own_cols, other_cols, own, received, *refs):
    outs = len(refs) - 6 - halos
    high, low, sums, held, left, *early, sems = refs[outs:]
    fields, refs = refs[: outs - halos - 3 * done], refs[outs - halos - 3 * done : outs]
    halo, refs = refs[:halos], refs[halos:]
    parts = refs[2 * done :]
    bands = Bands(done + 1, (*refs[:done], high, *refs[done : 2 * done], low))
    per_row, size = held.shape[1], held.shape[3]
    block_rows = own.shape[1]
    here = lax.axis_index("depth") == level
    first_row = lax.axis_index("lat") * block_rows
    for i, b in enumerate(rows):

        @pl.when(here)
        def _():
            pltpu.make_async_copy(own.at[0, b], held.at[i], sems.at[i]).start()

        @pl.when(jnp.logical_not(here))
        def _():
            pltpu.make_async_copy(received.at[0, b], held.at[i], sems.at[i]).start()

    span = 2 * block_rows + 1
    zeros = jnp.zeros((size, 2 * size), jnp.bfloat16)

    def clear(i, o):
        high[i, o] = zeros
        low[i, o] = zeros

    rows_at, rows_repeated = [], []
    for i, b in enumerate(rows):
        first = first_row + b - block_rows
        at = [
            jnp.where(here, own_cols[0, b, j], other_cols[0, b, j]) - first
            for j in range(per_row)
        ]
        bits = [jnp.left_shift(1, a) for a in at]
        present = functools.reduce(jnp.bitwise_or, bits)
        repeated = sum(bits) != present
        rows_at.append(at)
        rows_repeated.append(repeated)
        absent = (1 << span) - 1 - present
        lowest = sum(jnp.where(absent % (2 << o) == 0, 1, 0) for o in range(span - 1))
        highest = sum(jnp.where(absent >= (2 << o), 1, 0) for o in range(span - 1))
        clear(i, lowest)
        clear(i, highest)
        between = repeated if span - per_row == 2 else True

        @pl.when(between)
        def _():
            def clear_one(o, carry):
                @pl.when(jnp.bitwise_and(jnp.right_shift(absent, o), 1) == 1)
                def _():
                    clear(i, o)

                return carry

            lax.fori_loop(lowest + 1, highest, clear_one, 0)

    at_lane = 0
    for field in fields:
        left[:, at_lane : at_lane + field.shape[1]] = pieces(field[...])
        at_lane += field.shape[1]
    for i, b in enumerate(rows):
        at = rows_at[i]
        pltpu.make_async_copy(own.at[0, b], held.at[i], sems.at[i]).wait()

        @pl.when(rows_repeated[i])
        def _():
            for j in reversed(range(1, per_row)):
                target = jnp.int32(per_row)
                for k in range(j):
                    target = jnp.where(at[k] == at[j], k, target)

                @pl.when(target < per_row)
                def _():
                    held[i, target] = held[i, target] + held[i, j]

        def split(n, carry):
            part = pl.ds(pl.multiple_of(n * 16, 16), 16)
            for j in reversed(range(per_row)):
                head, tail = head_and_tail(
                    jnp.concatenate([held[i, j, 0, part], held[i, j, 1, part]], axis=1)
                )
                high[i, at[j], part] = head
                low[i, at[j], part] = tail
            return carry

        lax.fori_loop(0, size // 16, split, 0, unroll=2)
    finished = block_rows - len(rows) if halos else 0
    for i, b in enumerate(rows):
        band = slice(block_rows - b, 2 * block_rows - b)
        sums[finished + i] = product(left[...], high[i, band], low[i, band])
    if halos:
        early[0][...] = pieces(halo[0][...])

        def run(swapped_before):
            for b, (n, i) in enumerate(bands.rows):
                before = parts[n][i] if n < done else sums[b]
                sums[b] = before + side_product(b, 0, early[0], swapped_before, bands)

        by_side(run)


class Bands:
    def __init__(self, groups, refs):
        self.high, self.low = refs[:groups], refs[groups : 2 * groups]
        self.rows = [(n, i) for n, ref in enumerate(self.high) for i in range(ref.shape[0])]
        self.size = self.high[0].shape[2]

    def product(self, b, left, band):
        n, i = self.rows[b]
        return product(left, self.high[n][i, band], self.low[n][i, band])


def side_product(b, first, piece, is_before, bands):
    block_rows, size = len(bands.rows), bands.size
    last = first + piece.shape[1] // size
    if is_before:
        low_col, high_col, shift = max(b, first), last, -b
    else:
        low_col, high_col, shift = first, min(b + 1, last), 2 * block_rows - b
    if low_col >= high_col:
        return 0.0
    lanes = slice((low_col - first) * size, (high_col - first) * size)
    band = slice(low_col + shift, high_col + shift)
    return bands.product(b, piece[:, lanes], band)


def by_side(run):
    even = lax.axis_index("lat") % 2 == 0
    pl.when(even)(functools.partial(run, False))
    pl.when(jnp.logical_not(even))(functools.partial(run, True))


def late_products(rows, swapped, diagonal, bands, sums, finish):
    first = (diagonal.shape[1] - swapped.shape[1]) // bands.size

    def run(swapped_before):
        for i, b in enumerate(rows):
            finish(
                i,
                b,
                sums[b]
                + side_product(b, 0, diagonal, not swapped_before, bands)
                + side_product(b, first, swapped, swapped_before, bands),
            )

    by_side(run)


def take_late(swapped, relayed, diagonal, swapped_left, diagonal_left):
    points = relayed.shape[1]
    swapped_left[...] = pieces(swapped[...])
    diagonal_left[:, :points] = pieces(relayed[...])
    diagonal_left[:, points:] = pieces(diagonal[...])


def leaving(value):
    channels, size = value.shape[0] // 2, value.shape[1] // 2
    return (
        value[:channels, :size] - value[channels:, size:],
        value[:channels, size:] + value[channels:, :size],
    )


def level_rows(groups, rows, swapped, diagonal, *refs):
    bands, (sums, next_coef, out) = Bands(groups, refs), refs[2 * groups :]

    def finish(i, b, value):
        re, im = leaving(value)
        channels, size = re.shape
        lanes = slice(i * size, (i + 1) * size)
        re, im = reflected(re, im, next_coef[0:1, lanes], next_coef[1:2, lanes])
        out[:channels, lanes] = re
        out[channels:, lanes] = im

    late_products(rows, swapped, diagonal, bands, sums, finish)


def first_rows_kernel(groups, rows, swapped, relayed, diagonal, *refs):
    operands, (swapped_left, diagonal_left) = refs[:-2], refs[-2:]
    take_late(swapped, relayed, diagonal, swapped_left, diagonal_left)
    level_rows(groups, rows, swapped_left, diagonal_left, *operands)


def bottom_kernel(groups, swapped, relayed, diagonal, *refs):
    bands = Bands(groups, refs)
    sums, out, held, swapped_left, diagonal_left, sems = refs[2 * groups :]
    panels, _, part, _ = out.shape
    block_rows, size = len(bands.rows), bands.size
    take_late(swapped, relayed, diagonal, swapped_left, diagonal_left)

    def copy_out(b):
        lanes = pl.ds(b * size, size)
        return pltpu.make_async_copy(
            held.at[b], out.at[:, :, :, lanes], sems.at[b]
        )

    def finish(i, b, value):
        re, im = leaving(value)
        held[b, :, 0] = re.reshape(panels, part, size)
        held[b, :, 1] = im.reshape(panels, part, size)
        copy_out(b).start()

    late_products(range(block_rows), swapped_left, diagonal_left, bands, sums, finish)
    for b in range(block_rows):
        copy_out(b).wait()


def in_hbm(value):
    return pltpu.with_memory_space_constraint(value, pltpu.HBM)


def params(mib):
    return pltpu.CompilerParams(vmem_limit_bytes=mib * MIB)


def cost(flops, transferred):
    return pl.CostEstimate(flops=flops, bytes_accessed=transferred, transcendentals=0)


def per_device(sources, blocks, block_cols, refl_level, refl_coef):
    lat_count = lax.axis_size("lat")
    panels, _, part, points = sources.shape
    _, block_rows, _, _, size, _ = blocks.shape
    channels = panels * part
    f32, bf16 = jnp.float32, jnp.bfloat16
    axes = ("depth", "lat")
    over_depth = [(0, 1), (1, 0)]
    even = range(0, lat_count - 1, 2)
    uneven = range(1, lat_count - 1, 2)
    alone_even = range(lat_count - lat_count % 2, lat_count)
    alone_uneven = [0] + list(range(lat_count - 1 + lat_count % 2, lat_count))

    def over_lat(firsts, alone):
        pairs = [(d * lat_count + i, d * lat_count + i + 1) for d in range(2) for i in firsts]
        pairs += [(i, lat_count + i) for i in alone]
        return pairs + [(j, i) for i, j in pairs]

    across = over_lat(uneven, alone_uneven)
    beside = over_lat(even, alone_even)
    onward = [(i, i + 2) for i in range(0, lat_count - 2, 2)]
    onward += [(i + 2, i) for i in range(1, lat_count - 2, 2)]
    top = lat_count - 1
    onward += [(top, top - 1) if top % 2 == 0 else (top - 1, top), (1, 0)]
    onward = [(d * lat_count + i, d * lat_count + j) for d in range(2) for i, j in onward]
    half = block_rows // 2
    first_rows, second_rows = range(half), range(half, block_rows)

    def part_shape(rows):
        return jax.ShapeDtypeStruct((2 * channels, len(rows) * size), f32)

    def piece_shape(rows):
        return (4 * channels, len(rows) * size), bf16

    def exchange(first, second):
        first_swapped = lax.ppermute(first, axes, beside)
        second = second()
        second_swapped = lax.ppermute(second, axes, beside)
        second_diagonal = lax.ppermute(second, axes, across)
        relayed = lax.ppermute(first_swapped, axes, onward)
        return second, first_swapped, (second_swapped, relayed, second_diagonal)

    other_blocks = lax.ppermute(blocks, "depth", over_depth)
    other_cols = lax.ppermute(block_cols, "depth", over_depth)
    refl_level = refl_level.reshape(1, points)

    def enter(rows, *tables):
        width = len(rows) * size
        return pl.pallas_call(
            functools.partial(enter_kernel, rows[0] * size, len(tables)),
            out_shape=[
                part_shape(rows),
                jax.ShapeDtypeStruct((2, width), f32),
                *(jax.ShapeDtypeStruct(table.shape, table.dtype) for table in tables),
            ],
            in_specs=[HBM] * (3 + len(tables)),
            out_specs=[VMEM] * (2 + len(tables)),
            scratch_shapes=[
                pltpu.VMEM((panels, 2, part, width), f32),
                pltpu.VMEM((1, width), jnp.int32),
                pltpu.VMEM((2, width), f32),
                pltpu.VMEM((2, width), f32),
                pltpu.SemaphoreType.DMA((3 + len(tables),)),
            ],
            compiler_params=params(4),
            name="enter",
        )(*map(in_hbm, (sources, refl_level, refl_coef, *tables)))

    coefs = []

    def enter_second():
        part_total, coef = enter(second_rows)
        coefs.append(coef)
        return part_total

    first_total, coef, own_cols = enter(first_rows, block_cols)
    coefs.append(coef)
    second_total, early, late = exchange(first_total, enter_second)

    macs = 6 * channels * points * 2 * size

    every_row = range(block_rows)
    row_groups = ((every_row,), (every_row[:1], every_row[1:]))

    def prepare(level, rows, fields, halo, ready):
        band = jax.ShapeDtypeStruct((len(rows), 2 * block_rows + 1, size, 2 * size), bf16)
        sums_rows = block_rows if halo else len(rows)
        sums = jax.ShapeDtypeStruct((sums_rows, 2 * channels, 2 * size), f32)
        operands = (*fields, *halo, *(array for arrays in zip(*ready) for array in arrays))
        return pl.pallas_call(
            functools.partial(prepare_kernel, level, rows, len(halo), len(ready)),
            out_shape=[band, band, sums],
            in_specs=[SMEM, SMEM, HBM, HBM] + [VMEM] * len(operands),
            out_specs=[VMEM] * 3,
            scratch_shapes=[
                pltpu.VMEM((len(rows),) + blocks.shape[2:], f32),
                pltpu.VMEM((4 * channels, points), bf16),
                *[pltpu.VMEM(*piece_shape(first_rows))] * len(halo),
                pltpu.SemaphoreType.DMA((len(rows),)),
            ],
            compiler_params=params(16),
            cost_estimate=cost(2 * macs, 4 * blocks.size),
            name="prepare",
        )(own_cols, other_cols, in_hbm(blocks), other_blocks, *operands)

    def early_products(level, halo, *fields):
        ready = []
        for n, rows in enumerate(row_groups[level]):
            is_last = n + 1 == len(row_groups[level])
            prepared = prepare(
                level, rows, fields, (halo,) if is_last else (), ready if is_last else []
            )
            ready.append(prepared)
        high, low, parts = zip(*ready)
        return *high, *low, parts[-1]

    bands = early_products(0, early, first_total, second_total)
    first_part, swapped_left, diagonal_left = pl.pallas_call(
        functools.partial(first_rows_kernel, len(row_groups[0]), first_rows),
        out_shape=[
            part_shape(first_rows),
            jax.ShapeDtypeStruct(*piece_shape(second_rows)),
            jax.ShapeDtypeStruct(*piece_shape(every_row)),
        ],
        in_specs=[VMEM] * (4 + len(bands)),
        out_specs=[VMEM] * 3,
        compiler_params=params(12),
        cost_estimate=cost(macs, blocks.size),
        name="first_rows",
    )(*late, *bands, coefs[0])

    def level_second():
        return pl.pallas_call(
            functools.partial(level_rows, len(row_groups[0]), second_rows),
            out_shape=part_shape(second_rows),
            in_specs=[VMEM] * (3 + len(bands)),
            out_specs=VMEM,
            compiler_params=params(12),
            cost_estimate=cost(macs, blocks.size),
            name="second_rows",
        )(swapped_left, diagonal_left, *bands, coefs[1])

    second_part, early, late = exchange(first_part, level_second)
    last_bands = early_products(1, early, first_part, second_part)
    return pl.pallas_call(
        functools.partial(bottom_kernel, len(row_groups[1])),
        out_shape=jax.ShapeDtypeStruct(sources.shape, f32),
        in_specs=[VMEM] * (3 + len(last_bands)),
        out_specs=HBM,
        scratch_shapes=[
            pltpu.VMEM((block_rows, panels, 2, part, size), f32),
            pltpu.VMEM(*piece_shape(second_rows)),
            pltpu.VMEM(*piece_shape(every_row)),
            pltpu.SemaphoreType.DMA((block_rows,)),
        ],
        compiler_params=params(12),
        cost_estimate=cost(macs, blocks.size),
        name="bottom",
    )(*late, *last_bands)


def solution(mesh):
    placed = (
        P("shot", None, "depth", "lat"),
        P(("shot", "depth"), "lat", None, None, None, None),
        P("depth", "lat", None),
        P("lat"),
        P(None, "lat"),
    )
    return jax.shard_map(
        per_device,
        mesh=mesh,
        in_specs=placed,
        out_specs=P("shot", None, "depth", "lat"),
        check_vma=False,
    )
```

```python
import functools

import jax
import jax.numpy as jnp
from jax import lax
from jax.experimental import pallas as pl
from jax.experimental.pallas import tpu as pltpu
from jax.sharding import PartitionSpec as P


VMEM = pl.BlockSpec(memory_space=pltpu.VMEM)
SMEM = pl.BlockSpec(memory_space=pltpu.SMEM)
HBM = pl.BlockSpec(memory_space=pltpu.HBM)
MIB = 1 << 20


def reflected(field_re, field_im, coef_re, coef_im):
    return (
        field_re + coef_re * field_re - coef_im * field_im,
        field_im + coef_re * field_im + coef_im * field_re,
    )


def entered(sources, coef):
    panels = [
        reflected(sources[k, 0], sources[k, 1], coef[0:1, :], coef[1:2, :])
        for k in range(sources.shape[0])
    ]
    return jnp.concatenate([re for re, _ in panels] + [im for _, im in panels], axis=0)


def enter_kernel(first, tables, sources, refl_level, refl_coef, *refs):
    tables_in, (total, next_coef), refs = refs[:tables], refs[tables : tables + 2], refs[tables + 2 :]
    tables_out, (held, level_held, coef_held, coef, sems) = refs[:tables], refs[tables:]
    lanes = pl.ds(first, total.shape[1])
    copies = [
        pltpu.make_async_copy(a, b, sems.at[i])
        for i, (a, b) in enumerate(
            (
                (sources.at[:, :, :, lanes], held),
                (refl_level.at[:, lanes], level_held),
                (refl_coef.at[:, lanes], coef_held),
                *zip(tables_in, tables_out),
            )
        )
    ]
    for copy in copies:
        copy.start()
    for copy in copies:
        copy.wait()
    coef[...] = jnp.where(level_held[...] == 0, coef_held[...], 0.0)
    next_coef[...] = jnp.where(level_held[...] == 1, coef_held[...], 0.0)
    total[...] = entered(held, coef)


def head_and_tail(value):
    head = value.astype(jnp.bfloat16)
    return head, (value - head.astype(jnp.float32)).astype(jnp.bfloat16)


def pieces(value):
    return jnp.concatenate(head_and_tail(value), axis=0)


def product(left, high, low):
    rows = left.shape[0] // 2
    high = high.reshape(high.shape[0] * high.shape[1], high.shape[2])
    low = low.reshape(high.shape)
    both = jnp.dot(left, high, preferred_element_type=jnp.float32)
    cross = jnp.dot(left[:rows], low, preferred_element_type=jnp.float32)
    return both[:rows] + both[rows:] + cross


def prepare_kernel(level, rows, halos, done, own_cols, other_cols, own, received, *refs):
    outs = len(refs) - 6 - halos
    high, low, sums, held, left, *early, sems = refs[outs:]
    fields, refs = refs[: outs - halos - 3 * done], refs[outs - halos - 3 * done : outs]
    halo, refs = refs[:halos], refs[halos:]
    parts = refs[2 * done :]
    bands = Bands(done + 1, (*refs[:done], high, *refs[done : 2 * done], low))
    per_row, size = held.shape[1], held.shape[3]
    block_rows = own.shape[1]
    here = lax.axis_index("depth") == level
    first_row = lax.axis_index("lat") * block_rows
    for i, b in enumerate(rows):

        @pl.when(here)
        def _():
            pltpu.make_async_copy(own.at[0, b], held.at[i], sems.at[i]).start()

    span = 2 * block_rows + 1
    zeros = jnp.zeros((size, 2 * size), jnp.bfloat16)

    def clear(i, o):
        high[i, o] = zeros
        low[i, o] = zeros

    rows_at, rows_repeated = [], []
    for i, b in enumerate(rows):
        first = first_row + b - block_rows
        at = [
            jnp.where(here, own_cols[0, b, j], other_cols[0, b, j]) - first
            for j in range(per_row)
        ]
        bits = [jnp.left_shift(1, a) for a in at]
        present = functools.reduce(jnp.bitwise_or, bits)
        repeated = sum(bits) != present
        rows_at.append(at)
        rows_repeated.append(repeated)
        absent = (1 << span) - 1 - present
        lowest = sum(jnp.where(absent % (2 << o) == 0, 1, 0) for o in range(span - 1))
        highest = sum(jnp.where(absent >= (2 << o), 1, 0) for o in range(span - 1))
        clear(i, lowest)
        clear(i, highest)
        between = repeated if span - per_row == 2 else True

        @pl.when(between)
        def _():
            def clear_one(o, carry):
                @pl.when(jnp.bitwise_and(jnp.right_shift(absent, o), 1) == 1)
                def _():
                    clear(i, o)

                return carry

            lax.fori_loop(lowest + 1, highest, clear_one, 0)

    at_lane = 0
    for field in fields:
        left[:, at_lane : at_lane + field.shape[1]] = pieces(field[...])
        at_lane += field.shape[1]
    for i, b in enumerate(rows):
        at = rows_at[i]
        other = jnp.logical_not(here)

        @pl.when(here)
        def _():
            pltpu.make_async_copy(own.at[0, b], held.at[i], sems.at[i]).wait()

        @pl.when(rows_repeated[i])
        def _():
            @pl.when(other)
            def _():
                copy = pltpu.make_async_copy(received.at[0, b], held.at[i], sems.at[i])
                copy.start()
                copy.wait()

            for j in reversed(range(1, per_row)):
                target = jnp.int32(per_row)
                for k in range(j):
                    target = jnp.where(at[k] == at[j], k, target)

                @pl.when(target < per_row)
                def _():
                    held[i, target] = held[i, target] + held[i, j]

        def split_from(blocks):
            def split(n, carry):
                part = pl.ds(pl.multiple_of(n * 16, 16), 16)
                for j in reversed(range(per_row)):
                    head, tail = head_and_tail(
                        jnp.concatenate([blocks[j, 0, part], blocks[j, 1, part]], axis=1)
                    )
                    high[i, at[j], part] = head
                    low[i, at[j], part] = tail
                return carry

            lax.fori_loop(0, size // 16, split, 0, unroll=2)

        copied = jnp.logical_or(here, rows_repeated[i])

        @pl.when(copied)
        def _():
            split_from(held.at[i])

        @pl.when(jnp.logical_not(copied))
        def _():
            split_from(received.at[0, b])

    finished = block_rows - len(rows) if halos else 0
    for i, b in enumerate(rows):
        band = slice(block_rows - b, 2 * block_rows - b)
        sums[finished + i] = product(left[...], high[i, band], low[i, band])
    if halos:
        early[0][...] = pieces(halo[0][...])

        def run(swapped_before):
            for b, (n, i) in enumerate(bands.rows):
                before = parts[n][i] if n < done else sums[b]
                sums[b] = before + side_product(b, 0, early[0], swapped_before, bands)

        by_side(run)


class Bands:
    def __init__(self, groups, refs):
        self.high, self.low = refs[:groups], refs[groups : 2 * groups]
        self.rows = [(n, i) for n, ref in enumerate(self.high) for i in range(ref.shape[0])]
        self.size = self.high[0].shape[2]

    def product(self, b, left, band):
        n, i = self.rows[b]
        return product(left, self.high[n][i, band], self.low[n][i, band])


def side_product(b, first, piece, is_before, bands):
    block_rows, size = len(bands.rows), bands.size
    last = first + piece.shape[1] // size
    if is_before:
        low_col, high_col, shift = max(b, first), last, -b
    else:
        low_col, high_col, shift = first, min(b + 1, last), 2 * block_rows - b
    if low_col >= high_col:
        return 0.0
    lanes = slice((low_col - first) * size, (high_col - first) * size)
    band = slice(low_col + shift, high_col + shift)
    return bands.product(b, piece[:, lanes], band)


def by_side(run):
    even = lax.axis_index("lat") % 2 == 0
    pl.when(even)(functools.partial(run, False))
    pl.when(jnp.logical_not(even))(functools.partial(run, True))


def late_products(rows, swapped, diagonal, bands, sums, finish):
    first = (diagonal.shape[1] - swapped.shape[1]) // bands.size

    def run(swapped_before):
        for i, b in enumerate(rows):
            finish(
                i,
                b,
                sums[b]
                + side_product(b, 0, diagonal, not swapped_before, bands)
                + side_product(b, first, swapped, swapped_before, bands),
            )

    by_side(run)


def take_late(swapped, relayed, diagonal, swapped_left, diagonal_left):
    points = relayed.shape[1]
    swapped_left[...] = pieces(swapped[...])
    diagonal_left[:, :points] = pieces(relayed[...])
    diagonal_left[:, points:] = pieces(diagonal[...])


def leaving(value):
    channels, size = value.shape[0] // 2, value.shape[1] // 2
    return (
        value[:channels, :size] - value[channels:, size:],
        value[:channels, size:] + value[channels:, :size],
    )


def level_rows(groups, rows, swapped, diagonal, *refs):
    bands, (sums, next_coef, out) = Bands(groups, refs), refs[2 * groups :]

    def finish(i, b, value):
        re, im = leaving(value)
        channels, size = re.shape
        lanes = slice(i * size, (i + 1) * size)
        re, im = reflected(re, im, next_coef[0:1, lanes], next_coef[1:2, lanes])
        out[:channels, lanes] = re
        out[channels:, lanes] = im

    late_products(rows, swapped, diagonal, bands, sums, finish)


def first_rows_kernel(groups, rows, swapped, relayed, diagonal, *refs):
    operands, (swapped_left, diagonal_left) = refs[:-2], refs[-2:]
    take_late(swapped, relayed, diagonal, swapped_left, diagonal_left)
    level_rows(groups, rows, swapped_left, diagonal_left, *operands)


def bottom_kernel(groups, swapped, relayed, diagonal, *refs):
    bands = Bands(groups, refs)
    sums, out, held, swapped_left, diagonal_left, sems = refs[2 * groups :]
    panels, _, part, _ = out.shape
    block_rows, size = len(bands.rows), bands.size
    take_late(swapped, relayed, diagonal, swapped_left, diagonal_left)

    def copy_out(b):
        lanes = pl.ds(b * size, size)
        return pltpu.make_async_copy(
            held.at[b], out.at[:, :, :, lanes], sems.at[b]
        )

    def finish(i, b, value):
        re, im = leaving(value)
        held[b, :, 0] = re.reshape(panels, part, size)
        held[b, :, 1] = im.reshape(panels, part, size)
        copy_out(b).start()

    late_products(range(block_rows), swapped_left, diagonal_left, bands, sums, finish)
    for b in range(block_rows):
        copy_out(b).wait()


def in_hbm(value):
    return pltpu.with_memory_space_constraint(value, pltpu.HBM)


def params(mib):
    return pltpu.CompilerParams(vmem_limit_bytes=mib * MIB)


def cost(flops, transferred):
    return pl.CostEstimate(flops=flops, bytes_accessed=transferred, transcendentals=0)


def per_device(sources, blocks, block_cols, refl_level, refl_coef):
    lat_count = lax.axis_size("lat")
    panels, _, part, points = sources.shape
    _, block_rows, _, _, size, _ = blocks.shape
    channels = panels * part
    f32, bf16 = jnp.float32, jnp.bfloat16
    axes = ("depth", "lat")
    over_depth = [(0, 1), (1, 0)]
    even = range(0, lat_count - 1, 2)
    uneven = range(1, lat_count - 1, 2)
    alone_even = range(lat_count - lat_count % 2, lat_count)
    alone_uneven = [0] + list(range(lat_count - 1 + lat_count % 2, lat_count))

    def over_lat(firsts, alone):
        pairs = [(d * lat_count + i, d * lat_count + i + 1) for d in range(2) for i in firsts]
        pairs += [(i, lat_count + i) for i in alone]
        return pairs + [(j, i) for i, j in pairs]

    across = over_lat(uneven, alone_uneven)
    beside = over_lat(even, alone_even)
    onward = [(i, i + 2) for i in range(0, lat_count - 2, 2)]
    onward += [(i + 2, i) for i in range(1, lat_count - 2, 2)]
    top = lat_count - 1
    onward += [(top, top - 1) if top % 2 == 0 else (top - 1, top), (1, 0)]
    onward = [(d * lat_count + i, d * lat_count + j) for d in range(2) for i, j in onward]
    half = block_rows // 2
    first_rows, second_rows = range(half), range(half, block_rows)

    def part_shape(rows):
        return jax.ShapeDtypeStruct((2 * channels, len(rows) * size), f32)

    def piece_shape(rows):
        return (4 * channels, len(rows) * size), bf16

    def exchange(first, second):
        first_swapped = lax.ppermute(first, axes, beside)
        second = second()
        second_swapped = lax.ppermute(second, axes, beside)
        second_diagonal = lax.ppermute(second, axes, across)
        relayed = lax.ppermute(first_swapped, axes, onward)
        return second, first_swapped, (second_swapped, relayed, second_diagonal)

    other_blocks = lax.ppermute(blocks, "depth", over_depth)
    other_cols = lax.ppermute(block_cols, "depth", over_depth)
    refl_level = refl_level.reshape(1, points)

    def enter(rows, *tables):
        width = len(rows) * size
        return pl.pallas_call(
            functools.partial(enter_kernel, rows[0] * size, len(tables)),
            out_shape=[
                part_shape(rows),
                jax.ShapeDtypeStruct((2, width), f32),
                *(jax.ShapeDtypeStruct(table.shape, table.dtype) for table in tables),
            ],
            in_specs=[HBM] * (3 + len(tables)),
            out_specs=[VMEM] * (2 + len(tables)),
            scratch_shapes=[
                pltpu.VMEM((panels, 2, part, width), f32),
                pltpu.VMEM((1, width), jnp.int32),
                pltpu.VMEM((2, width), f32),
                pltpu.VMEM((2, width), f32),
                pltpu.SemaphoreType.DMA((3 + len(tables),)),
            ],
            compiler_params=params(4),
            name="enter",
        )(*map(in_hbm, (sources, refl_level, refl_coef, *tables)))

    coefs = []

    def enter_second():
        part_total, coef = enter(second_rows)
        coefs.append(coef)
        return part_total

    first_total, coef, own_cols = enter(first_rows, block_cols)
    coefs.append(coef)
    second_total, early, late = exchange(first_total, enter_second)

    macs = 6 * channels * points * 2 * size

    every_row = range(block_rows)
    row_groups = ((every_row,), (every_row[:1], every_row[1:]))

    def prepare(level, rows, fields, halo, ready):
        band = jax.ShapeDtypeStruct((len(rows), 2 * block_rows + 1, size, 2 * size), bf16)
        sums_rows = block_rows if halo else len(rows)
        sums = jax.ShapeDtypeStruct((sums_rows, 2 * channels, 2 * size), f32)
        operands = (*fields, *halo, *(array for arrays in zip(*ready) for array in arrays))
        return pl.pallas_call(
            functools.partial(prepare_kernel, level, rows, len(halo), len(ready)),
            out_shape=[band, band, sums],
            in_specs=[SMEM, SMEM, HBM, VMEM] + [VMEM] * len(operands),
            out_specs=[VMEM] * 3,
            scratch_shapes=[
                pltpu.VMEM((len(rows),) + blocks.shape[2:], f32),
                pltpu.VMEM((4 * channels, points), bf16),
                *[pltpu.VMEM(*piece_shape(first_rows))] * len(halo),
                pltpu.SemaphoreType.DMA((len(rows),)),
            ],
            compiler_params=params(16),
            cost_estimate=cost(2 * macs, 4 * blocks.size),
            name="prepare",
        )(own_cols, other_cols, in_hbm(blocks), other_blocks, *operands)

    def early_products(level, halo, *fields):
        ready = []
        for n, rows in enumerate(row_groups[level]):
            is_last = n + 1 == len(row_groups[level])
            prepared = prepare(
                level, rows, fields, (halo,) if is_last else (), ready if is_last else []
            )
            ready.append(prepared)
        high, low, parts = zip(*ready)
        return *high, *low, parts[-1]

    bands = early_products(0, early, first_total, second_total)
    first_part, swapped_left, diagonal_left = pl.pallas_call(
        functools.partial(first_rows_kernel, len(row_groups[0]), first_rows),
        out_shape=[
            part_shape(first_rows),
            jax.ShapeDtypeStruct(*piece_shape(second_rows)),
            jax.ShapeDtypeStruct(*piece_shape(every_row)),
        ],
        in_specs=[VMEM] * (4 + len(bands)),
        out_specs=[VMEM] * 3,
        compiler_params=params(12),
        cost_estimate=cost(macs, blocks.size),
        name="first_rows",
    )(*late, *bands, coefs[0])

    def level_second():
        return pl.pallas_call(
            functools.partial(level_rows, len(row_groups[0]), second_rows),
            out_shape=part_shape(second_rows),
            in_specs=[VMEM] * (3 + len(bands)),
            out_specs=VMEM,
            compiler_params=params(12),
            cost_estimate=cost(macs, blocks.size),
            name="second_rows",
        )(swapped_left, diagonal_left, *bands, coefs[1])

    second_part, early, late = exchange(first_part, level_second)
    last_bands = early_products(1, early, first_part, second_part)
    return pl.pallas_call(
        functools.partial(bottom_kernel, len(row_groups[1])),
        out_shape=jax.ShapeDtypeStruct(sources.shape, f32),
        in_specs=[VMEM] * (3 + len(last_bands)),
        out_specs=HBM,
        scratch_shapes=[
            pltpu.VMEM((block_rows, panels, 2, part, size), f32),
            pltpu.VMEM(*piece_shape(second_rows)),
            pltpu.VMEM(*piece_shape(every_row)),
            pltpu.SemaphoreType.DMA((block_rows,)),
        ],
        compiler_params=params(12),
        cost_estimate=cost(macs, blocks.size),
        name="bottom",
    )(*late, *last_bands)


def solution(mesh):
    placed = (
        P("shot", None, "depth", "lat"),
        P(("shot", "depth"), "lat", None, None, None, None),
        P("depth", "lat", None),
        P("lat"),
        P(None, "lat"),
    )
    return jax.shard_map(
        per_device,
        mesh=mesh,
        in_specs=placed,
        out_specs=P("shot", None, "depth", "lat"),
        check_vma=False,
    )
```

```python
import functools

import jax
import jax.numpy as jnp
from jax import lax
from jax.experimental import pallas as pl
from jax.experimental.pallas import tpu as pltpu
from jax.sharding import PartitionSpec as P


VMEM = pl.BlockSpec(memory_space=pltpu.VMEM)
SMEM = pl.BlockSpec(memory_space=pltpu.SMEM)
HBM = pl.BlockSpec(memory_space=pltpu.HBM)
MIB = 1 << 20


def reflected(field_re, field_im, coef_re, coef_im):
    return (
        field_re + coef_re * field_re - coef_im * field_im,
        field_im + coef_re * field_im + coef_im * field_re,
    )


def entered(sources, coef):
    panels = [
        reflected(sources[k, 0], sources[k, 1], coef[0:1, :], coef[1:2, :])
        for k in range(sources.shape[0])
    ]
    return jnp.concatenate([re for re, _ in panels] + [im for _, im in panels], axis=0)


def enter_kernel(first, tables, sources, refl_level, refl_coef, *refs):
    tables_in, (total, next_coef), refs = refs[:tables], refs[tables : tables + 2], refs[tables + 2 :]
    tables_out, (held, level_held, coef_held, coef, sems) = refs[:tables], refs[tables:]
    lanes = pl.ds(first, total.shape[1])
    copies = [
        pltpu.make_async_copy(a, b, sems.at[i])
        for i, (a, b) in enumerate(
            (
                (sources.at[:, :, :, lanes], held),
                (refl_level.at[:, lanes], level_held),
                (refl_coef.at[:, lanes], coef_held),
                *((a.at[:, : b.shape[1]], b) for a, b in zip(tables_in, tables_out)),
            )
        )
    ]
    for copy in copies:
        copy.start()
    for copy in copies:
        copy.wait()
    coef[...] = jnp.where(level_held[...] == 0, coef_held[...], 0.0)
    next_coef[...] = jnp.where(level_held[...] == 1, coef_held[...], 0.0)
    total[...] = entered(held, coef)


def fetch_kernel(table, out, sems):
    count = out.shape[1]
    for i in range(count):
        pltpu.make_async_copy(table.at[0, i], out.at[0, i], sems.at[i]).start()
    for i in range(count):
        pltpu.make_async_copy(table.at[0, i], out.at[0, i], sems.at[i]).wait()


def head_and_tail(value):
    head = value.astype(jnp.bfloat16)
    return head, (value - head.astype(jnp.float32)).astype(jnp.bfloat16)


def pieces(value):
    return jnp.concatenate(head_and_tail(value), axis=0)


def product(left, high, low):
    rows = left.shape[0] // 2
    high = high.reshape(high.shape[0] * high.shape[1], high.shape[2])
    low = low.reshape(high.shape)
    both = jnp.dot(left, high, preferred_element_type=jnp.float32)
    cross = jnp.dot(left[:rows], low, preferred_element_type=jnp.float32)
    return both[:rows] + both[rows:] + cross


def prepare_kernel(level, rows, halos, done, own_cols, other_cols, own, near, received, *refs):
    outs = len(refs) - 6 - halos
    high, low, sums, held, left, *early, sems = refs[outs:]
    fields, refs = refs[: outs - halos - 3 * done], refs[outs - halos - 3 * done : outs]
    halo, refs = refs[:halos], refs[halos:]
    parts = refs[2 * done :]
    bands = Bands(done + 1, (*refs[:done], high, *refs[done : 2 * done], low))
    per_row, size = held.shape[1], held.shape[3]
    block_rows = own.shape[1]
    here = lax.axis_index("depth") == level
    first_row = lax.axis_index("lat") * block_rows
    other = jnp.logical_not(here)
    far = [b >= near.shape[1] for b in rows]

    def start(condition, source, i, b):
        @pl.when(condition)
        def _():
            pltpu.make_async_copy(source.at[0, b], held.at[i], sems.at[i]).start()

    for i, b in enumerate(rows):
        if far[i]:
            start(here, own, i, b)

    span = 2 * block_rows + 1
    zeros = jnp.zeros((size, 2 * size), jnp.bfloat16)

    def clear(i, o):
        high[i, o] = zeros
        low[i, o] = zeros

    rows_at, rows_repeated = [], []
    for i, b in enumerate(rows):
        first = first_row + b - block_rows
        at = [
            jnp.where(here, own_cols[0, b, j], other_cols[0, b, j]) - first
            for j in range(per_row)
        ]
        bits = [jnp.left_shift(1, a) for a in at]
        present = functools.reduce(jnp.bitwise_or, bits)
        repeated = sum(bits) != present
        rows_at.append(at)
        rows_repeated.append(repeated)
        start(jnp.logical_and(other, repeated), received, i, b)
        if not far[i]:
            start(jnp.logical_and(here, repeated), near, i, b)
        absent = (1 << span) - 1 - present
        lowest = sum(jnp.where(absent % (2 << o) == 0, 1, 0) for o in range(span - 1))
        highest = sum(jnp.where(absent >= (2 << o), 1, 0) for o in range(span - 1))
        clear(i, lowest)
        clear(i, highest)
        between = repeated if span - per_row == 2 else True

        @pl.when(between)
        def _():
            def clear_one(o, carry):
                @pl.when(jnp.bitwise_and(jnp.right_shift(absent, o), 1) == 1)
                def _():
                    clear(i, o)

                return carry

            lax.fori_loop(lowest + 1, highest, clear_one, 0)

    at_lane = 0
    for field in fields:
        left[:, at_lane : at_lane + field.shape[1]] = pieces(field[...])
        at_lane += field.shape[1]
    for i, b in enumerate(rows):
        at = rows_at[i]
        copied = jnp.logical_or(here, rows_repeated[i]) if far[i] else rows_repeated[i]

        @pl.when(copied)
        def _():
            pltpu.make_async_copy(received.at[0, b], held.at[i], sems.at[i]).wait()

        @pl.when(rows_repeated[i])
        def _():
            for j in reversed(range(1, per_row)):
                target = jnp.int32(per_row)
                for k in range(j):
                    target = jnp.where(at[k] == at[j], k, target)

                @pl.when(target < per_row)
                def _():
                    held[i, target] = held[i, target] + held[i, j]

        def split_from(blocks):
            def split(n, carry):
                part = pl.ds(pl.multiple_of(n * 16, 16), 16)
                for j in reversed(range(per_row)):
                    head, tail = head_and_tail(
                        jnp.concatenate([blocks[j, 0, part], blocks[j, 1, part]], axis=1)
                    )
                    high[i, at[j], part] = head
                    low[i, at[j], part] = tail
                return carry

            lax.fori_loop(0, size // 16, split, 0, unroll=2)

        direct = jnp.logical_not(copied)

        @pl.when(copied)
        def _():
            split_from(held.at[i])

        @pl.when(jnp.logical_and(direct, other))
        def _():
            split_from(received.at[0, b])

        if not far[i]:

            @pl.when(jnp.logical_and(direct, here))
            def _():
                split_from(near.at[0, b])

    finished = block_rows - len(rows) if halos else 0
    for i, b in enumerate(rows):
        band = slice(block_rows - b, 2 * block_rows - b)
        sums[finished + i] = product(left[...], high[i, band], low[i, band])
    if halos:
        early[0][...] = pieces(halo[0][...])

        def run(swapped_before):
            for b, (n, i) in enumerate(bands.rows):
                before = parts[n][i] if n < done else sums[b]
                sums[b] = before + side_product(b, 0, early[0], swapped_before, bands)

        by_side(run)


class Bands:
    def __init__(self, groups, refs):
        self.high, self.low = refs[:groups], refs[groups : 2 * groups]
        self.rows = [(n, i) for n, ref in enumerate(self.high) for i in range(ref.shape[0])]
        self.size = self.high[0].shape[2]

    def product(self, b, left, band):
        n, i = self.rows[b]
        return product(left, self.high[n][i, band], self.low[n][i, band])


def side_product(b, first, piece, is_before, bands):
    block_rows, size = len(bands.rows), bands.size
    last = first + piece.shape[1] // size
    if is_before:
        low_col, high_col, shift = max(b, first), last, -b
    else:
        low_col, high_col, shift = first, min(b + 1, last), 2 * block_rows - b
    if low_col >= high_col:
        return 0.0
    lanes = slice((low_col - first) * size, (high_col - first) * size)
    band = slice(low_col + shift, high_col + shift)
    return bands.product(b, piece[:, lanes], band)


def by_side(run):
    even = lax.axis_index("lat") % 2 == 0
    pl.when(even)(functools.partial(run, False))
    pl.when(jnp.logical_not(even))(functools.partial(run, True))


def late_products(rows, swapped, diagonal, bands, sums, finish):
    first = (diagonal.shape[1] - swapped.shape[1]) // bands.size

    def run(swapped_before):
        for i, b in enumerate(rows):
            finish(
                i,
                b,
                sums[b]
                + side_product(b, 0, diagonal, not swapped_before, bands)
                + side_product(b, first, swapped, swapped_before, bands),
            )

    by_side(run)


def take_late(swapped, relayed, diagonal, swapped_left, diagonal_left):
    points = relayed.shape[1]
    swapped_left[...] = pieces(swapped[...])
    diagonal_left[:, :points] = pieces(relayed[...])
    diagonal_left[:, points:] = pieces(diagonal[...])


def leaving(value):
    channels, size = value.shape[0] // 2, value.shape[1] // 2
    return (
        value[:channels, :size] - value[channels:, size:],
        value[:channels, size:] + value[channels:, :size],
    )


def level_rows(groups, rows, swapped, diagonal, *refs):
    bands, (sums, next_coef, out) = Bands(groups, refs), refs[2 * groups :]

    def finish(i, b, value):
        re, im = leaving(value)
        channels, size = re.shape
        lanes = slice(i * size, (i + 1) * size)
        re, im = reflected(re, im, next_coef[0:1, lanes], next_coef[1:2, lanes])
        out[:channels, lanes] = re
        out[channels:, lanes] = im

    late_products(rows, swapped, diagonal, bands, sums, finish)


def first_rows_kernel(groups, rows, swapped, relayed, diagonal, *refs):
    operands, (swapped_left, diagonal_left) = refs[:-2], refs[-2:]
    take_late(swapped, relayed, diagonal, swapped_left, diagonal_left)
    level_rows(groups, rows, swapped_left, diagonal_left, *operands)


def bottom_kernel(groups, swapped, relayed, diagonal, *refs):
    bands = Bands(groups, refs)
    sums, out, held, swapped_left, diagonal_left, sems = refs[2 * groups :]
    panels, _, part, _ = out.shape
    block_rows, size = len(bands.rows), bands.size
    take_late(swapped, relayed, diagonal, swapped_left, diagonal_left)

    def copy_out(b):
        lanes = pl.ds(b * size, size)
        return pltpu.make_async_copy(
            held.at[b], out.at[:, :, :, lanes], sems.at[b]
        )

    def finish(i, b, value):
        re, im = leaving(value)
        held[b, :, 0] = re.reshape(panels, part, size)
        held[b, :, 1] = im.reshape(panels, part, size)
        copy_out(b).start()

    late_products(range(block_rows), swapped_left, diagonal_left, bands, sums, finish)
    for b in range(block_rows):
        copy_out(b).wait()


def in_hbm(value):
    return pltpu.with_memory_space_constraint(value, pltpu.HBM)


def params(mib):
    return pltpu.CompilerParams(vmem_limit_bytes=mib * MIB)


def cost(flops, transferred):
    return pl.CostEstimate(flops=flops, bytes_accessed=transferred, transcendentals=0)


def per_device(sources, blocks, block_cols, refl_level, refl_coef):
    lat_count = lax.axis_size("lat")
    panels, _, part, points = sources.shape
    _, block_rows, _, _, size, _ = blocks.shape
    channels = panels * part
    f32, bf16 = jnp.float32, jnp.bfloat16
    axes = ("depth", "lat")
    over_depth = [(0, 1), (1, 0)]
    even = range(0, lat_count - 1, 2)
    uneven = range(1, lat_count - 1, 2)
    alone_even = range(lat_count - lat_count % 2, lat_count)
    alone_uneven = [0] + list(range(lat_count - 1 + lat_count % 2, lat_count))

    def over_lat(firsts, alone):
        pairs = [(d * lat_count + i, d * lat_count + i + 1) for d in range(2) for i in firsts]
        pairs += [(i, lat_count + i) for i in alone]
        return pairs + [(j, i) for i, j in pairs]

    across = over_lat(uneven, alone_uneven)
    beside = over_lat(even, alone_even)
    onward = [(i, i + 2) for i in range(0, lat_count - 2, 2)]
    onward += [(i + 2, i) for i in range(1, lat_count - 2, 2)]
    top = lat_count - 1
    onward += [(top, top - 1) if top % 2 == 0 else (top - 1, top), (1, 0)]
    onward = [(d * lat_count + i, d * lat_count + j) for d in range(2) for i, j in onward]
    half = block_rows // 2
    first_rows, second_rows = range(half), range(half, block_rows)

    def part_shape(rows):
        return jax.ShapeDtypeStruct((2 * channels, len(rows) * size), f32)

    def piece_shape(rows):
        return (4 * channels, len(rows) * size), bf16

    def exchange(first, second):
        first_swapped = lax.ppermute(first, axes, beside)
        second = second()
        second_swapped = lax.ppermute(second, axes, beside)
        second_diagonal = lax.ppermute(second, axes, across)
        relayed = lax.ppermute(first_swapped, axes, onward)
        return second, first_swapped, (second_swapped, relayed, second_diagonal)

    other_blocks = lax.ppermute(blocks, "depth", over_depth)
    other_cols = lax.ppermute(block_cols, "depth", over_depth)
    refl_level = refl_level.reshape(1, points)

    def enter(rows, *tables):
        width = len(rows) * size
        return pl.pallas_call(
            functools.partial(enter_kernel, rows[0] * size, len(tables)),
            out_shape=[
                part_shape(rows),
                jax.ShapeDtypeStruct((2, width), f32),
                *(
                    jax.ShapeDtypeStruct((1, count) + table.shape[2:], table.dtype)
                    for table, count in tables
                ),
            ],
            in_specs=[HBM] * (3 + len(tables)),
            out_specs=[VMEM] * (2 + len(tables)),
            scratch_shapes=[
                pltpu.VMEM((panels, 2, part, width), f32),
                pltpu.VMEM((1, width), jnp.int32),
                pltpu.VMEM((2, width), f32),
                pltpu.VMEM((2, width), f32),
                pltpu.SemaphoreType.DMA((3 + len(tables),)),
            ],
            compiler_params=params(8),
            name="enter",
        )(*map(in_hbm, (sources, refl_level, refl_coef, *(table for table, _ in tables))))

    coefs = []

    def enter_second():
        part_total, coef = enter(second_rows)
        coefs.append(coef)
        return part_total

    near = pl.pallas_call(
        fetch_kernel,
        out_shape=jax.ShapeDtypeStruct((1, half) + blocks.shape[2:], f32),
        in_specs=[HBM],
        out_specs=VMEM,
        scratch_shapes=[pltpu.SemaphoreType.DMA((half,))],
        compiler_params=params(8),
        cost_estimate=cost(0, 2 * blocks.size),
        name="fetch",
    )(in_hbm(blocks))
    first_total, coef, own_cols = enter(first_rows, (block_cols, block_rows))
    coefs.append(coef)
    second_total, early, late = exchange(first_total, enter_second)

    macs = 6 * channels * points * 2 * size

    every_row = range(block_rows)
    row_groups = ((every_row,), (every_row[:1], every_row[1:half], every_row[half:]))

    def prepare(level, rows, fields, halo, ready):
        band = jax.ShapeDtypeStruct((len(rows), 2 * block_rows + 1, size, 2 * size), bf16)
        sums_rows = block_rows if halo else len(rows)
        sums = jax.ShapeDtypeStruct((sums_rows, 2 * channels, 2 * size), f32)
        operands = (*fields, *halo, *(array for arrays in zip(*ready) for array in arrays))
        return pl.pallas_call(
            functools.partial(prepare_kernel, level, rows, len(halo), len(ready)),
            out_shape=[band, band, sums],
            in_specs=[SMEM, SMEM, HBM, VMEM, VMEM] + [VMEM] * len(operands),
            out_specs=[VMEM] * 3,
            scratch_shapes=[
                pltpu.VMEM((len(rows),) + blocks.shape[2:], f32),
                pltpu.VMEM((4 * channels, points), bf16),
                *[pltpu.VMEM(*piece_shape(first_rows))] * len(halo),
                pltpu.SemaphoreType.DMA((len(rows),)),
            ],
            compiler_params=params(16),
            cost_estimate=cost(2 * macs, 4 * blocks.size),
            name="prepare",
        )(own_cols, other_cols, in_hbm(blocks), near, other_blocks, *operands)

    def early_products(level, halo, *fields):
        ready = []
        for n, rows in enumerate(row_groups[level]):
            is_last = n + 1 == len(row_groups[level])
            prepared = prepare(
                level, rows, fields, (halo,) if is_last else (), ready if is_last else []
            )
            ready.append(prepared)
        high, low, parts = zip(*ready)
        return *high, *low, parts[-1]

    bands = early_products(0, early, first_total, second_total)
    first_part, swapped_left, diagonal_left = pl.pallas_call(
        functools.partial(first_rows_kernel, len(row_groups[0]), first_rows),
        out_shape=[
            part_shape(first_rows),
            jax.ShapeDtypeStruct(*piece_shape(second_rows)),
            jax.ShapeDtypeStruct(*piece_shape(every_row)),
        ],
        in_specs=[VMEM] * (4 + len(bands)),
        out_specs=[VMEM] * 3,
        compiler_params=params(12),
        cost_estimate=cost(macs, blocks.size),
        name="first_rows",
    )(*late, *bands, coefs[0])

    def level_second():
        return pl.pallas_call(
            functools.partial(level_rows, len(row_groups[0]), second_rows),
            out_shape=part_shape(second_rows),
            in_specs=[VMEM] * (3 + len(bands)),
            out_specs=VMEM,
            compiler_params=params(12),
            cost_estimate=cost(macs, blocks.size),
            name="second_rows",
        )(swapped_left, diagonal_left, *bands, coefs[1])

    second_part, early, late = exchange(first_part, level_second)
    last_bands = early_products(1, early, first_part, second_part)
    return pl.pallas_call(
        functools.partial(bottom_kernel, len(row_groups[1])),
        out_shape=jax.ShapeDtypeStruct(sources.shape, f32),
        in_specs=[VMEM] * (3 + len(last_bands)),
        out_specs=HBM,
        scratch_shapes=[
            pltpu.VMEM((block_rows, panels, 2, part, size), f32),
            pltpu.VMEM(*piece_shape(second_rows)),
            pltpu.VMEM(*piece_shape(every_row)),
            pltpu.SemaphoreType.DMA((block_rows,)),
        ],
        compiler_params=params(12),
        cost_estimate=cost(macs, blocks.size),
        name="bottom",
    )(*late, *last_bands)


def solution(mesh):
    placed = (
        P("shot", None, "depth", "lat"),
        P(("shot", "depth"), "lat", None, None, None, None),
        P("depth", "lat", None),
        P("lat"),
        P(None, "lat"),
    )
    return jax.shard_map(
        per_device,
        mesh=mesh,
        in_specs=placed,
        out_specs=P("shot", None, "depth", "lat"),
        check_vma=False,
    )
```

```python
import functools

import jax
import jax.numpy as jnp
from jax import lax
from jax.experimental import pallas as pl
from jax.experimental.pallas import tpu as pltpu
from jax.sharding import PartitionSpec as P


VMEM = pl.BlockSpec(memory_space=pltpu.VMEM)
SMEM = pl.BlockSpec(memory_space=pltpu.SMEM)
HBM = pl.BlockSpec(memory_space=pltpu.HBM)
MIB = 1 << 20


def reflected(field_re, field_im, coef_re, coef_im):
    return (
        field_re + coef_re * field_re - coef_im * field_im,
        field_im + coef_re * field_im + coef_im * field_re,
    )


def entered(sources, coef):
    panels = [
        reflected(sources[k, 0], sources[k, 1], coef[0:1, :], coef[1:2, :])
        for k in range(sources.shape[0])
    ]
    return jnp.concatenate([re for re, _ in panels] + [im for _, im in panels], axis=0)


def enter_kernel(first, tables, sources, refl_level, refl_coef, *refs):
    tables_in, (total, next_coef), refs = refs[:tables], refs[tables : tables + 2], refs[tables + 2 :]
    tables_out, (held, level_held, coef_held, coef, sems) = refs[:tables], refs[tables:]
    lanes = pl.ds(first, total.shape[1])
    copies = [
        pltpu.make_async_copy(a, b, sems.at[i])
        for i, (a, b) in enumerate(
            (
                (sources.at[:, :, :, lanes], held),
                (refl_level.at[:, lanes], level_held),
                (refl_coef.at[:, lanes], coef_held),
                *((a.at[:, : b.shape[1]], b) for a, b in zip(tables_in, tables_out)),
            )
        )
    ]
    for copy in copies:
        copy.start()
    for copy in copies:
        copy.wait()
    coef[...] = jnp.where(level_held[...] == 0, coef_held[...], 0.0)
    next_coef[...] = jnp.where(level_held[...] == 1, coef_held[...], 0.0)
    total[...] = entered(held, coef)


def head_and_tail(value):
    head = value.astype(jnp.bfloat16)
    return head, (value - head.astype(jnp.float32)).astype(jnp.bfloat16)


def pieces(value):
    return jnp.concatenate(head_and_tail(value), axis=0)


def product(left, high, low):
    rows = left.shape[0] // 2
    high = high.reshape(high.shape[0] * high.shape[1], high.shape[2])
    low = low.reshape(high.shape)
    both = jnp.dot(left, high, preferred_element_type=jnp.float32)
    cross = jnp.dot(left[:rows], low, preferred_element_type=jnp.float32)
    return both[:rows] + both[rows:] + cross


def prepare_kernel(level, rows, halos, done, own_cols, other_cols, own, near, received, *refs):
    outs = len(refs) - 6 - halos
    high, low, sums, held, left, *early, sems = refs[outs:]
    fields, refs = refs[: outs - halos - 3 * done], refs[outs - halos - 3 * done : outs]
    halo, refs = refs[:halos], refs[halos:]
    parts = refs[2 * done :]
    bands = Bands(done + 1, (*refs[:done], high, *refs[done : 2 * done], low))
    per_row, size = held.shape[1], held.shape[3]
    block_rows = own.shape[1]
    here = lax.axis_index("depth") == level
    first_row = lax.axis_index("lat") * block_rows
    other = jnp.logical_not(here)
    far = [b >= near.shape[1] for b in rows]

    def start(condition, source, i, b):
        @pl.when(condition)
        def _():
            pltpu.make_async_copy(source.at[0, b], held.at[i], sems.at[i]).start()

    for i, b in enumerate(rows):
        if far[i]:
            start(here, own, i, b)

    span = 2 * block_rows + 1
    zeros = jnp.zeros((size, 2 * size), jnp.bfloat16)

    def clear(i, o):
        high[i, o] = zeros
        low[i, o] = zeros

    rows_at, rows_repeated = [], []
    for i, b in enumerate(rows):
        first = first_row + b - block_rows
        at = [
            jnp.where(here, own_cols[0, b, j], other_cols[0, b, j]) - first
            for j in range(per_row)
        ]
        bits = [jnp.left_shift(1, a) for a in at]
        present = functools.reduce(jnp.bitwise_or, bits)
        repeated = sum(bits) != present
        rows_at.append(at)
        rows_repeated.append(repeated)
        start(jnp.logical_and(other, repeated), received, i, b)
        if not far[i]:
            start(jnp.logical_and(here, repeated), near, i, b)
        absent = (1 << span) - 1 - present
        lowest = sum(jnp.where(absent % (2 << o) == 0, 1, 0) for o in range(span - 1))
        highest = sum(jnp.where(absent >= (2 << o), 1, 0) for o in range(span - 1))
        clear(i, lowest)
        clear(i, highest)
        between = repeated if span - per_row == 2 else True

        @pl.when(between)
        def _():
            def clear_one(o, carry):
                @pl.when(jnp.bitwise_and(jnp.right_shift(absent, o), 1) == 1)
                def _():
                    clear(i, o)

                return carry

            lax.fori_loop(lowest + 1, highest, clear_one, 0)

    at_lane = 0
    for field in fields:
        left[:, at_lane : at_lane + field.shape[1]] = pieces(field[...])
        at_lane += field.shape[1]
    finished = block_rows - len(rows) if halos else 0

    def add_early(b, before):
        def run(swapped_before):
            sums[b] = before + side_product(b, 0, early[0], swapped_before, bands)

        by_side(run)

    if halos:
        early[0][...] = pieces(halo[0][...])
        for b, (n, i) in enumerate(bands.rows):
            if n < done:
                add_early(b, parts[n][i])
    for i, b in enumerate(rows):
        at = rows_at[i]
        copied = jnp.logical_or(here, rows_repeated[i]) if far[i] else rows_repeated[i]

        @pl.when(copied)
        def _():
            pltpu.make_async_copy(received.at[0, b], held.at[i], sems.at[i]).wait()

        @pl.when(rows_repeated[i])
        def _():
            for j in reversed(range(1, per_row)):
                target = jnp.int32(per_row)
                for k in range(j):
                    target = jnp.where(at[k] == at[j], k, target)

                @pl.when(target < per_row)
                def _():
                    held[i, target] = held[i, target] + held[i, j]

        def split_from(blocks):
            def split(n, carry):
                part = pl.ds(pl.multiple_of(n * 16, 16), 16)
                for j in reversed(range(per_row)):
                    head, tail = head_and_tail(
                        jnp.concatenate([blocks[j, 0, part], blocks[j, 1, part]], axis=1)
                    )
                    high[i, at[j], part] = head
                    low[i, at[j], part] = tail
                return carry

            lax.fori_loop(0, size // 16, split, 0, unroll=2)

        direct = jnp.logical_not(copied)

        @pl.when(copied)
        def _():
            split_from(held.at[i])

        @pl.when(jnp.logical_and(direct, other))
        def _():
            split_from(received.at[0, b])

        if not far[i]:

            @pl.when(jnp.logical_and(direct, here))
            def _():
                split_from(near.at[0, b])

        band = slice(block_rows - b, 2 * block_rows - b)
        own_product = product(left[...], high[i, band], low[i, band])
        if halos:
            add_early(b, own_product)
        else:
            sums[finished + i] = own_product


class Bands:
    def __init__(self, groups, refs):
        self.high, self.low = refs[:groups], refs[groups : 2 * groups]
        self.rows = [(n, i) for n, ref in enumerate(self.high) for i in range(ref.shape[0])]
        self.size = self.high[0].shape[2]

    def product(self, b, left, band):
        n, i = self.rows[b]
        return product(left, self.high[n][i, band], self.low[n][i, band])


def side_product(b, first, piece, is_before, bands):
    block_rows, size = len(bands.rows), bands.size
    last = first + piece.shape[1] // size
    if is_before:
        low_col, high_col, shift = max(b, first), last, -b
    else:
        low_col, high_col, shift = first, min(b + 1, last), 2 * block_rows - b
    if low_col >= high_col:
        return 0.0
    lanes = slice((low_col - first) * size, (high_col - first) * size)
    band = slice(low_col + shift, high_col + shift)
    return bands.product(b, piece[:, lanes], band)


def by_side(run):
    even = lax.axis_index("lat") % 2 == 0
    pl.when(even)(functools.partial(run, False))
    pl.when(jnp.logical_not(even))(functools.partial(run, True))


def late_products(rows, swapped, diagonal, bands, sums, finish):
    first = (diagonal.shape[1] - swapped.shape[1]) // bands.size

    def run(swapped_before):
        for i, b in enumerate(rows):
            finish(
                i,
                b,
                sums[b]
                + side_product(b, 0, diagonal, not swapped_before, bands)
                + side_product(b, first, swapped, swapped_before, bands),
            )

    by_side(run)


def take_late(swapped, relayed, diagonal, swapped_left, diagonal_left):
    points = relayed.shape[1]
    swapped_left[...] = pieces(swapped[...])
    diagonal_left[:, :points] = pieces(relayed[...])
    diagonal_left[:, points:] = pieces(diagonal[...])


def leaving(value):
    channels, size = value.shape[0] // 2, value.shape[1] // 2
    return (
        value[:channels, :size] - value[channels:, size:],
        value[:channels, size:] + value[channels:, :size],
    )


def level_rows(groups, rows, swapped, diagonal, *refs):
    bands, (sums, next_coef, out) = Bands(groups, refs), refs[2 * groups :]

    def finish(i, b, value):
        re, im = leaving(value)
        channels, size = re.shape
        lanes = slice(i * size, (i + 1) * size)
        re, im = reflected(re, im, next_coef[0:1, lanes], next_coef[1:2, lanes])
        out[:channels, lanes] = re
        out[channels:, lanes] = im

    late_products(rows, swapped, diagonal, bands, sums, finish)


def first_rows_kernel(groups, rows, swapped, relayed, diagonal, *refs):
    operands, (swapped_left, diagonal_left) = refs[:-2], refs[-2:]
    take_late(swapped, relayed, diagonal, swapped_left, diagonal_left)
    level_rows(groups, rows, swapped_left, diagonal_left, *operands)


def bottom_kernel(groups, swapped, relayed, diagonal, *refs):
    bands = Bands(groups, refs)
    sums, out, held, swapped_left, diagonal_left, sems = refs[2 * groups :]
    panels, _, part, _ = out.shape
    block_rows, size = len(bands.rows), bands.size
    take_late(swapped, relayed, diagonal, swapped_left, diagonal_left)

    def copy_out(b):
        lanes = pl.ds(b * size, size)
        return pltpu.make_async_copy(
            held.at[b], out.at[:, :, :, lanes], sems.at[b]
        )

    def finish(i, b, value):
        re, im = leaving(value)
        held[b, :, 0] = re.reshape(panels, part, size)
        held[b, :, 1] = im.reshape(panels, part, size)
        copy_out(b).start()

    late_products(range(block_rows), swapped_left, diagonal_left, bands, sums, finish)
    for b in range(block_rows):
        copy_out(b).wait()


def in_hbm(value):
    return pltpu.with_memory_space_constraint(value, pltpu.HBM)


def params(mib):
    return pltpu.CompilerParams(vmem_limit_bytes=mib * MIB)


def cost(flops, transferred):
    return pl.CostEstimate(flops=flops, bytes_accessed=transferred, transcendentals=0)


def per_device(sources, blocks, block_cols, refl_level, refl_coef):
    lat_count = lax.axis_size("lat")
    panels, _, part, points = sources.shape
    _, block_rows, _, _, size, _ = blocks.shape
    channels = panels * part
    f32, bf16 = jnp.float32, jnp.bfloat16
    axes = ("depth", "lat")
    over_depth = [(0, 1), (1, 0)]
    even = range(0, lat_count - 1, 2)
    uneven = range(1, lat_count - 1, 2)
    alone_even = range(lat_count - lat_count % 2, lat_count)
    alone_uneven = [0] + list(range(lat_count - 1 + lat_count % 2, lat_count))

    def over_lat(firsts, alone):
        pairs = [(d * lat_count + i, d * lat_count + i + 1) for d in range(2) for i in firsts]
        pairs += [(i, lat_count + i) for i in alone]
        return pairs + [(j, i) for i, j in pairs]

    across = over_lat(uneven, alone_uneven)
    beside = over_lat(even, alone_even)
    onward = [(i, i + 2) for i in range(0, lat_count - 2, 2)]
    onward += [(i + 2, i) for i in range(1, lat_count - 2, 2)]
    top = lat_count - 1
    onward += [(top, top - 1) if top % 2 == 0 else (top - 1, top), (1, 0)]
    onward = [(d * lat_count + i, d * lat_count + j) for d in range(2) for i, j in onward]
    half = block_rows // 2
    first_rows, second_rows = range(half), range(half, block_rows)

    def part_shape(rows):
        return jax.ShapeDtypeStruct((2 * channels, len(rows) * size), f32)

    def piece_shape(rows):
        return (4 * channels, len(rows) * size), bf16

    def exchange(first, second):
        first_swapped = lax.ppermute(first, axes, beside)
        second = second()
        second_swapped = lax.ppermute(second, axes, beside)
        second_diagonal = lax.ppermute(second, axes, across)
        relayed = lax.ppermute(first_swapped, axes, onward)
        return second, first_swapped, (second_swapped, relayed, second_diagonal)

    other_blocks = lax.ppermute(blocks, "depth", over_depth)
    other_cols = lax.ppermute(block_cols, "depth", over_depth)
    refl_level = refl_level.reshape(1, points)

    def enter(rows, *tables):
        width = len(rows) * size
        return pl.pallas_call(
            functools.partial(enter_kernel, rows[0] * size, len(tables)),
            out_shape=[
                part_shape(rows),
                jax.ShapeDtypeStruct((2, width), f32),
                *(
                    jax.ShapeDtypeStruct((1, count) + table.shape[2:], table.dtype)
                    for table, count in tables
                ),
            ],
            in_specs=[HBM] * (3 + len(tables)),
            out_specs=[VMEM] * (2 + len(tables)),
            scratch_shapes=[
                pltpu.VMEM((panels, 2, part, width), f32),
                pltpu.VMEM((1, width), jnp.int32),
                pltpu.VMEM((2, width), f32),
                pltpu.VMEM((2, width), f32),
                pltpu.SemaphoreType.DMA((3 + len(tables),)),
            ],
            compiler_params=params(8),
            name="enter",
        )(*map(in_hbm, (sources, refl_level, refl_coef, *(table for table, _ in tables))))

    coefs = []

    def enter_second():
        part_total, coef, near = enter(second_rows, (blocks, 1))
        coefs.extend((coef, near))
        return part_total

    first_total, coef, own_cols = enter(first_rows, (block_cols, block_rows))
    coefs.append(coef)
    second_total, early, late = exchange(first_total, enter_second)

    macs = 6 * channels * points * 2 * size

    every_row = range(block_rows)
    row_groups = ((every_row,), (every_row[:1], every_row[1:]))

    def prepare(level, rows, fields, halo, ready):
        band = jax.ShapeDtypeStruct((len(rows), 2 * block_rows + 1, size, 2 * size), bf16)
        sums_rows = block_rows if halo else len(rows)
        sums = jax.ShapeDtypeStruct((sums_rows, 2 * channels, 2 * size), f32)
        operands = (*fields, *halo, *(array for arrays in zip(*ready) for array in arrays))
        return pl.pallas_call(
            functools.partial(prepare_kernel, level, rows, len(halo), len(ready)),
            out_shape=[band, band, sums],
            in_specs=[SMEM, SMEM, HBM, VMEM, VMEM] + [VMEM] * len(operands),
            out_specs=[VMEM] * 3,
            scratch_shapes=[
                pltpu.VMEM((len(rows),) + blocks.shape[2:], f32),
                pltpu.VMEM((4 * channels, points), bf16),
                *[pltpu.VMEM(*piece_shape(first_rows))] * len(halo),
                pltpu.SemaphoreType.DMA((len(rows),)),
            ],
            compiler_params=params(16),
            cost_estimate=cost(2 * macs, 4 * blocks.size),
            name="prepare",
        )(own_cols, other_cols, in_hbm(blocks), coefs[2], other_blocks, *operands)

    def early_products(level, halo, *fields):
        ready = []
        for n, rows in enumerate(row_groups[level]):
            is_last = n + 1 == len(row_groups[level])
            prepared = prepare(
                level, rows, fields, (halo,) if is_last else (), ready if is_last else []
            )
            ready.append(prepared)
        high, low, parts = zip(*ready)
        return *high, *low, parts[-1]

    bands = early_products(0, early, first_total, second_total)
    first_part, swapped_left, diagonal_left = pl.pallas_call(
        functools.partial(first_rows_kernel, len(row_groups[0]), first_rows),
        out_shape=[
            part_shape(first_rows),
            jax.ShapeDtypeStruct(*piece_shape(second_rows)),
            jax.ShapeDtypeStruct(*piece_shape(every_row)),
        ],
        in_specs=[VMEM] * (4 + len(bands)),
        out_specs=[VMEM] * 3,
        compiler_params=params(12),
        cost_estimate=cost(macs, blocks.size),
        name="first_rows",
    )(*late, *bands, coefs[0])

    def level_second():
        return pl.pallas_call(
            functools.partial(level_rows, len(row_groups[0]), second_rows),
            out_shape=part_shape(second_rows),
            in_specs=[VMEM] * (3 + len(bands)),
            out_specs=VMEM,
            compiler_params=params(12),
            cost_estimate=cost(macs, blocks.size),
            name="second_rows",
        )(swapped_left, diagonal_left, *bands, coefs[1])

    second_part, early, late = exchange(first_part, level_second)
    last_bands = early_products(1, early, first_part, second_part)
    return pl.pallas_call(
        functools.partial(bottom_kernel, len(row_groups[1])),
        out_shape=jax.ShapeDtypeStruct(sources.shape, f32),
        in_specs=[VMEM] * (3 + len(last_bands)),
        out_specs=HBM,
        scratch_shapes=[
            pltpu.VMEM((block_rows, panels, 2, part, size), f32),
            pltpu.VMEM(*piece_shape(second_rows)),
            pltpu.VMEM(*piece_shape(every_row)),
            pltpu.SemaphoreType.DMA((block_rows,)),
        ],
        compiler_params=params(12),
        cost_estimate=cost(macs, blocks.size),
        name="bottom",
    )(*late, *last_bands)


def solution(mesh):
    placed = (
        P("shot", None, "depth", "lat"),
        P(("shot", "depth"), "lat", None, None, None, None),
        P("depth", "lat", None),
        P("lat"),
        P(None, "lat"),
    )
    return jax.shard_map(
        per_device,
        mesh=mesh,
        in_specs=placed,
        out_specs=P("shot", None, "depth", "lat"),
        check_vma=False,
    )
```

```python
import functools

import jax
import jax.numpy as jnp
from jax import lax
from jax.experimental import pallas as pl
from jax.experimental.pallas import tpu as pltpu
from jax.sharding import PartitionSpec as P


VMEM = pl.BlockSpec(memory_space=pltpu.VMEM)
SMEM = pl.BlockSpec(memory_space=pltpu.SMEM)
HBM = pl.BlockSpec(memory_space=pltpu.HBM)
MIB = 1 << 20


def reflected(field_re, field_im, coef_re, coef_im):
    return (
        field_re + coef_re * field_re - coef_im * field_im,
        field_im + coef_re * field_im + coef_im * field_re,
    )


def entered(sources, coef):
    panels = [
        reflected(sources[k, 0], sources[k, 1], coef[0:1, :], coef[1:2, :])
        for k in range(sources.shape[0])
    ]
    return jnp.concatenate([re for re, _ in panels] + [im for _, im in panels], axis=0)


def enter_kernel(first, tables, sources, refl_level, refl_coef, *refs):
    tables_in, (total, next_coef), refs = refs[:tables], refs[tables : tables + 2], refs[tables + 2 :]
    tables_out, (held, level_held, coef_held, coef, sems) = refs[:tables], refs[tables:]
    lanes = pl.ds(first, total.shape[1])
    copies = [
        pltpu.make_async_copy(a, b, sems.at[i])
        for i, (a, b) in enumerate(
            (
                (sources.at[:, :, :, lanes], held),
                (refl_level.at[:, lanes], level_held),
                (refl_coef.at[:, lanes], coef_held),
                *((a.at[:, : b.shape[1]], b) for a, b in zip(tables_in, tables_out)),
            )
        )
    ]
    for copy in copies:
        copy.start()
    for copy in copies:
        copy.wait()
    coef[...] = jnp.where(level_held[...] == 0, coef_held[...], 0.0)
    next_coef[...] = jnp.where(level_held[...] == 1, coef_held[...], 0.0)
    total[...] = entered(held, coef)


def head_and_tail(value):
    head = value.astype(jnp.bfloat16)
    return head, (value - head.astype(jnp.float32)).astype(jnp.bfloat16)


def pieces(value):
    return jnp.concatenate(head_and_tail(value), axis=0)


def product(left, high, low):
    rows = left.shape[0] // 2
    high = high.reshape(high.shape[0] * high.shape[1], high.shape[2])
    low = low.reshape(high.shape)
    both = jnp.dot(left, high, preferred_element_type=jnp.float32)
    cross = jnp.dot(left[:rows], low, preferred_element_type=jnp.float32)
    return both[:rows] + both[rows:] + cross


def prepare_kernel(level, rows, halos, done, own_cols, other_cols, own, near, received, *refs):
    outs = len(refs) - 6 - halos
    high, low, sums, held, left, *early, sems = refs[outs:]
    fields, refs = refs[: outs - halos - 3 * done], refs[outs - halos - 3 * done : outs]
    halo, refs = refs[:halos], refs[halos:]
    parts = refs[2 * done :]
    bands = Bands(done + 1, (*refs[:done], high, *refs[done : 2 * done], low))
    per_row, size = held.shape[1], held.shape[3]
    block_rows = own.shape[1]
    here = lax.axis_index("depth") == level
    first_row = lax.axis_index("lat") * block_rows
    other = jnp.logical_not(here)
    far = [b >= near.shape[1] for b in rows]

    def start(condition, source, i, b):
        @pl.when(condition)
        def _():
            pltpu.make_async_copy(source.at[0, b], held.at[i], sems.at[i]).start()

    for i, b in enumerate(rows):
        if far[i]:
            start(here, own, i, b)

    span = 2 * block_rows + 1
    zeros = jnp.zeros((size, 2 * size), jnp.bfloat16)

    def clear(i, o):
        high[i, o] = zeros
        low[i, o] = zeros

    rows_at, rows_repeated = [], []
    for i, b in enumerate(rows):
        first = first_row + b - block_rows
        at = [
            jnp.where(here, own_cols[0, b, j], other_cols[0, b, j]) - first
            for j in range(per_row)
        ]
        bits = [jnp.left_shift(1, a) for a in at]
        present = functools.reduce(jnp.bitwise_or, bits)
        repeated = sum(bits) != present
        rows_at.append(at)
        rows_repeated.append(repeated)
        absent = (1 << span) - 1 - present
        lowest = sum(jnp.where(absent % (2 << o) == 0, 1, 0) for o in range(span - 1))
        highest = sum(jnp.where(absent >= (2 << o), 1, 0) for o in range(span - 1))
        clear(i, lowest)
        clear(i, highest)
        between = repeated if span - per_row == 2 else True

        @pl.when(between)
        def _():
            def clear_one(o, carry):
                @pl.when(jnp.bitwise_and(jnp.right_shift(absent, o), 1) == 1)
                def _():
                    clear(i, o)

                return carry

            lax.fori_loop(lowest + 1, highest, clear_one, 0)

    at_lane = 0
    for field in fields:
        left[:, at_lane : at_lane + field.shape[1]] = pieces(field[...])
        at_lane += field.shape[1]
    for i, b in enumerate(rows):
        at = rows_at[i]
        repeats = [
            functools.reduce(jnp.logical_or, [a == at[j] for a in at[j + 1 :]])
            for j in range(per_row - 1)
        ]

        def merge(blocks):
            for j in reversed(range(1, per_row)):
                target = jnp.int32(per_row)
                for k in range(j):
                    target = jnp.where(at[k] == at[j], k, target)
                found = target < per_row
                again = repeats[j] if j < per_row - 1 else False

                @pl.when(jnp.logical_and(found, again))
                def _():
                    held[i, target] = blocks[target] + held[i, j]

                @pl.when(jnp.logical_and(found, jnp.logical_not(again)))
                def _():
                    held[i, target] = blocks[target] + blocks[j]

        def split_from(blocks, entries):
            def split(n, carry):
                part = pl.ds(pl.multiple_of(n * 16, 16), 16)
                for j in entries:
                    head, tail = head_and_tail(
                        jnp.concatenate([blocks[j, 0, part], blocks[j, 1, part]], axis=1)
                    )
                    high[i, at[j], part] = head
                    low[i, at[j], part] = tail
                return carry

            lax.fori_loop(0, size // 16, split, 0, unroll=2)

        def take_row(blocks):
            split_from(blocks, range(per_row)[::-1])

            @pl.when(rows_repeated[i])
            def _():
                merge(blocks)
                for j in reversed(range(per_row - 1)):

                    @pl.when(repeats[j])
                    def _():
                        split_from(held.at[i], (j,))

        @pl.when(here)
        def _():
            if far[i]:
                pltpu.make_async_copy(own.at[0, b], held.at[i], sems.at[i]).wait()
                pl.when(rows_repeated[i])(functools.partial(merge, held.at[i]))
                split_from(held.at[i], range(per_row)[::-1])
            else:
                take_row(near.at[0, b])

        @pl.when(other)
        def _():
            take_row(received.at[0, b])

    finished = block_rows - len(rows) if halos else 0
    for i, b in enumerate(rows):
        band = slice(block_rows - b, 2 * block_rows - b)
        sums[finished + i] = product(left[...], high[i, band], low[i, band])
    if halos:
        early[0][...] = pieces(halo[0][...])

        def run(swapped_before):
            for b, (n, i) in enumerate(bands.rows):
                before = parts[n][i] if n < done else sums[b]
                sums[b] = before + side_product(b, 0, early[0], swapped_before, bands)

        by_side(run)


class Bands:
    def __init__(self, groups, refs):
        self.high, self.low = refs[:groups], refs[groups : 2 * groups]
        self.rows = [(n, i) for n, ref in enumerate(self.high) for i in range(ref.shape[0])]
        self.size = self.high[0].shape[2]

    def product(self, b, left, band):
        n, i = self.rows[b]
        return product(left, self.high[n][i, band], self.low[n][i, band])


def side_product(b, first, piece, is_before, bands):
    block_rows, size = len(bands.rows), bands.size
    last = first + piece.shape[1] // size
    if is_before:
        low_col, high_col, shift = max(b, first), last, -b
    else:
        low_col, high_col, shift = first, min(b + 1, last), 2 * block_rows - b
    if low_col >= high_col:
        return 0.0
    lanes = slice((low_col - first) * size, (high_col - first) * size)
    band = slice(low_col + shift, high_col + shift)
    return bands.product(b, piece[:, lanes], band)


def by_side(run):
    even = lax.axis_index("lat") % 2 == 0
    pl.when(even)(functools.partial(run, False))
    pl.when(jnp.logical_not(even))(functools.partial(run, True))


def late_products(rows, swapped, diagonal, bands, sums, finish):
    first = (diagonal.shape[1] - swapped.shape[1]) // bands.size

    def run(swapped_before):
        for i, b in enumerate(rows):
            finish(
                i,
                b,
                sums[b]
                + side_product(b, 0, diagonal, not swapped_before, bands)
                + side_product(b, first, swapped, swapped_before, bands),
            )

    by_side(run)


def take_late(swapped, relayed, diagonal, swapped_left, diagonal_left):
    points = relayed.shape[1]
    swapped_left[...] = pieces(swapped[...])
    diagonal_left[:, :points] = pieces(relayed[...])
    diagonal_left[:, points:] = pieces(diagonal[...])


def leaving(value):
    channels, size = value.shape[0] // 2, value.shape[1] // 2
    return (
        value[:channels, :size] - value[channels:, size:],
        value[:channels, size:] + value[channels:, :size],
    )


def level_rows(groups, rows, swapped, diagonal, *refs):
    bands, (sums, next_coef, out) = Bands(groups, refs), refs[2 * groups :]

    def finish(i, b, value):
        re, im = leaving(value)
        channels, size = re.shape
        lanes = slice(i * size, (i + 1) * size)
        re, im = reflected(re, im, next_coef[0:1, lanes], next_coef[1:2, lanes])
        out[:channels, lanes] = re
        out[channels:, lanes] = im

    late_products(rows, swapped, diagonal, bands, sums, finish)


def first_rows_kernel(groups, rows, swapped, relayed, diagonal, *refs):
    operands, (swapped_left, diagonal_left) = refs[:-2], refs[-2:]
    take_late(swapped, relayed, diagonal, swapped_left, diagonal_left)
    level_rows(groups, rows, swapped_left, diagonal_left, *operands)


def bottom_kernel(groups, swapped, relayed, diagonal, *refs):
    bands = Bands(groups, refs)
    sums, out, held, swapped_left, diagonal_left, sems = refs[2 * groups :]
    panels, _, part, _ = out.shape
    block_rows, size = len(bands.rows), bands.size
    take_late(swapped, relayed, diagonal, swapped_left, diagonal_left)

    def copy_out(b):
        lanes = pl.ds(b * size, size)
        return pltpu.make_async_copy(
            held.at[b], out.at[:, :, :, lanes], sems.at[b]
        )

    def finish(i, b, value):
        re, im = leaving(value)
        held[b, :, 0] = re.reshape(panels, part, size)
        held[b, :, 1] = im.reshape(panels, part, size)
        copy_out(b).start()

    late_products(range(block_rows), swapped_left, diagonal_left, bands, sums, finish)
    for b in range(block_rows):
        copy_out(b).wait()


def in_hbm(value):
    return pltpu.with_memory_space_constraint(value, pltpu.HBM)


def params(mib):
    return pltpu.CompilerParams(vmem_limit_bytes=mib * MIB)


def cost(flops, transferred):
    return pl.CostEstimate(flops=flops, bytes_accessed=transferred, transcendentals=0)


def per_device(sources, blocks, block_cols, refl_level, refl_coef):
    lat_count = lax.axis_size("lat")
    panels, _, part, points = sources.shape
    _, block_rows, _, _, size, _ = blocks.shape
    channels = panels * part
    f32, bf16 = jnp.float32, jnp.bfloat16
    axes = ("depth", "lat")
    over_depth = [(0, 1), (1, 0)]
    even = range(0, lat_count - 1, 2)
    uneven = range(1, lat_count - 1, 2)
    alone_even = range(lat_count - lat_count % 2, lat_count)
    alone_uneven = [0] + list(range(lat_count - 1 + lat_count % 2, lat_count))

    def over_lat(firsts, alone):
        pairs = [(d * lat_count + i, d * lat_count + i + 1) for d in range(2) for i in firsts]
        pairs += [(i, lat_count + i) for i in alone]
        return pairs + [(j, i) for i, j in pairs]

    across = over_lat(uneven, alone_uneven)
    beside = over_lat(even, alone_even)
    onward = [(i, i + 2) for i in range(0, lat_count - 2, 2)]
    onward += [(i + 2, i) for i in range(1, lat_count - 2, 2)]
    top = lat_count - 1
    onward += [(top, top - 1) if top % 2 == 0 else (top - 1, top), (1, 0)]
    onward = [(d * lat_count + i, d * lat_count + j) for d in range(2) for i, j in onward]
    half = block_rows // 2
    first_rows, second_rows = range(half), range(half, block_rows)

    def part_shape(rows):
        return jax.ShapeDtypeStruct((2 * channels, len(rows) * size), f32)

    def piece_shape(rows):
        return (4 * channels, len(rows) * size), bf16

    def exchange(first, second):
        first_swapped = lax.ppermute(first, axes, beside)
        second = second()
        second_swapped = lax.ppermute(second, axes, beside)
        second_diagonal = lax.ppermute(second, axes, across)
        relayed = lax.ppermute(first_swapped, axes, onward)
        return second, first_swapped, (second_swapped, relayed, second_diagonal)

    other_blocks = lax.ppermute(blocks, "depth", over_depth)
    other_cols = lax.ppermute(block_cols, "depth", over_depth)
    refl_level = refl_level.reshape(1, points)

    def enter(rows, *tables):
        width = len(rows) * size
        return pl.pallas_call(
            functools.partial(enter_kernel, rows[0] * size, len(tables)),
            out_shape=[
                part_shape(rows),
                jax.ShapeDtypeStruct((2, width), f32),
                *(
                    jax.ShapeDtypeStruct((1, count) + table.shape[2:], table.dtype)
                    for table, count in tables
                ),
            ],
            in_specs=[HBM] * (3 + len(tables)),
            out_specs=[VMEM] * (2 + len(tables)),
            scratch_shapes=[
                pltpu.VMEM((panels, 2, part, width), f32),
                pltpu.VMEM((1, width), jnp.int32),
                pltpu.VMEM((2, width), f32),
                pltpu.VMEM((2, width), f32),
                pltpu.SemaphoreType.DMA((3 + len(tables),)),
            ],
            compiler_params=params(8),
            name="enter",
        )(*map(in_hbm, (sources, refl_level, refl_coef, *(table for table, _ in tables))))

    coefs = []

    def enter_second():
        part_total, coef, near = enter(second_rows, (blocks, 1))
        coefs.extend((coef, near))
        return part_total

    first_total, coef, own_cols = enter(first_rows, (block_cols, block_rows))
    coefs.append(coef)
    second_total, early, late = exchange(first_total, enter_second)

    macs = 6 * channels * points * 2 * size

    every_row = range(block_rows)
    row_groups = ((every_row,), (every_row[:1], every_row[1:]))

    def prepare(level, rows, fields, halo, ready):
        band = jax.ShapeDtypeStruct((len(rows), 2 * block_rows + 1, size, 2 * size), bf16)
        sums_rows = block_rows if halo else len(rows)
        sums = jax.ShapeDtypeStruct((sums_rows, 2 * channels, 2 * size), f32)
        operands = (*fields, *halo, *(array for arrays in zip(*ready) for array in arrays))
        return pl.pallas_call(
            functools.partial(prepare_kernel, level, rows, len(halo), len(ready)),
            out_shape=[band, band, sums],
            in_specs=[SMEM, SMEM, HBM, VMEM, VMEM] + [VMEM] * len(operands),
            out_specs=[VMEM] * 3,
            scratch_shapes=[
                pltpu.VMEM((len(rows),) + blocks.shape[2:], f32),
                pltpu.VMEM((4 * channels, points), bf16),
                *[pltpu.VMEM(*piece_shape(first_rows))] * len(halo),
                pltpu.SemaphoreType.DMA((len(rows),)),
            ],
            compiler_params=params(16),
            cost_estimate=cost(2 * macs, 4 * blocks.size),
            name="prepare",
        )(own_cols, other_cols, in_hbm(blocks), coefs[2], other_blocks, *operands)

    def early_products(level, halo, *fields):
        ready = []
        for n, rows in enumerate(row_groups[level]):
            is_last = n + 1 == len(row_groups[level])
            prepared = prepare(
                level, rows, fields, (halo,) if is_last else (), ready if is_last else []
            )
            ready.append(prepared)
        high, low, parts = zip(*ready)
        return *high, *low, parts[-1]

    bands = early_products(0, early, first_total, second_total)
    first_part, swapped_left, diagonal_left = pl.pallas_call(
        functools.partial(first_rows_kernel, len(row_groups[0]), first_rows),
        out_shape=[
            part_shape(first_rows),
            jax.ShapeDtypeStruct(*piece_shape(second_rows)),
            jax.ShapeDtypeStruct(*piece_shape(every_row)),
        ],
        in_specs=[VMEM] * (4 + len(bands)),
        out_specs=[VMEM] * 3,
        compiler_params=params(12),
        cost_estimate=cost(macs, blocks.size),
        name="first_rows",
    )(*late, *bands, coefs[0])

    def level_second():
        return pl.pallas_call(
            functools.partial(level_rows, len(row_groups[0]), second_rows),
            out_shape=part_shape(second_rows),
            in_specs=[VMEM] * (3 + len(bands)),
            out_specs=VMEM,
            compiler_params=params(12),
            cost_estimate=cost(macs, blocks.size),
            name="second_rows",
        )(swapped_left, diagonal_left, *bands, coefs[1])

    second_part, early, late = exchange(first_part, level_second)
    last_bands = early_products(1, early, first_part, second_part)
    return pl.pallas_call(
        functools.partial(bottom_kernel, len(row_groups[1])),
        out_shape=jax.ShapeDtypeStruct(sources.shape, f32),
        in_specs=[VMEM] * (3 + len(last_bands)),
        out_specs=HBM,
        scratch_shapes=[
            pltpu.VMEM((block_rows, panels, 2, part, size), f32),
            pltpu.VMEM(*piece_shape(second_rows)),
            pltpu.VMEM(*piece_shape(every_row)),
            pltpu.SemaphoreType.DMA((block_rows,)),
        ],
        compiler_params=params(12),
        cost_estimate=cost(macs, blocks.size),
        name="bottom",
    )(*late, *last_bands)


def solution(mesh):
    placed = (
        P("shot", None, "depth", "lat"),
        P(("shot", "depth"), "lat", None, None, None, None),
        P("depth", "lat", None),
        P("lat"),
        P(None, "lat"),
    )
    return jax.shard_map(
        per_device,
        mesh=mesh,
        in_specs=placed,
        out_specs=P("shot", None, "depth", "lat"),
        check_vma=False,
    )
```

```python
import functools

import jax
import jax.numpy as jnp
from jax import lax
from jax.experimental import pallas as pl
from jax.experimental.pallas import tpu as pltpu
from jax.sharding import PartitionSpec as P


VMEM = pl.BlockSpec(memory_space=pltpu.VMEM)
SMEM = pl.BlockSpec(memory_space=pltpu.SMEM)
HBM = pl.BlockSpec(memory_space=pltpu.HBM)
MIB = 1 << 20


def reflected(field_re, field_im, coef_re, coef_im):
    return (
        field_re + coef_re * field_re - coef_im * field_im,
        field_im + coef_re * field_im + coef_im * field_re,
    )


def entered(sources, coef):
    panels = [
        reflected(sources[k, 0], sources[k, 1], coef[0:1, :], coef[1:2, :])
        for k in range(sources.shape[0])
    ]
    return jnp.concatenate([re for re, _ in panels] + [im for _, im in panels], axis=0)


def enter_kernel(first, tables, sources, refl_level, refl_coef, *refs):
    tables_in, (total, next_coef), refs = refs[:tables], refs[tables : tables + 2], refs[tables + 2 :]
    tables_out, (held, level_held, coef_held, coef, sems) = refs[:tables], refs[tables:]
    lanes = pl.ds(first, total.shape[1])
    copies = [
        pltpu.make_async_copy(a, b, sems.at[i])
        for i, (a, b) in enumerate(
            (
                (sources.at[:, :, :, lanes], held),
                (refl_level.at[:, lanes], level_held),
                (refl_coef.at[:, lanes], coef_held),
                *((a.at[:, : b.shape[1]], b) for a, b in zip(tables_in, tables_out)),
            )
        )
    ]
    for copy in copies:
        copy.start()
    for copy in copies:
        copy.wait()
    coef[...] = jnp.where(level_held[...] == 0, coef_held[...], 0.0)
    next_coef[...] = jnp.where(level_held[...] == 1, coef_held[...], 0.0)
    total[...] = entered(held, coef)


def head_and_tail(value):
    head = value.astype(jnp.bfloat16)
    return head, (value - head.astype(jnp.float32)).astype(jnp.bfloat16)


def pieces(value):
    return jnp.concatenate(head_and_tail(value), axis=0)


def product(left, high, low):
    rows = left.shape[0] // 2
    high = high.reshape(high.shape[0] * high.shape[1], high.shape[2])
    low = low.reshape(high.shape)
    both = jnp.dot(left, high, preferred_element_type=jnp.float32)
    cross = jnp.dot(left[:rows], low, preferred_element_type=jnp.float32)
    return both[:rows] + both[rows:] + cross


def prepare_kernel(level, rows, halos, done, own_cols, other_cols, own, near, received, *refs):
    outs = len(refs) - 6 - halos
    high, low, sums, held, left, *early, sems = refs[outs:]
    fields, refs = refs[: outs - halos - 3 * done], refs[outs - halos - 3 * done : outs]
    halo, refs = refs[:halos], refs[halos:]
    parts = refs[2 * done :]
    bands = Bands(done + 1, (*refs[:done], high, *refs[done : 2 * done], low))
    per_row, size = held.shape[1], held.shape[3]
    block_rows = own.shape[1]
    here = lax.axis_index("depth") == level
    first_row = lax.axis_index("lat") * block_rows
    other = jnp.logical_not(here)
    far = [b >= near.shape[1] for b in rows]

    def start(condition, source, i, b):
        @pl.when(condition)
        def _():
            pltpu.make_async_copy(source.at[0, b], held.at[i], sems.at[i]).start()

    for i, b in enumerate(rows):
        if far[i]:
            start(here, own, i, b)

    span = 2 * block_rows + 1
    zeros = jnp.zeros((size, 2 * size), jnp.bfloat16)

    def clear(i, o):
        high[i, o] = zeros
        low[i, o] = zeros

    rows_at, rows_repeated = [], []
    for i, b in enumerate(rows):
        first = first_row + b - block_rows
        at = [
            jnp.where(here, own_cols[0, b, j], other_cols[0, b, j]) - first
            for j in range(per_row)
        ]
        bits = [jnp.left_shift(1, a) for a in at]
        present = functools.reduce(jnp.bitwise_or, bits)
        repeated = sum(bits) != present
        rows_at.append(at)
        rows_repeated.append(repeated)
        start(jnp.logical_and(other, repeated), received, i, b)
        if not far[i]:
            start(jnp.logical_and(here, repeated), near, i, b)
        absent = (1 << span) - 1 - present
        lowest = sum(jnp.where(absent % (2 << o) == 0, 1, 0) for o in range(span - 1))
        highest = sum(jnp.where(absent >= (2 << o), 1, 0) for o in range(span - 1))
        clear(i, lowest)
        clear(i, highest)
        between = repeated if span - per_row == 2 else True

        @pl.when(between)
        def _():
            def clear_one(o, carry):
                @pl.when(jnp.bitwise_and(jnp.right_shift(absent, o), 1) == 1)
                def _():
                    clear(i, o)

                return carry

            lax.fori_loop(lowest + 1, highest, clear_one, 0)

    at_lane = 0
    for field in fields:
        left[:, at_lane : at_lane + field.shape[1]] = pieces(field[...])
        at_lane += field.shape[1]
    for i, b in enumerate(rows):
        at = rows_at[i]
        copied = jnp.logical_or(here, rows_repeated[i]) if far[i] else rows_repeated[i]

        @pl.when(copied)
        def _():
            pltpu.make_async_copy(received.at[0, b], held.at[i], sems.at[i]).wait()

        @pl.when(rows_repeated[i])
        def _():
            for j in reversed(range(1, per_row)):
                target = jnp.int32(per_row)
                for k in range(j):
                    target = jnp.where(at[k] == at[j], k, target)

                @pl.when(target < per_row)
                def _():
                    held[i, target] = held[i, target] + held[i, j]

        def split_from(blocks):
            def split(n, carry):
                part = pl.ds(pl.multiple_of(n * 16, 16), 16)
                for j in reversed(range(per_row)):
                    head, tail = head_and_tail(
                        jnp.concatenate([blocks[j, 0, part], blocks[j, 1, part]], axis=1)
                    )
                    high[i, at[j], part] = head
                    low[i, at[j], part] = tail
                return carry

            lax.fori_loop(0, size // 16, split, 0, unroll=4)

        direct = jnp.logical_not(copied)

        @pl.when(copied)
        def _():
            split_from(held.at[i])

        @pl.when(jnp.logical_and(direct, other))
        def _():
            split_from(received.at[0, b])

        if not far[i]:

            @pl.when(jnp.logical_and(direct, here))
            def _():
                split_from(near.at[0, b])

    finished = block_rows - len(rows) if halos else 0
    for i, b in enumerate(rows):
        band = slice(block_rows - b, 2 * block_rows - b)
        sums[finished + i] = product(left[...], high[i, band], low[i, band])
    if halos:
        early[0][...] = pieces(halo[0][...])

        def run(swapped_before):
            for b, (n, i) in enumerate(bands.rows):
                before = parts[n][i] if n < done else sums[b]
                sums[b] = before + side_product(b, 0, early[0], swapped_before, bands)

        by_side(run)


class Bands:
    def __init__(self, groups, refs):
        self.high, self.low = refs[:groups], refs[groups : 2 * groups]
        self.rows = [(n, i) for n, ref in enumerate(self.high) for i in range(ref.shape[0])]
        self.size = self.high[0].shape[2]

    def product(self, b, left, band):
        n, i = self.rows[b]
        return product(left, self.high[n][i, band], self.low[n][i, band])


def side_product(b, first, piece, is_before, bands):
    block_rows, size = len(bands.rows), bands.size
    last = first + piece.shape[1] // size
    if is_before:
        low_col, high_col, shift = max(b, first), last, -b
    else:
        low_col, high_col, shift = first, min(b + 1, last), 2 * block_rows - b
    if low_col >= high_col:
        return 0.0
    lanes = slice((low_col - first) * size, (high_col - first) * size)
    band = slice(low_col + shift, high_col + shift)
    return bands.product(b, piece[:, lanes], band)


def by_side(run):
    even = lax.axis_index("lat") % 2 == 0
    pl.when(even)(functools.partial(run, False))
    pl.when(jnp.logical_not(even))(functools.partial(run, True))


def late_products(rows, swapped, diagonal, bands, sums, finish):
    first = (diagonal.shape[1] - swapped.shape[1]) // bands.size

    def run(swapped_before):
        for i, b in enumerate(rows):
            finish(
                i,
                b,
                sums[b]
                + side_product(b, 0, diagonal, not swapped_before, bands)
                + side_product(b, first, swapped, swapped_before, bands),
            )

    by_side(run)


def take_late(swapped, relayed, diagonal, swapped_left, diagonal_left):
    points = relayed.shape[1]
    swapped_left[...] = pieces(swapped[...])
    diagonal_left[:, :points] = pieces(relayed[...])
    diagonal_left[:, points:] = pieces(diagonal[...])


def leaving(value):
    channels, size = value.shape[0] // 2, value.shape[1] // 2
    return (
        value[:channels, :size] - value[channels:, size:],
        value[:channels, size:] + value[channels:, :size],
    )


def level_rows(groups, rows, swapped, diagonal, *refs):
    bands, (sums, next_coef, out) = Bands(groups, refs), refs[2 * groups :]

    def finish(i, b, value):
        re, im = leaving(value)
        channels, size = re.shape
        lanes = slice(i * size, (i + 1) * size)
        re, im = reflected(re, im, next_coef[0:1, lanes], next_coef[1:2, lanes])
        out[:channels, lanes] = re
        out[channels:, lanes] = im

    late_products(rows, swapped, diagonal, bands, sums, finish)


def first_rows_kernel(groups, rows, swapped, relayed, diagonal, *refs):
    operands, (swapped_left, diagonal_left) = refs[:-2], refs[-2:]
    take_late(swapped, relayed, diagonal, swapped_left, diagonal_left)
    level_rows(groups, rows, swapped_left, diagonal_left, *operands)


def bottom_kernel(groups, swapped, relayed, diagonal, *refs):
    bands = Bands(groups, refs)
    sums, out, held, swapped_left, diagonal_left, sems = refs[2 * groups :]
    panels, _, part, _ = out.shape
    block_rows, size = len(bands.rows), bands.size
    take_late(swapped, relayed, diagonal, swapped_left, diagonal_left)

    def copy_out(b):
        lanes = pl.ds(b * size, size)
        return pltpu.make_async_copy(
            held.at[b], out.at[:, :, :, lanes], sems.at[b]
        )

    def finish(i, b, value):
        re, im = leaving(value)
        held[b, :, 0] = re.reshape(panels, part, size)
        held[b, :, 1] = im.reshape(panels, part, size)
        copy_out(b).start()

    late_products(range(block_rows), swapped_left, diagonal_left, bands, sums, finish)
    for b in range(block_rows):
        copy_out(b).wait()


def in_hbm(value):
    return pltpu.with_memory_space_constraint(value, pltpu.HBM)


def params(mib):
    return pltpu.CompilerParams(vmem_limit_bytes=mib * MIB)


def cost(flops, transferred):
    return pl.CostEstimate(flops=flops, bytes_accessed=transferred, transcendentals=0)


def per_device(sources, blocks, block_cols, refl_level, refl_coef):
    lat_count = lax.axis_size("lat")
    panels, _, part, points = sources.shape
    _, block_rows, _, _, size, _ = blocks.shape
    channels = panels * part
    f32, bf16 = jnp.float32, jnp.bfloat16
    axes = ("depth", "lat")
    over_depth = [(0, 1), (1, 0)]
    even = range(0, lat_count - 1, 2)
    uneven = range(1, lat_count - 1, 2)
    alone_even = range(lat_count - lat_count % 2, lat_count)
    alone_uneven = [0] + list(range(lat_count - 1 + lat_count % 2, lat_count))

    def over_lat(firsts, alone):
        pairs = [(d * lat_count + i, d * lat_count + i + 1) for d in range(2) for i in firsts]
        pairs += [(i, lat_count + i) for i in alone]
        return pairs + [(j, i) for i, j in pairs]

    across = over_lat(uneven, alone_uneven)
    beside = over_lat(even, alone_even)
    onward = [(i, i + 2) for i in range(0, lat_count - 2, 2)]
    onward += [(i + 2, i) for i in range(1, lat_count - 2, 2)]
    top = lat_count - 1
    onward += [(top, top - 1) if top % 2 == 0 else (top - 1, top), (1, 0)]
    onward = [(d * lat_count + i, d * lat_count + j) for d in range(2) for i, j in onward]
    half = block_rows // 2
    first_rows, second_rows = range(half), range(half, block_rows)

    def part_shape(rows):
        return jax.ShapeDtypeStruct((2 * channels, len(rows) * size), f32)

    def piece_shape(rows):
        return (4 * channels, len(rows) * size), bf16

    def exchange(first, second):
        first_swapped = lax.ppermute(first, axes, beside)
        second = second()
        second_swapped = lax.ppermute(second, axes, beside)
        second_diagonal = lax.ppermute(second, axes, across)
        relayed = lax.ppermute(first_swapped, axes, onward)
        return second, first_swapped, (second_swapped, relayed, second_diagonal)

    other_blocks = lax.ppermute(blocks, "depth", over_depth)
    other_cols = lax.ppermute(block_cols, "depth", over_depth)
    refl_level = refl_level.reshape(1, points)

    def enter(rows, *tables):
        width = len(rows) * size
        return pl.pallas_call(
            functools.partial(enter_kernel, rows[0] * size, len(tables)),
            out_shape=[
                part_shape(rows),
                jax.ShapeDtypeStruct((2, width), f32),
                *(
                    jax.ShapeDtypeStruct((1, count) + table.shape[2:], table.dtype)
                    for table, count in tables
                ),
            ],
            in_specs=[HBM] * (3 + len(tables)),
            out_specs=[VMEM] * (2 + len(tables)),
            scratch_shapes=[
                pltpu.VMEM((panels, 2, part, width), f32),
                pltpu.VMEM((1, width), jnp.int32),
                pltpu.VMEM((2, width), f32),
                pltpu.VMEM((2, width), f32),
                pltpu.SemaphoreType.DMA((3 + len(tables),)),
            ],
            compiler_params=params(8),
            name="enter",
        )(*map(in_hbm, (sources, refl_level, refl_coef, *(table for table, _ in tables))))

    coefs = []

    def enter_second():
        part_total, coef, near = enter(second_rows, (blocks, half))
        coefs.extend((coef, near))
        return part_total

    first_total, coef, own_cols = enter(first_rows, (block_cols, block_rows))
    coefs.append(coef)
    second_total, early, late = exchange(first_total, enter_second)

    macs = 6 * channels * points * 2 * size

    every_row = range(block_rows)
    row_groups = ((every_row,), (every_row[:1], every_row[1:]))

    def prepare(level, rows, fields, halo, ready):
        band = jax.ShapeDtypeStruct((len(rows), 2 * block_rows + 1, size, 2 * size), bf16)
        sums_rows = block_rows if halo else len(rows)
        sums = jax.ShapeDtypeStruct((sums_rows, 2 * channels, 2 * size), f32)
        operands = (*fields, *halo, *(array for arrays in zip(*ready) for array in arrays))
        return pl.pallas_call(
            functools.partial(prepare_kernel, level, rows, len(halo), len(ready)),
            out_shape=[band, band, sums],
            in_specs=[SMEM, SMEM, HBM, VMEM, VMEM] + [VMEM] * len(operands),
            out_specs=[VMEM] * 3,
            scratch_shapes=[
                pltpu.VMEM((len(rows),) + blocks.shape[2:], f32),
                pltpu.VMEM((4 * channels, points), bf16),
                *[pltpu.VMEM(*piece_shape(first_rows))] * len(halo),
                pltpu.SemaphoreType.DMA((len(rows),)),
            ],
            compiler_params=params(16),
            cost_estimate=cost(2 * macs, 4 * blocks.size),
            name="prepare",
        )(own_cols, other_cols, in_hbm(blocks), coefs[2], other_blocks, *operands)

    def early_products(level, halo, *fields):
        ready = []
        for n, rows in enumerate(row_groups[level]):
            is_last = n + 1 == len(row_groups[level])
            prepared = prepare(
                level, rows, fields, (halo,) if is_last else (), ready if is_last else []
            )
            ready.append(prepared)
        high, low, parts = zip(*ready)
        return *high, *low, parts[-1]

    bands = early_products(0, early, first_total, second_total)
    first_part, swapped_left, diagonal_left = pl.pallas_call(
        functools.partial(first_rows_kernel, len(row_groups[0]), first_rows),
        out_shape=[
            part_shape(first_rows),
            jax.ShapeDtypeStruct(*piece_shape(second_rows)),
            jax.ShapeDtypeStruct(*piece_shape(every_row)),
        ],
        in_specs=[VMEM] * (4 + len(bands)),
        out_specs=[VMEM] * 3,
        compiler_params=params(12),
        cost_estimate=cost(macs, blocks.size),
        name="first_rows",
    )(*late, *bands, coefs[0])

    def level_second():
        return pl.pallas_call(
            functools.partial(level_rows, len(row_groups[0]), second_rows),
            out_shape=part_shape(second_rows),
            in_specs=[VMEM] * (3 + len(bands)),
            out_specs=VMEM,
            compiler_params=params(12),
            cost_estimate=cost(macs, blocks.size),
            name="second_rows",
        )(swapped_left, diagonal_left, *bands, coefs[1])

    second_part, early, late = exchange(first_part, level_second)
    last_bands = early_products(1, early, first_part, second_part)
    return pl.pallas_call(
        functools.partial(bottom_kernel, len(row_groups[1])),
        out_shape=jax.ShapeDtypeStruct(sources.shape, f32),
        in_specs=[VMEM] * (3 + len(last_bands)),
        out_specs=HBM,
        scratch_shapes=[
            pltpu.VMEM((block_rows, panels, 2, part, size), f32),
            pltpu.VMEM(*piece_shape(second_rows)),
            pltpu.VMEM(*piece_shape(every_row)),
            pltpu.SemaphoreType.DMA((block_rows,)),
        ],
        compiler_params=params(12),
        cost_estimate=cost(macs, blocks.size),
        name="bottom",
    )(*late, *last_bands)


def solution(mesh):
    placed = (
        P("shot", None, "depth", "lat"),
        P(("shot", "depth"), "lat", None, None, None, None),
        P("depth", "lat", None),
        P("lat"),
        P(None, "lat"),
    )
    return jax.shard_map(
        per_device,
        mesh=mesh,
        in_specs=placed,
        out_specs=P("shot", None, "depth", "lat"),
        check_vma=False,
    )
```
